128 devices in a mesh: dom: 128 (over z, x, y, core).
Axes of the slice: x: 4, y: 4, z: 4, core: 2. Of those that a mesh axis runs over, the one named last changes fastest.
Arguments:
- node_feat: float32 [524288, 128], P('dom'), may hold values from -6 to 6
- out_grad: float32 [524288, 128], P('dom'), may hold values from -6 to 6
- lattice_of: int32 [1024, 512], P('dom'), may hold values from 0 to 511, each once within a row
- element_place: int32 [128, 8], P('dom'), may hold values from 0 to 7, each once within a row
- edge_in: float32 [256, 128], replicated, may hold values from -0.375 to 0.375
- edge_mid: float32 [2, 128, 128], replicated, may hold values from -0.5 to 0.5
- edge_bias: float32 [3, 128], replicated, may hold values from -3 to 3
- node_in: float32 [256, 128], replicated, may hold values from -0.375 to 0.375
- node_mid: float32 [2, 128, 128], replicated, may hold values from -0.5 to 0.5
- node_bias: float32 [3, 128], replicated, may hold values from -3 to 3
Outputs:
- new_feat: float32 [524288, 128], P('dom')
- feat_grad: float32 [524288, 128], P('dom')
- edge_in_grad: float32 [256, 128], replicated
- edge_mid_grad: float32 [2, 128, 128], replicated
- edge_bias_grad: float32 [3, 128], replicated
- node_in_grad: float32 [256, 128], replicated
- node_mid_grad: float32 [2, 128, 128], replicated
- node_bias_grad: float32 [3, 128], replicated
The draws below stay inside these ranges and needn't reach their ends.
Inputs may be any that keep to these rules, and one draw needn't show every extreme that they name: `lattice_of`: row s lists, for node k of element slot s, its lattice point x * 8 * 8 + y * 8 + z; every row is a permutation. `element_place`: row d lists, for each element slot of partition d, its place p in the partition's 2 x 2 x 2 block of elements, at offset (p // 4, p // 2 % 2, p % 2) in elements; every row is a permutation.
All inputs are finite; a program needn't handle non-finite values.
Results may differ from the reference program's by a relative error of at most 0.0003.
Values sent between devices are 32-bit elements; how exact they have to be, the bound alone decides.
No kernel may reach another device: no remote copies, remote signals or barrier semaphores. Data moves between devices by JAX's collectives and lax.ppermute only.
A program may use at most 128 MiB of HBM per device.

```python
import math
import jax
import jax.numpy as jnp
from jax import lax

H = 128
SIDE = 8
ELEM_DEV = 8
DGX = 4
DGY = 4
NODES_EL = 512
ELEMS = 1024
NODES = 524288
N_DOM = 128


def levels(key, dims, cuts, least, largest):
    gain = 1.0
    for axis_at, shards_of in cuts:
        draws = jax.random.uniform(jax.random.fold_in(jax.random.fold_in(key, 6), axis_at), (shards_of,), jnp.float32, least / len(cuts), largest / len(cuts))
        gain = gain * jnp.repeat(jnp.exp(draws), dims[axis_at] // shards_of).reshape((-1,) + (1,) * (len(dims) - 1 - axis_at))
    return gain


def bell_draw(rng, dims, scale, limit, split=(), kind=jnp.bfloat16):
    entries = scale * jax.random.normal(rng, dims, jnp.float32)
    if split:
        entries = entries * levels(rng, dims, split, -0.22, 0.18)
    return jnp.clip(entries, -limit, limit).astype(kind)


def setup_inputs(seed: int = 0) -> dict:
    key_of = jax.random.split(jax.random.key(seed), 11)
    return {
        "node_feat": bell_draw(key_of[0], (NODES, H), 1.0, 6.0, ((0, 128),), jnp.float32),
        "out_grad": bell_draw(key_of[1], (NODES, H), 1.0, 6.0, ((0, 128),), jnp.float32),
        "lattice_of": jax.vmap(lambda own: jax.random.permutation(own, NODES_EL))(jax.random.split(key_of[2], ELEMS)).reshape((ELEMS, NODES_EL)).astype(jnp.int32),
        "element_place": jax.vmap(lambda own: jax.random.permutation(own, ELEM_DEV))(jax.random.split(key_of[3], N_DOM)).reshape((N_DOM, ELEM_DEV)).astype(jnp.int32),
        "edge_in": bell_draw(key_of[4], (2 * H, H), (2 * H) ** -0.5, 0.375, (), jnp.float32),
        "edge_mid": bell_draw(key_of[5], (2, H, H), H ** -0.5, 0.5, (), jnp.float32),
        "edge_bias": bell_draw(key_of[6], (3, H), 0.5, 3.0, (), jnp.float32),
        "node_in": bell_draw(key_of[7], (2 * H, H), (2 * H) ** -0.5, 0.375, (), jnp.float32),
        "node_mid": bell_draw(key_of[8], (2, H, H), H ** -0.5, 0.5, (), jnp.float32),
        "node_bias": bell_draw(key_of[9], (3, H), 0.5, 3.0, (), jnp.float32),
    }


highest = lax.Precision.HIGHEST

def matmul(values, weight):
    flat = values.reshape(-1, values.shape[-1])
    result = jnp.dot(flat, weight, precision=highest, preferred_element_type=jnp.float32)
    return result.reshape(values.shape[:-1] + (weight.shape[1],))

def edge_messages(lattice, edge_in, edge_mid, edge_bias):
    channels = lattice.shape[-1]
    extent = lattice.shape[1]
    toward = matmul(lattice, edge_in[:channels])
    source = matmul(lattice, edge_in[channels:])
    summed = jnp.zeros_like(lattice)
    for spatial in (1, 2, 3):
        for upward in (True, False):
            if upward:
                target = lax.slice_in_dim(toward, 0, extent - 1, axis=spatial)
                anchor = lax.slice_in_dim(source, 1, extent, axis=spatial)
                padding = (0, 1)
            else:
                target = lax.slice_in_dim(toward, 1, extent, axis=spatial)
                anchor = lax.slice_in_dim(source, 0, extent - 1, axis=spatial)
                padding = (1, 0)
            hidden = jax.nn.silu(target + anchor + edge_bias[0])
            hidden = jax.nn.silu(matmul(hidden, edge_mid[0]) + edge_bias[1])
            message = matmul(hidden, edge_mid[1]) + edge_bias[2]
            widths = [(0, 0)] * 5
            widths[spatial] = padding
            summed = summed + jnp.pad(message, widths)
    return summed

def node_update(lattice, gathered, node_in, node_mid, node_bias):
    channels = lattice.shape[-1]
    hidden = jax.nn.silu(matmul(lattice, node_in[:channels]) + matmul(gathered, node_in[channels:]) + node_bias[0])
    hidden = jax.nn.silu(matmul(hidden, node_mid[0]) + node_bias[1])
    return lattice + matmul(hidden, node_mid[1]) + node_bias[2]

def to_lattice(node_rows, lattice_of):
    channels = node_rows.shape[-1]
    count = lattice_of.shape[0]
    blocks = node_rows.reshape(count, -1, channels)
    placed = jax.vmap(lambda values, ordering: jnp.zeros_like(values).at[ordering].set(values))(blocks, lattice_of)
    return placed.reshape(count, SIDE, SIDE, SIDE, channels)

def from_lattice(lattice, lattice_of):
    channels = lattice.shape[-1]
    count = lattice_of.shape[0]
    blocks = lattice.reshape(count, -1, channels)
    picked = jax.vmap(lambda values, ordering: values[ordering])(blocks, lattice_of)
    return picked.reshape(-1, channels)

def block_corner(element_place, global_slot):
    device = global_slot // ELEM_DEV
    slot = global_slot % ELEM_DEV
    offset = element_place[device, slot].astype(jnp.int32)
    grid_x = device % DGX
    grid_y = device // DGX % DGY
    grid_z = device // (DGX * DGY)
    stride = SIDE - 1
    corner_x = ((2 * grid_x + offset // 4) * stride).astype(jnp.int32)
    corner_y = ((2 * grid_y + offset // 2 % 2) * stride).astype(jnp.int32)
    corner_z = ((2 * grid_z + offset % 2) * stride).astype(jnp.int32)
    return (corner_x, corner_y, corner_z, jnp.zeros((), jnp.int32))

def consistent(summed, element_place):
    channels = summed.shape[-1]
    flat = summed.reshape((-1, SIDE, SIDE, SIDE, channels))
    total = flat.shape[0]
    depth = N_DOM // (DGX * DGY)
    extent = 2 * (SIDE - 1)
    field = jnp.zeros((DGX * extent + 1, DGY * extent + 1, depth * extent + 1, channels), summed.dtype)
    sizes = (SIDE, SIDE, SIDE, channels)

    def add_one(global_slot, field):
        global_slot = jnp.asarray(global_slot).astype(jnp.int32)
        start = block_corner(element_place, global_slot)
        current = lax.dynamic_slice(field, start, sizes)
        return lax.dynamic_update_slice(field, current + flat[global_slot], start)
    field = lax.fori_loop(0, total, add_one, field)

    def take_one(global_slot):
        return lax.dynamic_slice(field, block_corner(element_place, global_slot), sizes)
    return lax.map(take_one, jnp.arange(total, dtype=jnp.int32)).reshape(summed.shape)

def reference(node_feat, out_grad, lattice_of, element_place, edge_in, edge_mid, edge_bias, node_in, node_mid, node_bias):
    channels = node_feat.shape[-1]
    shaped = (N_DOM, ELEM_DEV, SIDE, SIDE, SIDE, channels)
    lattice = to_lattice(node_feat, lattice_of).reshape(shaped)
    cotangent = to_lattice(out_grad, lattice_of).reshape(shaped)
    summed = lax.map(lambda block: edge_messages(block, edge_in, edge_mid, edge_bias), lattice)
    gathered = consistent(summed, element_place)
    updated = lax.map(lambda pair: node_update(pair[0], pair[1], node_in, node_mid, node_bias), (lattice, gathered))

    def node_back(triple):
        block, around, incoming = triple
        _, pullback = jax.vjp(node_update, block, around, node_in, node_mid, node_bias)
        return pullback(incoming)
    direct_grad, around_grad, node_in_grad, node_mid_grad, node_bias_grad = lax.map(node_back, (lattice, gathered, cotangent))
    around_total = consistent(around_grad, element_place)

    def edge_back(pair):
        block, incoming = pair
        _, pullback = jax.vjp(edge_messages, block, edge_in, edge_mid, edge_bias)
        return pullback(incoming)
    edge_grad, edge_in_grad, edge_mid_grad, edge_bias_grad = lax.map(edge_back, (lattice, around_total))
    scale = 1.0 / math.sqrt(NODES)
    flat_shape = (-1, SIDE, SIDE, SIDE, channels)
    new_feat = from_lattice(updated.reshape(flat_shape), lattice_of)
    feat_grad = from_lattice((direct_grad + edge_grad).reshape(flat_shape), lattice_of)
    return (new_feat, feat_grad, lax.optimization_barrier(jnp.sum(edge_in_grad, 0)) * scale, lax.optimization_barrier(jnp.sum(edge_mid_grad, 0)) * scale, lax.optimization_barrier(jnp.sum(edge_bias_grad, 0)) * scale, lax.optimization_barrier(jnp.sum(node_in_grad, 0)) * scale, lax.optimization_barrier(jnp.sum(node_mid_grad, 0)) * scale, lax.optimization_barrier(jnp.sum(node_bias_grad, 0)) * scale)
```

```python
import functools
import math

import jax
import jax.numpy as jnp
from jax import lax
from jax.experimental import pallas as pl
from jax.experimental.pallas import tpu as pltpu
from jax.sharding import PartitionSpec as P

SIDE = 8
ELEM_DEV = 8
DGX = 4
DGY = 4
NODES_EL = 512
H = 128
ROWS = ELEM_DEV * NODES_EL
PAYLOAD = 1024
F32 = jnp.float32
BF16 = jnp.bfloat16


def split(x):
    high = x.astype(BF16)
    low = (x - high.astype(F32)).astype(BF16)
    return jnp.concatenate([high, low], axis=-1)


def weight_split(w):
    row = split(w)
    return jnp.concatenate([row, row], axis=0)


def dot(a, b):
    return jnp.dot(a, b, preferred_element_type=F32)


def fold(o):
    return o[:, :H] + o[:, H:]


def mm(xs, w):
    return fold(dot(xs, w))


def mm_t(xs, ys):
    return lax.dot_general(xs, ys, (((0,), (0,)), ((), ())), preferred_element_type=F32)


def quad(o):
    return o[:H, :H] + o[:H, H:] + o[H:, :H] + o[H:, H:]


def row_sum(x):
    return jnp.sum(x.reshape(-1, 8, H), axis=0)


def exact_dot(a, b):
    return jnp.dot(a, b, precision=lax.Precision.HIGHEST, preferred_element_type=F32)


def to_lattice_onehot(lat_ref, slot):
    row = lat_ref[pl.ds(slot, 1), :]
    level = lax.broadcasted_iota(jnp.int32, (NODES_EL, NODES_EL), 0)
    return jnp.where(level == row, 1.0, 0.0).astype(BF16)


def from_lattice_onehot(lat_ref, slot):
    turned = lat_ref[...].astype(F32).T
    lane = lax.broadcasted_iota(jnp.int32, (NODES_EL, ELEM_DEV), 1)
    column = jnp.sum(jnp.where(lane == slot, turned, 0.0), axis=1, keepdims=True)
    level = lax.broadcasted_iota(jnp.int32, (NODES_EL, NODES_EL), 1)
    return jnp.where(level == column.astype(jnp.int32), 1.0, 0.0).astype(BF16)


def z_mask(upward):
    z = lax.broadcasted_iota(jnp.int32, (NODES_EL, H), 0) % SIDE
    return jnp.where(z < SIDE - 1, 1.0, 0.0) if upward else jnp.where(z > 0, 1.0, 0.0)


def part(value, axis, upper):
    four = value.reshape(SIDE, SIDE, SIDE, H)
    at = slice(1, SIDE) if upper else slice(0, SIDE - 1)
    return (four[at] if axis == 0 else four[:, at]).reshape(-1, H)


def shift(value, up):
    return pltpu.roll(value, NODES_EL - 1 if up else 1, 0)


def add_part(ref, axis, upper, rows):
    at = pl.ds(1, SIDE - 1) if upper else pl.ds(0, SIDE - 1)
    if axis == 0:
        ref[at] += rows.reshape(SIDE - 1, SIDE, SIDE, H)
    else:
        ref[:, at] += rows.reshape(SIDE, SIDE - 1, SIDE, H)


def assemble(ref):
    for p in range(0, 8, 2):
        a, b = pl.ds(SIDE - 1, 64, stride=SIDE), pl.ds(0, 64, stride=SIDE)
        total = ref[p, a, :] + ref[p + 1, b, :]
        ref[p, a, :] = total
        ref[p + 1, b, :] = total
    for p in (0, 1, 4, 5):
        for x in range(SIDE):
            a, b = pl.ds(x * 64 + 56, 8), pl.ds(x * 64, 8)
            total = ref[p, a, :] + ref[p + 2, b, :]
            ref[p, a, :] = total
            ref[p + 2, b, :] = total
    for p in range(4):
        a, b = pl.ds(448, 64), pl.ds(0, 64)
        total = ref[p, a, :] + ref[p + 4, b, :]
        ref[p, a, :] = total
        ref[p + 4, b, :] = total


def bits(p):
    return p // 4, p // 2 % 2, p % 2


def slot_in_plane(axis, p):
    px, py, pz = bits(p)
    return (py * 2 + pz, px * 2 + pz, px * 2 + py)[axis]


def emit_planes(ref, planes):
    for p in range(8):
        at = bits(p)
        edge = [7 * b for b in at]
        planes[0][at[0]][slot_in_plane(0, p)] = ref[p, pl.ds(edge[0] * 64, 64), :]
        for x in range(SIDE):
            planes[1][at[1]][slot_in_plane(1, p), pl.ds(x * 8, 8), :] = ref[p, pl.ds(x * 64 + edge[1] * 8, 8), :]
        planes[2][at[2]][slot_in_plane(2, p)] = ref[p, pl.ds(edge[2], 64, stride=SIDE), :]


def add_planes(ref, planes, p):
    for q in range(8):

        @pl.when(p == q)
        def _():
            at = bits(q)
            edge = [7 * b for b in at]
            rows = pl.ds(edge[2], 64, stride=SIDE)
            ref[rows, :] += planes[2][at[2]][slot_in_plane(2, q)]
            for x in range(SIDE):
                rows = pl.ds(x * 64 + edge[1] * 8, 8)
                ref[rows, :] += planes[1][at[1]][slot_in_plane(1, q), pl.ds(x * 8, 8), :]
            rows = pl.ds(edge[0] * 64, 64)
            ref[rows, :] += planes[0][at[0]][slot_in_plane(0, q)]


def half_silu(u):
    t = jnp.tanh(u)
    q = 1.0 + t
    return t, q, u * q


def twice_slope(t, q, s):
    return q + s * (1.0 - t)


DIRECTIONS = [(axis, up) for axis in (0, 1, 2) for up in (True, False)]


def edge_forward_kernel(meta, h_ref, lat_ref, win_ref, wmid_ref, eb_ref,
                        hl_ref, t_ref, s_ref, sum_ref, *rest):
    planes = [(rest[0], rest[1]), (rest[2], rest[3]), (rest[4], rest[5])]
    wts, w2, acc = rest[6:]
    p = pl.program_id(0)

    @pl.when(p == 0)
    def _():
        wts[:, 0:256] = weight_split(0.5 * win_ref[0:H, :])
        wts[:, 256:512] = weight_split(0.5 * win_ref[H:, :])
        w2[...] = weight_split(0.5 * wmid_ref[0])

    hl = dot(to_lattice_onehot(lat_ref, meta[p]), split(h_ref[...])).astype(BF16)
    hl_ref[0] = hl
    both = dot(hl, wts[...])
    t = fold(both[:, 0:256]) + 0.5 * eb_ref[0:1, :]
    s = fold(both[:, 256:512])
    t_ref[0] = t
    s_ref[0] = s
    bias = 0.5 * eb_ref[1:2, :]

    def second(u1):
        _, _, s1 = half_silu(u1)
        _, _, s2 = half_silu(mm(split(s1), w2[...]) + bias)
        return s2

    up = second(t + shift(s, True)) * z_mask(True)
    down = second(t + shift(s, False)) * z_mask(False)
    acc[...] = (up + down).reshape(SIDE, SIDE, SIDE, H)
    for axis, upward in DIRECTIONS[:4]:
        s2 = second(part(t, axis, not upward) + part(s, axis, upward))
        add_part(acc, axis, not upward, s2)
    sum_ref[p] = acc[...].reshape(NODES_EL, H)

    @pl.when(p == ELEM_DEV - 1)
    def _():
        assemble(sum_ref)
        emit_planes(sum_ref, planes)


def degrees(meta, p):
    r = lax.broadcasted_iota(jnp.int32, (NODES_EL, H), 0)
    at = (r // 64, r // 8 % 8, r % 8)
    count = None
    inner = None
    for axis, limit in ((0, DGX), (1, DGY), (2, meta[11])):
        b = (p // 4, p // 2 % 2, p % 2)[axis]
        g = meta[8 + axis]
        low = jnp.where((b == 0) & (g == 0), 1.0, 2.0)
        high = jnp.where((b == 1) & (g == limit - 1), 1.0, 2.0)
        first, last = at[axis] == 0, at[axis] == SIDE - 1
        times = jnp.where(first, low, jnp.where(last, high, 1.0))
        own = jnp.where(first | last, 1.0, 2.0)
        count = times if count is None else count * times
        inner = own if inner is None else inner + own
    return count * inner


def node_kernel(meta, sum_ref, hl_ref, g_ref, h_ref, lat_ref, nin_ref, nmid_ref, nb_ref, wmid_ref, eb_ref, *rest):
    received = [(rest[0], rest[1]), (rest[2], rest[3]), (rest[4], rest[5])]
    new_ref, dh_ref, dz_ref, grad_ref = rest[6:10]
    planes = [(rest[10], rest[11]), (rest[12], rest[13]), (rest[14], rest[15])]
    wa, wc, w0, w1, w0t, w1t, wat, row, gath, g_a, g_m, g_0, g_1, sums = rest[16:]
    p = pl.program_id(0)

    @pl.when(p == 0)
    def _():
        lower = nin_ref[H:, :]
        wa[...] = weight_split(0.5 * nin_ref[0:H, :])
        wc[...] = weight_split(0.5 * exact_dot(wmid_ref[1], lower))
        w0[...] = weight_split(0.5 * nmid_ref[0])
        w1[...] = weight_split(nmid_ref[1])
        w0t[...] = weight_split(0.5 * nmid_ref[0].T)
        w1t[...] = weight_split(0.5 * nmid_ref[1].T)
        wat[...] = weight_split(nin_ref[0:H, :].T)
        row[...] = 0.5 * exact_dot(jnp.broadcast_to(eb_ref[2:3, :], (8, H)), lower)
        for ref in (g_a, g_m, g_0, g_1, sums):
            ref[...] = jnp.zeros_like(ref)

    gath[...] = sum_ref[0]
    add_planes(gath, received, p)
    degree = degrees(meta, p)
    hl = hl_ref[0]
    gs = split(gath[...])
    u = mm(hl, wa[...]) + mm(gs, wc[...]) + degree * row[0:1, :] + 0.5 * nb_ref[0:1, :]
    t, q, s = half_silu(u)
    slope = twice_slope(t, q, s)
    ss = split(s)
    t, q, s = half_silu(mm(ss, w0[...]) + 0.5 * nb_ref[1:2, :])
    slope1 = twice_slope(t, q, s)
    ss1 = split(s)
    update = mm(ss1, w1[...])
    back = from_lattice_onehot(lat_ref, meta[p])
    new_ref[...] = h_ref[...] + fold(dot(back, split(update))) + nb_ref[2:3, :]

    gl = dot(to_lattice_onehot(lat_ref, meta[p]), split(g_ref[...])).astype(BF16)
    sums[2] += row_sum(g_ref[...])
    g_1[...] += mm_t(ss1, gl)
    dz1 = mm(gl, w1t[...]) * slope1
    sums[1] += row_sum(dz1)
    dz1s = split(dz1)
    g_0[...] += mm_t(ss, dz1s)
    dz = mm(dz1s, w0t[...]) * slope
    sums[0] += row_sum(dz)
    sums[3] += row_sum(dz * degree)
    dz_ref[p] = dz
    dzs = split(dz)
    g_a[...] += mm_t(hl, dzs)
    g_m[...] += mm_t(gs, dzs)
    dh_ref[0] = mm(dzs, wat[...])

    @pl.when(p == ELEM_DEV - 1)
    def _():
        grad_ref[0:H, :] = quad(g_m[...])
        grad_ref[H:2 * H, :] = quad(g_a[...])
        grad_ref[2 * H:3 * H, :] = quad(g_0[...])
        grad_ref[3 * H:4 * H, :] = quad(g_1[...])
        for i in range(4):
            grad_ref[4 * H + i * 8:4 * H + i * 8 + 8, :] = sums[i]
        assemble(dz_ref)
        emit_planes(dz_ref, planes)


def edge_backward_kernel(meta, dz_ref, hl_ref, t_ref, s_ref, dh_ref, g_ref, lat_ref, win_ref, wmid_ref, nin_ref, eb_ref, ngrad_ref, *rest):
    received = [(rest[0], rest[1]), (rest[2], rest[3]), (rest[4], rest[5])]
    feat_ref, grad_ref = rest[6:8]
    w2, w2t, wct, wtt, wst, d, dt, ds, g_2, g_t, g_s, sums = rest[8:]
    p = pl.program_id(0)

    @pl.when(p == 0)
    def _():
        w2[...] = weight_split(0.5 * wmid_ref[0])
        w2t[...] = weight_split(0.5 * wmid_ref[0].T)
        wct[...] = weight_split(0.5 * exact_dot(wmid_ref[1], nin_ref[H:, :]).T)
        wtt[...] = weight_split(win_ref[0:H, :].T)
        wst[...] = weight_split(win_ref[H:, :].T)
        for ref in (g_2, g_t, g_s, sums):
            ref[...] = jnp.zeros_like(ref)

    d[...] = dz_ref[0]
    add_planes(d, received, p)
    g = mm(split(d[...]), wct[...])
    t = t_ref[0]
    s = s_ref[0]
    bias = 0.5 * eb_ref[1:2, :]

    def chain(u1, cot):
        t1, q1, s1 = half_silu(u1)
        s1s = split(s1)
        t2, q2, s2 = half_silu(mm(s1s, w2[...]) + bias)
        dz2 = cot * twice_slope(t2, q2, s2)
        sums[1] += row_sum(dz2)
        dz2s = split(dz2)
        g_2[...] += mm_t(s1s, dz2s)
        return mm(dz2s, w2t[...]) * twice_slope(t1, q1, s1)

    up = chain(t + shift(s, True), g * z_mask(True))
    down = chain(t + shift(s, False), g * z_mask(False))
    dt[...] = (up + down).reshape(SIDE, SIDE, SIDE, H)
    ds[...] = (shift(up, False) + shift(down, True)).reshape(SIDE, SIDE, SIDE, H)
    for axis, upward in DIRECTIONS[:4]:
        dz1 = chain(part(t, axis, not upward) + part(s, axis, upward), part(g, axis, not upward))
        add_part(dt, axis, not upward, dz1)
        add_part(ds, axis, upward, dz1)
    dtv = dt[...].reshape(NODES_EL, H)
    dts = split(dtv)
    dss = split(ds[...].reshape(NODES_EL, H))
    sums[0] += row_sum(dtv)
    hl = hl_ref[0]
    g_t[...] += mm_t(hl, dts)
    g_s[...] += mm_t(hl, dss)
    dh = mm(dts, wtt[...]) + mm(dss, wst[...]) + dh_ref[0]
    back = from_lattice_onehot(lat_ref, meta[p])
    feat_ref[...] = g_ref[...] + fold(dot(back, split(dh)))

    @pl.when(p == ELEM_DEV - 1)
    def _():
        grad_ref[0:4 * H, :] = ngrad_ref[0:4 * H, :]
        grad_ref[4 * H:5 * H, :] = quad(g_t[...])
        grad_ref[5 * H:6 * H, :] = quad(g_s[...])
        grad_ref[6 * H:7 * H, :] = quad(g_2[...])
        rest_rows = jnp.zeros((PAYLOAD - 7 * H, H), F32)
        grad_ref[7 * H:, :] = rest_rows
        for i in range(4):
            grad_ref[7 * H + i:7 * H + i + 1, :] = jnp.sum(ngrad_ref[4 * H + i * 8:4 * H + i * 8 + 8, :], axis=0, keepdims=True)
        for i in range(2):
            grad_ref[7 * H + 4 + i:7 * H + 5 + i, :] = jnp.sum(sums[i], axis=0, keepdims=True)


def finish_kernel(scale, total_ref, wmid_ref, nin_ref, eb_ref, ein_ref, emid_ref, ebias_ref, nino_ref, nmid_ref, nbias_ref):
    def rows(i):
        return total_ref[i * H:(i + 1) * H, :]

    m = rows(0)
    lower = nin_ref[H:, :]
    v = total_ref[7 * H + 3:7 * H + 4, :]
    ein_ref[0:H, :] = rows(4) * scale
    ein_ref[H:, :] = rows(5) * scale
    emid_ref[0] = rows(6) * scale
    emid_ref[1] = exact_dot(m, lower.T) * scale
    ebias_ref[0:2, :] = total_ref[7 * H + 4:7 * H + 6, :] * scale
    ebias_ref[2:3, :] = exact_dot(jnp.broadcast_to(v, (8, H)), lower.T)[0:1] * scale
    nino_ref[0:H, :] = rows(1) * scale
    outer = eb_ref[2:3, :].T * v
    nino_ref[H:, :] = (exact_dot(wmid_ref[1].T, m) + outer) * scale
    nmid_ref[0] = rows(2) * scale
    nmid_ref[1] = rows(3) * scale
    nbias_ref[...] = total_ref[7 * H:7 * H + 3, :] * scale


def fix_y_kernel(yl, yh, rzl, rzh, oyl, oyh):
    rz, src, out = (rzl, rzh), (yl, yh), (oyl, oyh)
    oyl[...] = yl[...]
    oyh[...] = yh[...]
    for p in range(8):
        b = bits(p)
        rows = pl.ds(7 * b[2], 8, stride=SIDE)
        out[b[1]][slot_in_plane(1, p), rows, :] += rz[b[2]][slot_in_plane(2, p), pl.ds(7 * b[1], 8, stride=SIDE), :]


def fix_x_kernel(xl, xh, rzl, rzh, ryl, ryh, oxl, oxh):
    rz, ry, out = (rzl, rzh), (ryl, ryh), (oxl, oxh)
    oxl[...] = xl[...]
    oxh[...] = xh[...]
    for p in range(8):
        b = bits(p)
        mine = slot_in_plane(0, p)
        rows = pl.ds(7 * b[2], 8, stride=SIDE)
        out[b[0]][mine, rows, :] += rz[b[2]][slot_in_plane(2, p), pl.ds(56 * b[0], 8), :]
        rows = pl.ds(56 * b[1], 8)
        out[b[0]][mine, rows, :] += ry[b[1]][slot_in_plane(1, p), pl.ds(56 * b[0], 8), :]


PLANE = jax.ShapeDtypeStruct((4, 64, H), F32)
VM = pl.BlockSpec(memory_space=pltpu.VMEM)


def shifted(block, distance):
    n = lax.axis_size("dom")
    depth = n // (DGX * DGY)
    limits, strides = (DGX, DGY, depth), (1, DGX, DGX * DGY)
    axis = strides.index(abs(distance))
    step = 1 if distance > 0 else -1
    route = []
    for i in range(n):
        to = i // strides[axis] % limits[axis] + step
        if 0 <= to < limits[axis]:
            route.append((i, i + distance))
    return lax.ppermute(block, "dom", route)


def exchange(planes):
    (xl, xh), (yl, yh), (zl, zh) = planes
    rzh, rzl = shifted(zl, -DGX * DGY), shifted(zh, DGX * DGY)
    yl, yh = pl.pallas_call(fix_y_kernel, out_shape=(PLANE, PLANE), in_specs=[VM] * 4, out_specs=(VM, VM), name="fix_y")(yl, yh, rzl, rzh)
    ryh, ryl = shifted(yl, -DGX), shifted(yh, DGX)
    xl, xh = pl.pallas_call(fix_x_kernel, out_shape=(PLANE, PLANE), in_specs=[VM] * 6, out_specs=(VM, VM), name="fix_x")(xl, xh, rzl, rzh, ryl, ryh)
    rxh, rxl = shifted(xl, -1), shifted(xh, 1)
    return rxl, rxh, ryl, ryh, rzl, rzh


def at_slot(p, meta):
    return (meta[p], 0)


def whole(shape):
    return pl.BlockSpec(shape, lambda p, meta: (0,) * len(shape))


def per_element(*shape):
    return pl.BlockSpec((1,) + shape, lambda p, meta: (p,) + (0,) * len(shape))


NODE_BLOCK = pl.BlockSpec((NODES_EL, H), at_slot)
PARAMS = pltpu.CompilerParams(dimension_semantics=("arbitrary",), vmem_limit_bytes=60 * 1024 * 1024)


def sds(*shape, dtype=F32):
    return jax.ShapeDtypeStruct(shape, dtype)


def total_over_devices(block):
    n = lax.axis_size("dom")
    mine = lax.all_to_all(block.reshape(n, -1, H), "dom", 0, 0, tiled=True).sum(0)
    spread = jnp.broadcast_to(mine[None], (n,) + mine.shape)
    return lax.all_to_all(spread, "dom", 0, 0, tiled=True).reshape(-1, H)


def body(node_feat, out_grad, lattice_of, element_place, edge_in, edge_mid, edge_bias, node_in, node_mid, node_bias):
    n = lax.axis_size("dom")
    index = lax.axis_index("dom")
    places = element_place[0]
    slots = jnp.sum(jnp.where(places[None, :] == jnp.arange(8)[:, None], jnp.arange(8)[None, :], 0), axis=1)
    grid = jnp.stack([index % DGX, index // DGX % DGY, index // (DGX * DGY), jnp.full((), n // (DGX * DGY), index.dtype)])
    meta = jnp.concatenate([slots.astype(jnp.int32), grid.astype(jnp.int32)])

    elem = (ELEM_DEV, NODES_EL, H)
    outs = pl.pallas_call(
        edge_forward_kernel,
        grid_spec=pltpu.PrefetchScalarGridSpec(
            num_scalar_prefetch=1, grid=(ELEM_DEV,),
            in_specs=[NODE_BLOCK, whole((8, NODES_EL)), whole((256, H)), whole((2, H, H)), whole((3, H))],
            out_specs=[per_element(NODES_EL, 256), per_element(NODES_EL, H), per_element(NODES_EL, H), whole(elem)] + [whole((4, 64, H))] * 6,
            scratch_shapes=[pltpu.VMEM((256, 512), BF16), pltpu.VMEM((256, 256), BF16), pltpu.VMEM((SIDE, SIDE, SIDE, H), F32)]),
        out_shape=[sds(ELEM_DEV, NODES_EL, 256, dtype=BF16), sds(*elem), sds(*elem), sds(*elem)] + [PLANE] * 6,
        compiler_params=PARAMS, name="edge_forward",
    )(meta, node_feat, lattice_of, edge_in, edge_mid, edge_bias)
    hl, tv, sv, sums = outs[:4]
    got = exchange(((outs[4], outs[5]), (outs[6], outs[7]), (outs[8], outs[9])))

    outs = pl.pallas_call(
        node_kernel,
        grid_spec=pltpu.PrefetchScalarGridSpec(
            num_scalar_prefetch=1, grid=(ELEM_DEV,),
            in_specs=[per_element(NODES_EL, H), per_element(NODES_EL, 256), NODE_BLOCK, NODE_BLOCK, whole((8, NODES_EL)),
                      whole((256, H)), whole((2, H, H)), whole((3, H)), whole((2, H, H)), whole((3, H))] + [whole((4, 64, H))] * 6,
            out_specs=[NODE_BLOCK, per_element(NODES_EL, H), whole(elem), whole((4 * H + 32, H))] + [whole((4, 64, H))] * 6,
            scratch_shapes=[pltpu.VMEM((256, 256), BF16)] * 7 + [pltpu.VMEM((8, H), F32), pltpu.VMEM((NODES_EL, H), F32)]
            + [pltpu.VMEM((256, 256), F32)] * 4 + [pltpu.VMEM((4, 8, H), F32)]),
        out_shape=[sds(ROWS, H), sds(*elem), sds(*elem), sds(4 * H + 32, H)] + [PLANE] * 6,
        compiler_params=PARAMS, name="node_update",
    )(meta, sums, hl, out_grad, node_feat, lattice_of, node_in, node_mid, node_bias, edge_mid, edge_bias, *got)
    new_feat, dh, dz, ngrad = outs[:4]
    got = exchange(((outs[4], outs[5]), (outs[6], outs[7]), (outs[8], outs[9])))

    feat_grad, payload = pl.pallas_call(
        edge_backward_kernel,
        grid_spec=pltpu.PrefetchScalarGridSpec(
            num_scalar_prefetch=1, grid=(ELEM_DEV,),
            in_specs=[per_element(NODES_EL, H), per_element(NODES_EL, 256), per_element(NODES_EL, H), per_element(NODES_EL, H), per_element(NODES_EL, H),
                      NODE_BLOCK, whole((8, NODES_EL)), whole((256, H)), whole((2, H, H)), whole((256, H)), whole((3, H)), whole((4 * H + 32, H))] + [whole((4, 64, H))] * 6,
            out_specs=[NODE_BLOCK, whole((PAYLOAD, H))],
            scratch_shapes=[pltpu.VMEM((256, 256), BF16)] * 5 + [pltpu.VMEM((NODES_EL, H), F32)] + [pltpu.VMEM((SIDE, SIDE, SIDE, H), F32)] * 2
            + [pltpu.VMEM((256, 256), F32)] * 3 + [pltpu.VMEM((2, 8, H), F32)]),
        out_shape=[sds(ROWS, H), sds(PAYLOAD, H)],
        compiler_params=PARAMS, name="edge_backward",
    )(meta, dz, hl, tv, sv, dh, out_grad, lattice_of, edge_in, edge_mid, node_in, edge_bias, ngrad, *got)

    total = total_over_devices(payload)
    scale = 1.0 / math.sqrt(n * ELEM_DEV * NODES_EL)
    weights = pl.pallas_call(
        functools.partial(finish_kernel, scale),
        out_shape=(sds(256, H), sds(2, H, H), sds(3, H), sds(256, H), sds(2, H, H), sds(3, H)),
        in_specs=[VM] * 4, out_specs=(VM,) * 6, name="finish",
    )(total, edge_mid, node_in, edge_bias)
    return (new_feat, feat_grad) + tuple(weights)


def solution(mesh):
    in_specs = (P("dom", None),) * 4 + (P(),) * 6
    out_specs = (P("dom", None), P("dom", None)) + (P(),) * 6
    return jax.shard_map(body, mesh=mesh, in_specs=in_specs, out_specs=out_specs, check_vma=False)
```

```python
import functools
import math

import jax
import jax.numpy as jnp
from jax import lax
from jax.experimental import pallas as pl
from jax.experimental.pallas import tpu as pltpu
from jax.sharding import PartitionSpec as P

SIDE = 8
ELEM_DEV = 8
DGX = 4
DGY = 4
NODES_EL = 512
H = 128
ROWS = ELEM_DEV * NODES_EL
PAYLOAD = 1024
F32 = jnp.float32
BF16 = jnp.bfloat16


def split(x):
    high = x.astype(BF16)
    low = (x - high.astype(F32)).astype(BF16)
    return jnp.concatenate([high, low], axis=-1)


def weight_split(w):
    row = split(w)
    return jnp.concatenate([row, row], axis=0)


def dot(a, b):
    return jnp.dot(a, b, preferred_element_type=F32)


def fold(o):
    return o[:, :H] + o[:, H:]


def mm(xs, w):
    return fold(dot(xs, w))


def mm_t(xs, ys):
    return lax.dot_general(xs, ys, (((0,), (0,)), ((), ())), preferred_element_type=F32)


def quad(o):
    return o[:H, :H] + o[:H, H:] + o[H:, :H] + o[H:, H:]


def row_sum(x):
    return jnp.sum(x.reshape(-1, 8, H), axis=0)


def exact_dot(a, b):
    return jnp.dot(a, b, precision=lax.Precision.HIGHEST, preferred_element_type=F32)


def flip(e):
    return (e // 4) * 448 + (e // 2 % 2) * 56 + (e % 2) * 7


def to_lattice_onehot(lat_ref, slot, e):
    row = lat_ref[pl.ds(slot, 1), :] ^ flip(e)
    level = lax.broadcasted_iota(jnp.int32, (NODES_EL, NODES_EL), 0)
    return jnp.where(level == row, 1.0, 0.0).astype(BF16)


def from_lattice_onehot(lat_ref, slot, e):
    turned = lat_ref[...].astype(F32).T
    lane = lax.broadcasted_iota(jnp.int32, (NODES_EL, ELEM_DEV), 1)
    column = jnp.sum(jnp.where(lane == slot, turned, 0.0), axis=1, keepdims=True).astype(jnp.int32) ^ flip(e)
    level = lax.broadcasted_iota(jnp.int32, (NODES_EL, NODES_EL), 1)
    return jnp.where(level == column, 1.0, 0.0).astype(BF16)


def slot_rows(slot):
    return pl.ds(pl.multiple_of(slot * NODES_EL, NODES_EL), NODES_EL)


def element_rows(e):
    return pl.ds(e, NODES_EL, stride=ELEM_DEV)


def to_lattice(meta, lat_ref, src_ref, dst_ref):
    def one(e, carry):
        slot = meta[e]
        both = dot(to_lattice_onehot(lat_ref, slot, e), split(src_ref[slot_rows(slot), :]))
        dst_ref[element_rows(e), :] = fold(both)
        return carry

    lax.fori_loop(0, ELEM_DEV, one, 0)


def from_lattice(meta, lat_ref, src_ref, add_ref, dst_ref, bias):
    def one(e, carry):
        slot = meta[e]
        back = from_lattice_onehot(lat_ref, slot, e)
        rows = fold(dot(back, split(src_ref[element_rows(e), :])))
        rows = rows + add_ref[slot_rows(slot), :]
        dst_ref[slot_rows(slot), :] = rows if bias is None else rows + bias
        return carry

    lax.fori_loop(0, ELEM_DEV, one, 0)


FULL = (SIDE, SIDE, SIDE, ELEM_DEV, H)
OUTER = [((0, 1), (0, 8), (0, 8)), ((1, 8), (0, 1), (0, 8)), ((1, 8), (1, 8), (0, 1))]
INNER = [((1, 8), (1, 8), (1, 8))]


def at_box(box):
    return tuple(pl.ds(a, b - a) for a, b in box)


def get(ref, box):
    return ref[at_box(box)].reshape(-1, H)


def shape_of(box):
    return tuple(b - a for a, b in box) + (ELEM_DEV, H)


def put(ref, box, rows):
    ref[at_box(box)] = rows.reshape(shape_of(box))


def add(ref, box, rows):
    ref[at_box(box)] += rows.reshape(shape_of(box))


def pairs_of(box):
    out = []
    for axis in range(3):
        for step in (1, -1):
            a, b = box[axis]
            a, b = (a, min(b, SIDE - 1)) if step == 1 else (max(a, 1), b)
            if a < b:
                out.append((box[:axis] + ((a, b),) + box[axis + 1:], box[:axis] + ((a + step, b + step),) + box[axis + 1:]))
    return out


SLAB = ((1, 8), (1, 8))


def slab_pairs(x):
    out = [((x, SLAB), (x - 1, SLAB), None)]
    for axis in range(2):
        for step in (1, -1):
            a, b = (1, SIDE - 1) if step == 1 else (1, SIDE)
            receivers = SLAB[:axis] + ((a, b),) + SLAB[axis + 1:]
            senders = SLAB[:axis] + ((a + step, b + step),) + SLAB[axis + 1:]
            out.append(((x, receivers), (x, senders), None))
    upper = jnp.where(x < SIDE - 1, 1.0, 0.0)
    out.append(((x, SLAB), (jnp.minimum(x + 1, SIDE - 1), SLAB), upper))
    return out


def at_slab(where):
    x, box = where
    return (x,) + tuple(pl.ds(a, b - a) for a, b in box)


def sget(ref, where):
    return ref[at_slab(where)].reshape(-1, H)


def sshape(where):
    return tuple(b - a for a, b in where[1]) + (ELEM_DEV, H)


def sput(ref, where, rows):
    ref[at_slab(where)] = rows.reshape(sshape(where))


def sadd(ref, where, rows):
    ref[at_slab(where)] += rows.reshape(sshape(where))


def swap(v, axis):
    if axis == 0:
        return pltpu.roll(v, 4, 1)
    by = 2 if axis == 1 else 1
    e = lax.broadcasted_iota(jnp.int32, v.shape, 1)
    return jnp.where((e & by) == 0, pltpu.roll(v, ELEM_DEV - by, 1), pltpu.roll(v, by, 1))


def assemble(ref, boxes):
    for axis in (2, 1, 0):
        for box in boxes:
            if box[axis][1] == SIDE:
                face = box[:axis] + ((SIDE - 1, SIDE),) + box[axis + 1:]
                v = ref[at_box(face)].reshape(-1, ELEM_DEV, H)
                put(ref, face, v + swap(v, axis))


def bits(p):
    return p // 4, p // 2 % 2, p % 2


def slot_in_plane(axis, p):
    px, py, pz = bits(p)
    return (py * 2 + pz, px * 2 + pz, px * 2 + py)[axis]


def outer_rows(axis, e):
    if axis == 0:
        return [(pl.ds(e, 64, stride=8), pl.ds(0, 64))]
    if axis == 2:
        return [(pl.ds(e, 64, stride=64), pl.ds(0, 64))]
    return [(pl.ds(x * 512 + e, 8, stride=8), pl.ds(x * 8, 8)) for x in range(SIDE)]


def emit_planes(ref, planes):
    flat = ref.reshape((ROWS, H))
    for axis in range(3):
        for e in range(ELEM_DEV):
            for rows, there in outer_rows(axis, e):
                planes[axis][bits(e)[axis]][slot_in_plane(axis, e), there, :] = flat[rows, :]


def add_planes(ref, planes):
    flat = ref.reshape((ROWS, H))
    for axis in range(3):
        for e in range(ELEM_DEV):
            for rows, there in outer_rows(axis, e):
                flat[rows, :] += planes[axis][bits(e)[axis]][slot_in_plane(axis, e), there, :]


def half_silu(u):
    t = jnp.tanh(u)
    q = 1.0 + t
    return t, q, u * q


def twice_slope(t, q, s):
    return q + s * (1.0 - t)


def forward_edge(u1, w2, bias):
    _, _, s1 = half_silu(u1)
    _, _, s2 = half_silu(mm(split(s1), w2[...]) + bias)
    return s2


def edge_outer_kernel(meta, h_ref, lat_ref, win_ref, wmid_ref, eb_ref, hs_ref, t_ref, s_ref, sum_ref, xl, xh, yl, yh, zl, zh, wts, w2):
    wts[:, 0:256] = weight_split(0.5 * win_ref[0:H, :])
    wts[:, 256:512] = weight_split(0.5 * win_ref[H:, :])
    w2[...] = weight_split(0.5 * wmid_ref[0])
    to_lattice(meta, lat_ref, h_ref, hs_ref.reshape((ROWS, H)))
    half_bias = 0.5 * eb_ref[0:1, :]

    def plane(x, carry):
        both = dot(split(hs_ref[x].reshape(-1, H)), wts[...])
        t_ref[x] = (fold(both[:, 0:256]) + half_bias).reshape(FULL[1:])
        s_ref[x] = fold(both[:, 256:512]).reshape(FULL[1:])
        return carry

    lax.fori_loop(0, SIDE, plane, 0)
    bias = 0.5 * eb_ref[1:2, :]
    for box in OUTER:
        put(sum_ref, box, jnp.zeros((math.prod(shape_of(box)) // H, H), F32))
        for receivers, senders in pairs_of(box):
            add(sum_ref, receivers, forward_edge(get(t_ref, receivers) + get(s_ref, senders), w2, bias))
    assemble(sum_ref, OUTER)
    emit_planes(sum_ref, ((xl, xh), (yl, yh), (zl, zh)))


def edge_inner_kernel(meta, t_ref, s_ref, g_ref, lat_ref, wmid_ref, eb_ref, sum_ref, gl_ref, w2):
    w2[...] = weight_split(0.5 * wmid_ref[0])
    bias = 0.5 * eb_ref[1:2, :]

    def plane(x, carry):
        sput(sum_ref, (x, SLAB), jnp.zeros((49 * 8, H), F32))
        for receivers, senders, factor in slab_pairs(x):
            s2 = forward_edge(sget(t_ref, receivers) + sget(s_ref, senders), w2, bias)
            sadd(sum_ref, receivers, s2 if factor is None else s2 * factor)
        return carry

    lax.fori_loop(1, SIDE, plane, 0)
    assemble(sum_ref, INNER)
    to_lattice(meta, lat_ref, g_ref, gl_ref.reshape((ROWS, H)))


def degree_of(meta, where, shape):
    full = shape + (ELEM_DEV, H)
    e = lax.broadcasted_iota(jnp.int32, (ELEM_DEV, H), 0)
    count, own = None, None
    for axis, limit in ((0, DGX), (1, DGY), (2, meta[11])):
        side = (e >> (2 - axis)) & 1
        low = jnp.where(meta[8 + axis] > 0, 2.0, 1.0)
        high = jnp.where(meta[8 + axis] < limit - 1, 2.0, 1.0)
        outer = jnp.broadcast_to(jnp.where(side == 0, low, high), full)
        at = lax.broadcasted_iota(jnp.int32, full, axis) + where[axis]
        times = jnp.where(at == 0, outer, jnp.where(at == SIDE - 1, 2.0, 1.0))
        messages = jnp.where((at == 0) | (at == SIDE - 1), 1.0, 2.0)
        count = times if count is None else count * times
        own = messages if own is None else own + messages
    return (count * own).reshape(-1, H)


def node_weights(nin_ref, nmid_ref, wmid_ref, eb_ref, weights):
    wa, wc, w0, w1, w0t, w1t, wat, row = weights
    lower = nin_ref[H:, :]
    wa[...] = weight_split(0.5 * nin_ref[0:H, :])
    wc[...] = weight_split(0.5 * exact_dot(wmid_ref[1], lower))
    w0[...] = weight_split(0.5 * nmid_ref[0])
    w1[...] = weight_split(nmid_ref[1])
    w0t[...] = weight_split(0.5 * nmid_ref[0].T)
    w1t[...] = weight_split(0.5 * nmid_ref[1].T)
    wat[...] = weight_split(nin_ref[0:H, :].T)
    row[...] = 0.5 * exact_dot(jnp.broadcast_to(eb_ref[2:3, :], (8, H)), lower)


def node_chunk(gathered, h, g, degree, nb_ref, weights, totals, sums):
    wa, wc, w0, w1, w0t, w1t, wat, row = weights
    g_a, g_m, g_0, g_1 = totals
    hs = split(h)
    gs = split(gathered)
    u = mm(hs, wa[...]) + mm(gs, wc[...]) + degree * row[0:1, :] + 0.5 * nb_ref[0:1, :]
    t, q, s = half_silu(u)
    slope = twice_slope(t, q, s)
    ss = split(s)
    t, q, s = half_silu(mm(ss, w0[...]) + 0.5 * nb_ref[1:2, :])
    slope1 = twice_slope(t, q, s)
    ss1 = split(s)
    update = mm(ss1, w1[...])
    gl = split(g)
    sums[2] += row_sum(g)
    g_1[...] += mm_t(ss1, gl)
    dz1 = mm(gl, w1t[...]) * slope1
    sums[1] += row_sum(dz1)
    dz1s = split(dz1)
    g_0[...] += mm_t(ss, dz1s)
    dz = mm(dz1s, w0t[...]) * slope
    sums[0] += row_sum(dz)
    sums[3] += row_sum(dz * degree)
    dzs = split(dz)
    g_a[...] += mm_t(hs, dzs)
    g_m[...] += mm_t(gs, dzs)
    return update, dz, mm(dzs, wat[...])


def node_inner_kernel(meta, sum_ref, hs_ref, gl_ref, nin_ref, nmid_ref, nb_ref, wmid_ref, eb_ref, up_ref, dh_ref, dz_ref, g_out, sums_out, *weights):
    node_weights(nin_ref, nmid_ref, wmid_ref, eb_ref, weights)
    totals = [g_out.at[i] for i in range(4)]
    g_out[...] = jnp.zeros_like(g_out)
    sums_out[...] = jnp.zeros_like(sums_out)

    def plane(x, carry):
        where = (x, SLAB)
        degree = degree_of(meta, (x, 1, 1), (1, 7, 7))
        update, dz, dh = node_chunk(sget(sum_ref, where), sget(hs_ref, where), sget(gl_ref, where), degree, nb_ref, weights, totals, sums_out)
        sput(up_ref, where, update)
        sput(dz_ref, where, dz)
        sput(dh_ref, where, dh)
        return carry

    lax.fori_loop(1, SIDE, plane, 0)
    assemble(dz_ref, INNER)


def node_outer_kernel(meta, sum_ref, hs_ref, gl_ref, nin_ref, nmid_ref, nb_ref, wmid_ref, eb_ref, up_in, dh_in, g_in, sums_in,
                      rxl, rxh, ryl, ryh, rzl, rzh, up_ref, dh_ref, dz_ref, grad_ref, xl, xh, yl, yh, zl, zh, acc, totals_ref, sums, *weights):
    node_weights(nin_ref, nmid_ref, wmid_ref, eb_ref, weights)
    totals_ref[...] = g_in[...]
    sums[...] = sums_in[...]
    totals = [totals_ref.at[i] for i in range(4)]

    def inner(x, carry):
        up_ref[at_slab((x, SLAB))] = up_in[at_slab((x, SLAB))]
        dh_ref[at_slab((x, SLAB))] = dh_in[at_slab((x, SLAB))]
        return carry

    lax.fori_loop(1, SIDE, inner, 0)
    for box in OUTER:
        acc[at_box(box)] = sum_ref[at_box(box)]
    add_planes(acc, ((rxl, rxh), (ryl, ryh), (rzl, rzh)))
    for box in OUTER:
        degree = degree_of(meta, tuple(a for a, _ in box), tuple(b - a for a, b in box))
        update, dz, dh = node_chunk(get(acc, box), get(hs_ref, box), get(gl_ref, box), degree, nb_ref, weights, totals, sums)
        put(up_ref, box, update)
        put(dz_ref, box, dz)
        put(dh_ref, box, dh)
    assemble(dz_ref, OUTER)
    emit_planes(dz_ref, ((xl, xh), (yl, yh), (zl, zh)))
    grad_ref[0:H, :] = quad(totals_ref[1])
    grad_ref[H:2 * H, :] = quad(totals_ref[0])
    grad_ref[2 * H:3 * H, :] = quad(totals_ref[2])
    grad_ref[3 * H:4 * H, :] = quad(totals_ref[3])
    for i in range(4):
        grad_ref[4 * H + i * 8:4 * H + i * 8 + 8, :] = sums[i]


def new_feat_kernel(meta, up_ref, h_ref, lat_ref, nb_ref, new_ref):
    from_lattice(meta, lat_ref, up_ref.reshape((ROWS, H)), h_ref, new_ref, nb_ref[2:3, :])


def back_weights(wmid_ref, nin_ref, w2, w2t, wct):
    w2[...] = weight_split(0.5 * wmid_ref[0])
    w2t[...] = weight_split(0.5 * wmid_ref[0].T)
    wct[...] = weight_split(0.5 * exact_dot(wmid_ref[1], nin_ref[H:, :]).T)


def backward_edge(u1, cot, w2, w2t, bias, g_2, total):
    t1, q1, s1 = half_silu(u1)
    s1s = split(s1)
    t2, q2, s2 = half_silu(mm(s1s, w2[...]) + bias)
    dz2 = cot * twice_slope(t2, q2, s2)
    total[...] += row_sum(dz2)
    dz2s = split(dz2)
    g_2[...] += mm_t(s1s, dz2s)
    return mm(dz2s, w2t[...]) * twice_slope(t1, q1, s1)


def back_inner_kernel(first, last, meta, dz_ref, t_ref, s_ref, wmid_ref, nin_ref, eb_ref, dt_ref, ds_ref, g2_ref, total_ref, w2, w2t, wct, cot):
    back_weights(wmid_ref, nin_ref, w2, w2t, wct)
    bias = 0.5 * eb_ref[1:2, :]
    g2_ref[...] = jnp.zeros_like(g2_ref)
    total_ref[...] = jnp.zeros_like(total_ref)

    def clear(x, carry):
        ds_ref[x] = jnp.zeros(FULL[1:], F32)
        return carry

    lax.fori_loop(0, SIDE, clear, 0)

    def plane(x, carry):
        sput(dt_ref, (x, SLAB), jnp.zeros((49 * 8, H), F32))
        cot[0, pl.ds(1, 7), pl.ds(1, 7)] = mm(split(sget(dz_ref, (x, SLAB))), wct[...]).reshape(7, 7, ELEM_DEV, H)
        for receivers, senders, factor in slab_pairs(x):
            g = sget(cot, (0, receivers[1]))
            g = g if factor is None else g * factor
            dz1 = backward_edge(sget(t_ref, receivers) + sget(s_ref, senders), g, w2, w2t, bias, g2_ref, total_ref)
            sadd(dt_ref, receivers, dz1)
            sadd(ds_ref, senders, dz1)
        return carry

    lax.fori_loop(first, last, plane, 0)


def back_outer_kernel(meta, dz_ref, t_ref, s_ref, hs_ref, dh_ref, g_ref, lat_ref, win_ref, wmid_ref, nin_ref, eb_ref, ngrad_ref, dt_a, ds_a, g2_a, total_a, dt_b, ds_b, g2_b, total_b,
                      rxl, rxh, ryl, ryh, rzl, rzh, feat_ref, grad_ref, dt_ref, ds_ref, acc, w2, w2t, wct, wtt, wst, g_2, g_t, g_s, sums):
    back_weights(wmid_ref, nin_ref, w2, w2t, wct)
    wtt[...] = weight_split(win_ref[0:H, :].T)
    wst[...] = weight_split(win_ref[H:, :].T)
    g_2[...] = g2_a[...] + g2_b[...]
    g_t[...] = jnp.zeros_like(g_t)
    g_s[...] = jnp.zeros_like(g_s)
    sums[0] = jnp.zeros((8, H), F32)
    sums[1] = total_a[...] + total_b[...]
    bias = 0.5 * eb_ref[1:2, :]
    for box in OUTER:
        acc[at_box(box)] = dz_ref[at_box(box)]
    add_planes(acc, ((rxl, rxh), (ryl, ryh), (rzl, rzh)))

    def senders_so_far(x, carry):
        ds_ref[x] = ds_a[x] + ds_b[x]
        return carry

    lax.fori_loop(0, SIDE, senders_so_far, 0)
    for source, first, last in ((dt_a, 1, HALF), (dt_b, HALF, SIDE)):
        dt_ref[first:last, 1:, 1:] = source[first:last, 1:, 1:]
    for box in OUTER:
        put(acc, box, mm(split(get(acc, box)), wct[...]))
        put(dt_ref, box, jnp.zeros((math.prod(shape_of(box)) // H, H), F32))
        for receivers, senders in pairs_of(box):
            dz1 = backward_edge(get(t_ref, receivers) + get(s_ref, senders), get(acc, receivers), w2, w2t, bias, g_2, sums.at[1])
            add(dt_ref, receivers, dz1)
            add(ds_ref, senders, dz1)

    def plane(x, carry):
        dt = dt_ref[x].reshape(-1, H)
        dts = split(dt)
        dss = split(ds_ref[x].reshape(-1, H))
        hs = split(hs_ref[x].reshape(-1, H))
        sums[0] += row_sum(dt)
        g_t[...] += mm_t(hs, dts)
        g_s[...] += mm_t(hs, dss)
        dh = mm(dts, wtt[...]) + mm(dss, wst[...]) + dh_ref[x].reshape(-1, H)
        acc[x] = dh.reshape(FULL[1:])
        return carry

    lax.fori_loop(0, SIDE, plane, 0)
    from_lattice(meta, lat_ref, acc.reshape((ROWS, H)), g_ref, feat_ref, None)
    grad_ref[0:4 * H, :] = ngrad_ref[0:4 * H, :]
    grad_ref[4 * H:5 * H, :] = quad(g_t[...])
    grad_ref[5 * H:6 * H, :] = quad(g_s[...])
    grad_ref[6 * H:7 * H, :] = quad(g_2[...])
    grad_ref[7 * H:, :] = jnp.zeros((PAYLOAD - 7 * H, H), F32)
    for i in range(4):
        grad_ref[7 * H + i:7 * H + i + 1, :] = jnp.sum(ngrad_ref[4 * H + i * 8:4 * H + i * 8 + 8, :], axis=0, keepdims=True)
    for i in range(2):
        grad_ref[7 * H + 4 + i:7 * H + 5 + i, :] = jnp.sum(sums[i], axis=0, keepdims=True)


def finish_kernel(scale, total_ref, wmid_ref, nin_ref, eb_ref, ein_ref, emid_ref, ebias_ref, nino_ref, nmid_ref, nbias_ref):
    def rows(i):
        return total_ref[i * H:(i + 1) * H, :]

    m = rows(0)
    lower = nin_ref[H:, :]
    v = total_ref[7 * H + 3:7 * H + 4, :]
    ein_ref[0:H, :] = rows(4) * scale
    ein_ref[H:, :] = rows(5) * scale
    emid_ref[0] = rows(6) * scale
    emid_ref[1] = exact_dot(m, lower.T) * scale
    ebias_ref[0:2, :] = total_ref[7 * H + 4:7 * H + 6, :] * scale
    ebias_ref[2:3, :] = exact_dot(jnp.broadcast_to(v, (8, H)), lower.T)[0:1] * scale
    nino_ref[0:H, :] = rows(1) * scale
    outer = eb_ref[2:3, :].T * v
    nino_ref[H:, :] = (exact_dot(wmid_ref[1].T, m) + outer) * scale
    nmid_ref[0] = rows(2) * scale
    nmid_ref[1] = rows(3) * scale
    nbias_ref[...] = total_ref[7 * H:7 * H + 3, :] * scale


def fix_y_kernel(yl, yh, rzl, rzh, oyl, oyh):
    rz, out = (rzl, rzh), (oyl, oyh)
    oyl[...] = yl[...]
    oyh[...] = yh[...]
    line = pl.ds(0, 8, stride=SIDE)
    for p in range(8):
        b = bits(p)
        out[b[1]][slot_in_plane(1, p), line, :] += rz[b[2]][slot_in_plane(2, p), line, :]


def fix_x_kernel(xl, xh, rzl, rzh, ryl, ryh, oxl, oxh):
    rz, ry, out = (rzl, rzh), (ryl, ryh), (oxl, oxh)
    oxl[...] = xl[...]
    oxh[...] = xh[...]
    first = pl.ds(0, 8)
    for p in range(8):
        b = bits(p)
        mine = slot_in_plane(0, p)
        out[b[0]][mine, pl.ds(0, 8, stride=SIDE), :] += rz[b[2]][slot_in_plane(2, p), first, :]
        out[b[0]][mine, first, :] += ry[b[1]][slot_in_plane(1, p), first, :]


PLANE = jax.ShapeDtypeStruct((4, 64, H), F32)
VM = pl.BlockSpec(memory_space=pltpu.VMEM)
SM = pl.BlockSpec(memory_space=pltpu.SMEM)


def shifted(block, distance):
    n = lax.axis_size("dom")
    depth = n // (DGX * DGY)
    limits, strides = (DGX, DGY, depth), (1, DGX, DGX * DGY)
    axis = strides.index(abs(distance))
    step = 1 if distance > 0 else -1
    route = []
    for i in range(n):
        to = i // strides[axis] % limits[axis] + step
        if 0 <= to < limits[axis]:
            route.append((i, i + distance))
    return lax.ppermute(block, "dom", route)


def sds(*shape, dtype=F32):
    return jax.ShapeDtypeStruct(shape, dtype)


HALF = 5
LATTICE = jax.ShapeDtypeStruct(FULL, F32)
LIMIT = 14
SMALL = pltpu.CompilerParams(vmem_limit_bytes=6 * 1024 * 1024)


def run(kernel, name, outs, scratch, args, micros, aliases={}):
    call = pl.pallas_call(
        kernel, out_shape=outs, in_specs=[SM] + [VM] * (len(args) - 1), out_specs=[VM] * len(outs), scratch_shapes=scratch,
        input_output_aliases=aliases, name=name,
        cost_estimate=pl.CostEstimate(flops=micros * 1000000000, bytes_accessed=8000000, transcendentals=0),
        compiler_params=pltpu.CompilerParams(vmem_limit_bytes=LIMIT * 1024 * 1024),
    )
    return list(call(*args))


def exchange(planes, beside_z, beside_y):
    xl, xh, yl, yh, zl, zh = planes
    with jax.named_scope("along_z"):
        rzh, rzl = shifted(zl, -DGX * DGY), shifted(zh, DGX * DGY)
    rzl, rzh = beside_z(rzl, rzh)
    yl, yh = pl.pallas_call(fix_y_kernel, out_shape=(PLANE, PLANE), in_specs=[VM] * 4, out_specs=(VM, VM), name="fix_y", compiler_params=SMALL)(yl, yh, rzl, rzh)
    with jax.named_scope("along_y"):
        ryh, ryl = shifted(yl, -DGX), shifted(yh, DGX)
    ryl, ryh = beside_y(ryl, ryh)
    xl, xh = pl.pallas_call(fix_x_kernel, out_shape=(PLANE, PLANE), in_specs=[VM] * 6, out_specs=(VM, VM), name="fix_x", compiler_params=SMALL)(xl, xh, rzl, rzh, ryl, ryh)
    with jax.named_scope("along_x"):
        rxh, rxl = shifted(xl, -1), shifted(xh, 1)
    return [rxl, rxh, ryl, ryh, rzl, rzh]


def total_over_devices(block):
    n = lax.axis_size("dom")
    mine = lax.all_to_all(block.reshape(n, -1, H), "dom", 0, 0, tiled=True).sum(0)
    spread = jnp.broadcast_to(mine[None], (n,) + mine.shape)
    return lax.all_to_all(spread, "dom", 0, 0, tiled=True).reshape(-1, H)


def body(node_feat, out_grad, lattice_of, element_place, edge_in, edge_mid, edge_bias, node_in, node_mid, node_bias):
    n = lax.axis_size("dom")
    index = lax.axis_index("dom")
    places = element_place[0]
    slots = jnp.sum(jnp.where(places[None, :] == jnp.arange(8)[:, None], jnp.arange(8)[None, :], 0), axis=1)
    grid = jnp.stack([index % DGX, index // DGX % DGY, index // (DGX * DGY), jnp.full((), n // (DGX * DGY), index.dtype)])
    meta = jnp.concatenate([slots.astype(jnp.int32), grid.astype(jnp.int32)])
    square, wide, acc = pltpu.VMEM((256, 256), BF16), pltpu.VMEM((256, 512), BF16), pltpu.VMEM(FULL, F32)
    total = pltpu.VMEM((256, 256), F32)

    outs = run(edge_outer_kernel, "edge_outer", [LATTICE] * 4 + [PLANE] * 6, [wide, square],
               (meta, node_feat, lattice_of, edge_in, edge_mid, edge_bias), 8)
    hs, tv, sv, outer_sum = outs[:4]
    node_args = (node_in, node_mid, node_bias, edge_mid, edge_bias)
    weights = [square] * 7 + [pltpu.VMEM((8, H), F32)]

    done = {}

    def beside_z(*got):
        inner_sum, gl = run(edge_inner_kernel, "edge_inner", [LATTICE] * 2, [square], (meta, tv, sv, out_grad, lattice_of, edge_mid, edge_bias), 12)
        *got, done["sum"], done["gl"] = lax.optimization_barrier((*got, inner_sum, gl))
        return got

    def beside_y(*got):
        done["node"] = run(node_inner_kernel, "node_inner", [LATTICE] * 3 + [sds(4, 256, 256), sds(4, 8, H)], weights,
                           (meta, done["sum"], hs, done["gl"]) + node_args, 12)
        *got, done["node"][4] = lax.optimization_barrier((*got, done["node"][4]))
        return got

    received = exchange(outs[4:], beside_z, beside_y)
    gl = done["gl"]
    up, dh, dz_inner, g4, g_sums = done["node"]
    outs = run(node_outer_kernel, "node_outer", [LATTICE] * 3 + [sds(4 * H + 32, H)] + [PLANE] * 6,
               [acc, pltpu.VMEM((4, 256, 256), F32), pltpu.VMEM((4, 8, H), F32)] + weights,
               (meta, outer_sum, hs, gl) + node_args + (up, dh, g4, g_sums, *received), 8)
    up, dh, dz_outer, ngrad = outs[:4]

    def back_inner(first, last, dz):
        return run(functools.partial(back_inner_kernel, first, last), "back_inner", [LATTICE] * 2 + [sds(256, 256), sds(8, H)],
                   [square] * 3 + [pltpu.VMEM((1,) + FULL[1:], F32)], (meta, dz, tv, sv, edge_mid, node_in, edge_bias), 10)

    done = {}

    def under_z(*got):
        done["a"] = back_inner(1, HALF, dz_inner)
        *got, done["a"][2] = lax.optimization_barrier((*got, done["a"][2]))
        return got

    def under_y(*got):
        done["b"] = back_inner(HALF, SIDE, dz_inner)
        *got, done["b"][2] = lax.optimization_barrier((*got, done["b"][2]))
        return got

    received = exchange(outs[4:], under_z, under_y)
    new_feat, = run(new_feat_kernel, "new_feat", [sds(ROWS, H)], [], (meta, up, node_feat, lattice_of, node_bias), 4)
    received[0], new_feat = lax.optimization_barrier((received[0], new_feat))
    part_a, part_b = done["a"], done["b"]
    feat_grad, payload = run(back_outer_kernel, "back_outer", [sds(ROWS, H), sds(PAYLOAD, H)],
                             [acc] * 3 + [square] * 5 + [total] * 3 + [pltpu.VMEM((2, 8, H), F32)],
                             (meta, dz_outer, tv, sv, hs, dh, out_grad, lattice_of, edge_in, edge_mid, node_in, edge_bias, ngrad, *part_a, *part_b, *received), 16)
    total = total_over_devices(payload)
    scale = 1.0 / math.sqrt(n * ELEM_DEV * NODES_EL)
    weights = pl.pallas_call(
        functools.partial(finish_kernel, scale),
        out_shape=(sds(256, H), sds(2, H, H), sds(3, H), sds(256, H), sds(2, H, H), sds(3, H)),
        in_specs=[VM] * 4, out_specs=(VM,) * 6, name="finish", compiler_params=SMALL,
    )(total, edge_mid, node_in, edge_bias)
    return (new_feat, feat_grad) + tuple(weights)


def solution(mesh):
    in_specs = (P("dom", None),) * 4 + (P(),) * 6
    out_specs = (P("dom", None), P("dom", None)) + (P(),) * 6
    return jax.shard_map(body, mesh=mesh, in_specs=in_specs, out_specs=out_specs, check_vma=False)
```

```python
import functools
import math

import jax
import jax.numpy as jnp
from jax import lax
from jax.experimental import pallas as pl
from jax.experimental.pallas import tpu as pltpu
from jax.sharding import PartitionSpec as P

SIDE = 8
ELEM_DEV = 8
DGX = 4
DGY = 4
NODES_EL = 512
H = 128
ROWS = ELEM_DEV * NODES_EL
PAYLOAD = 1024
F32 = jnp.float32
BF16 = jnp.bfloat16


def split(x):
    high = x.astype(BF16)
    low = (x - high.astype(F32)).astype(BF16)
    return jnp.concatenate([high, low], axis=-1)


def weight_split(w):
    row = split(w)
    return jnp.concatenate([row, row], axis=0)


def dot(a, b):
    return jnp.dot(a, b, preferred_element_type=F32)


def fold(o):
    return o[:, :H] + o[:, H:]


def mm(xs, w):
    return fold(dot(xs, w))


def mm_t(xs, ys):
    return lax.dot_general(xs, ys, (((0,), (0,)), ((), ())), preferred_element_type=F32)


def quad(o):
    return o[:H, :H] + o[:H, H:] + o[H:, :H] + o[H:, H:]


def row_sum(x):
    return jnp.sum(x.reshape(-1, 8, H), axis=0)


def exact_dot(a, b):
    return jnp.dot(a, b, precision=lax.Precision.HIGHEST, preferred_element_type=F32)


def flip(e):
    return (e // 4) * 448 + (e // 2 % 2) * 56 + (e % 2) * 7


def to_lattice_onehot(lat_ref, slot, e):
    row = lat_ref[pl.ds(slot, 1), :] ^ flip(e)
    level = lax.broadcasted_iota(jnp.int32, (NODES_EL, NODES_EL), 0)
    return jnp.where(level == row, 1.0, 0.0).astype(BF16)


def from_lattice_onehot(turned, slot, e):
    lane = lax.broadcasted_iota(jnp.int32, (NODES_EL, ELEM_DEV), 1)
    column = jnp.sum(jnp.where(lane == slot, turned, 0.0), axis=1, keepdims=True).astype(jnp.int32) ^ flip(e)
    level = lax.broadcasted_iota(jnp.int32, (NODES_EL, NODES_EL), 1)
    return jnp.where(level == column, 1.0, 0.0).astype(BF16)


def slot_of(place, e):
    slot = jnp.int32(0)
    for i in range(1, ELEM_DEV):
        slot = jnp.where(place[0, i] == e, jnp.int32(i), slot)
    return slot


def slot_rows(slot):
    return pl.ds(pl.multiple_of(slot * NODES_EL, NODES_EL), NODES_EL)


def element_rows(e):
    return pl.ds(e, NODES_EL, stride=ELEM_DEV)


def to_lattice(place, lat_ref, src_ref, dst_ref):
    def one(e, carry):
        slot = slot_of(place, e)
        both = dot(to_lattice_onehot(lat_ref, slot, e), split(src_ref[slot_rows(slot), :]))
        dst_ref[element_rows(e), :] = fold(both)
        return carry

    lax.fori_loop(0, ELEM_DEV, one, 0)


def from_lattice(place, lat_ref, src_ref, add_ref, dst_ref, bias):
    turned = lat_ref[...].astype(F32).T

    def one(e, carry):
        slot = slot_of(place, e)
        back = from_lattice_onehot(turned, slot, e)
        rows = fold(dot(back, split(src_ref[element_rows(e), :])))
        rows = rows + add_ref[slot_rows(slot), :]
        dst_ref[slot_rows(slot), :] = rows if bias is None else rows + bias
        return carry

    lax.fori_loop(0, ELEM_DEV, one, 0)


FULL = (SIDE, SIDE, SIDE, ELEM_DEV, H)
OUTER = [((0, 1), (0, 8), (0, 8)), ((1, 8), (0, 1), (0, 8)), ((1, 8), (1, 8), (0, 1))]
INNER = [((1, 8), (1, 8), (1, 8))]


def at_box(box):
    return tuple(pl.ds(a, b - a) for a, b in box)


def get(ref, box):
    return ref[at_box(box)].reshape(-1, H)


def shape_of(box):
    return tuple(b - a for a, b in box) + (ELEM_DEV, H)


def put(ref, box, rows):
    ref[at_box(box)] = rows.reshape(shape_of(box))


def add(ref, box, rows):
    ref[at_box(box)] += rows.reshape(shape_of(box))


def pairs_of(box):
    out = []
    for axis in range(3):
        for step in (1, -1):
            a, b = box[axis]
            a, b = (a, min(b, SIDE - 1)) if step == 1 else (max(a, 1), b)
            if a < b:
                out.append((box[:axis] + ((a, b),) + box[axis + 1:], box[:axis] + ((a + step, b + step),) + box[axis + 1:]))
    return out


SLAB = ((1, 8), (1, 8))


def slab_pairs(x):
    out = [((x, SLAB), (x - 1, SLAB), None)]
    for axis in range(2):
        for step in (1, -1):
            a, b = (1, SIDE - 1) if step == 1 else (1, SIDE)
            receivers = SLAB[:axis] + ((a, b),) + SLAB[axis + 1:]
            senders = SLAB[:axis] + ((a + step, b + step),) + SLAB[axis + 1:]
            out.append(((x, receivers), (x, senders), None))
    upper = jnp.where(x < SIDE - 1, 1.0, 0.0)
    out.append(((x, SLAB), (jnp.minimum(x + 1, SIDE - 1), SLAB), upper))
    return out


def at_slab(where):
    x, box = where
    return (x,) + tuple(pl.ds(a, b - a) for a, b in box)


def sget(ref, where):
    return ref[at_slab(where)].reshape(-1, H)


def sshape(where):
    return tuple(b - a for a, b in where[1]) + (ELEM_DEV, H)


def sput(ref, where, rows):
    ref[at_slab(where)] = rows.reshape(sshape(where))


def sadd(ref, where, rows):
    ref[at_slab(where)] += rows.reshape(sshape(where))


def swap(v, axis):
    if axis == 0:
        return pltpu.roll(v, 4, 1)
    by = 2 if axis == 1 else 1
    e = lax.broadcasted_iota(jnp.int32, v.shape, 1)
    return jnp.where((e & by) == 0, pltpu.roll(v, ELEM_DEV - by, 1), pltpu.roll(v, by, 1))


def assemble(ref, boxes):
    for axis in (2, 1, 0):
        for box in boxes:
            if box[axis][1] == SIDE:
                face = box[:axis] + ((SIDE - 1, SIDE),) + box[axis + 1:]
                v = ref[at_box(face)].reshape(-1, ELEM_DEV, H)
                put(ref, face, v + swap(v, axis))


def bits(p):
    return p // 4, p // 2 % 2, p % 2


def slot_in_plane(axis, p):
    px, py, pz = bits(p)
    return (py * 2 + pz, px * 2 + pz, px * 2 + py)[axis]


def outer_rows(axis, e):
    if axis == 0:
        return [(pl.ds(e, 64, stride=8), pl.ds(0, 64))]
    if axis == 2:
        return [(pl.ds(e, 64, stride=64), pl.ds(0, 64))]
    return [(pl.ds(x * 512 + e, 8, stride=8), pl.ds(x * 8, 8)) for x in range(SIDE)]


def emit_planes(ref, planes):
    flat = ref.reshape((ROWS, H))
    for axis in range(3):
        for e in range(ELEM_DEV):
            for rows, there in outer_rows(axis, e):
                planes[axis][bits(e)[axis]][slot_in_plane(axis, e), there, :] = flat[rows, :]


def add_planes(ref, planes):
    flat = ref.reshape((ROWS, H))
    for axis in range(3):
        for e in range(ELEM_DEV):
            for rows, there in outer_rows(axis, e):
                flat[rows, :] += planes[axis][bits(e)[axis]][slot_in_plane(axis, e), there, :]


def half_silu(u):
    t = jnp.tanh(u)
    q = 1.0 + t
    return t, q, u * q


def twice_slope(t, q, s):
    return q + s * (1.0 - t)


def forward_edge(u1, w2, bias):
    _, _, s1 = half_silu(u1)
    _, _, s2 = half_silu(mm(split(s1), w2[...]) + bias)
    return s2


def edge_outer_kernel(place, h_hbm, lat_hbm, win_hbm, wmid_hbm, eb_hbm, hs_ref, t_ref, s_ref, sum_ref, xl, xh, yl, yh, zl, zh,
                      wts, w2, h_ref, lat_ref, win_ref, wmid_ref, eb_ref, sems, h_sems):
    small = [pltpu.make_async_copy(a, b, sems.at[i]) for i, (a, b) in enumerate(
        ((lat_hbm, lat_ref), (win_hbm, win_ref), (wmid_hbm, wmid_ref), (eb_hbm, eb_ref)))]
    for copy in small:
        copy.start()

    def rows_of(e):
        return pltpu.make_async_copy(h_hbm.at[slot_rows(slot_of(place, e)), :], h_ref.at[e], h_sems.at[e])

    for e in range(ELEM_DEV):
        rows_of(e).start()
    for copy in small:
        copy.wait()
    wts[:, 0:256] = weight_split(0.5 * win_ref[0:H, :])
    wts[:, 256:512] = weight_split(0.5 * win_ref[H:, :])
    w2[...] = weight_split(0.5 * wmid_ref[0])
    flat = hs_ref.reshape((ROWS, H))

    def one(e, carry):
        rows_of(e).wait()
        both = dot(to_lattice_onehot(lat_ref, slot_of(place, e), e), split(h_ref[e]))
        flat[element_rows(e), :] = fold(both)
        return carry

    lax.fori_loop(0, ELEM_DEV, one, 0)
    half_bias = 0.5 * eb_ref[0:1, :]

    def plane(x, carry):
        both = dot(split(hs_ref[x].reshape(-1, H)), wts[...])
        t_ref[x] = (fold(both[:, 0:256]) + half_bias).reshape(FULL[1:])
        s_ref[x] = fold(both[:, 256:512]).reshape(FULL[1:])
        return carry

    lax.fori_loop(0, SIDE, plane, 0)
    bias = 0.5 * eb_ref[1:2, :]
    for box in OUTER:
        put(sum_ref, box, jnp.zeros((math.prod(shape_of(box)) // H, H), F32))
        for receivers, senders in pairs_of(box):
            add(sum_ref, receivers, forward_edge(get(t_ref, receivers) + get(s_ref, senders), w2, bias))
    assemble(sum_ref, OUTER)
    emit_planes(sum_ref, ((xl, xh), (yl, yh), (zl, zh)))


def edge_inner_kernel(place, t_ref, s_ref, g_ref, lat_ref, wmid_ref, eb_ref, sum_ref, gl_ref, w2):
    w2[...] = weight_split(0.5 * wmid_ref[0])
    bias = 0.5 * eb_ref[1:2, :]

    def plane(x, carry):
        sput(sum_ref, (x, SLAB), jnp.zeros((49 * 8, H), F32))
        for receivers, senders, factor in slab_pairs(x):
            s2 = forward_edge(sget(t_ref, receivers) + sget(s_ref, senders), w2, bias)
            sadd(sum_ref, receivers, s2 if factor is None else s2 * factor)
        return carry

    lax.fori_loop(1, SIDE, plane, 0)
    assemble(sum_ref, INNER)
    to_lattice(place, lat_ref, g_ref, gl_ref.reshape((ROWS, H)))


def degree_of(where, shape):
    full = shape + (ELEM_DEV, H)
    e = lax.broadcasted_iota(jnp.int32, (ELEM_DEV, H), 0)
    count, own = None, None
    index, depth = lax.axis_index("dom"), lax.axis_size("dom") // (DGX * DGY)
    grid = (index % DGX, index // DGX % DGY, index // (DGX * DGY))
    for axis, limit in ((0, DGX), (1, DGY), (2, depth)):
        side = (e >> (2 - axis)) & 1
        low = jnp.where(grid[axis] > 0, 2.0, 1.0)
        high = jnp.where(grid[axis] < limit - 1, 2.0, 1.0)
        outer = jnp.broadcast_to(jnp.where(side == 0, low, high), full)
        at = lax.broadcasted_iota(jnp.int32, full, axis) + where[axis]
        times = jnp.where(at == 0, outer, jnp.where(at == SIDE - 1, 2.0, 1.0))
        messages = jnp.where((at == 0) | (at == SIDE - 1), 1.0, 2.0)
        count = times if count is None else count * times
        own = messages if own is None else own + messages
    return (count * own).reshape(-1, H)


def node_weights(nin_ref, nmid_ref, wmid_ref, eb_ref, weights):
    wa, wc, w0, w0t, w1t, row = weights
    lower = nin_ref[H:, :]
    wa[...] = weight_split(0.5 * nin_ref[0:H, :])
    wc[...] = weight_split(0.5 * exact_dot(wmid_ref[1], lower))
    w0[...] = weight_split(0.5 * nmid_ref[0])
    w0t[...] = weight_split(0.5 * nmid_ref[0].T)
    w1t[...] = weight_split(0.5 * nmid_ref[1].T)
    row[...] = 0.5 * exact_dot(jnp.broadcast_to(eb_ref[2:3, :], (8, H)), lower)


def node_chunk(gathered, h, g, degree, nb_ref, weights, totals, sums):
    wa, wc, w0, w0t, w1t, row = weights
    g_a, g_m, g_0, g_1 = totals
    hs = split(h)
    gs = split(gathered)
    u = mm(hs, wa[...]) + mm(gs, wc[...]) + degree * row[0:1, :] + 0.5 * nb_ref[0:1, :]
    t, q, s = half_silu(u)
    slope = twice_slope(t, q, s)
    ss = split(s)
    t, q, s = half_silu(mm(ss, w0[...]) + 0.5 * nb_ref[1:2, :])
    slope1 = twice_slope(t, q, s)
    ss1 = split(s)
    hidden = s
    gl = split(g)
    sums[2] += row_sum(g)
    g_1[...] += mm_t(ss1, gl)
    dz1 = mm(gl, w1t[...]) * slope1
    sums[1] += row_sum(dz1)
    dz1s = split(dz1)
    g_0[...] += mm_t(ss, dz1s)
    dz = mm(dz1s, w0t[...]) * slope
    sums[0] += row_sum(dz)
    sums[3] += row_sum(dz * degree)
    dzs = split(dz)
    g_a[...] += mm_t(hs, dzs)
    g_m[...] += mm_t(gs, dzs)
    return hidden, dz


def node_inner_kernel(place, sum_ref, hs_ref, gl_ref, nin_ref, nmid_ref, nb_ref, wmid_ref, eb_ref, hid_hbm, raw_hbm, dz_ref, g_out, sums_out, hid_ref, raw_ref, sems, *weights):
    node_weights(nin_ref, nmid_ref, wmid_ref, eb_ref, weights)
    totals = [g_out.at[i] for i in range(4)]
    g_out[...] = jnp.zeros_like(g_out)
    sums_out[...] = jnp.zeros_like(sums_out)

    def plane(x, carry):
        where = (x, SLAB)
        degree = degree_of((x, 1, 1), (1, 7, 7))
        hidden, dz = node_chunk(sget(sum_ref, where), sget(hs_ref, where), sget(gl_ref, where), degree, nb_ref, weights, totals, sums_out)
        sput(hid_ref, where, hidden)
        sput(dz_ref, where, dz)
        sput(raw_ref, where, dz)
        for copy in copies(x):
            copy.start()
        return carry

    def copies(x):
        at = at_slab((x, SLAB))
        return [pltpu.make_async_copy(a.at[at], b.at[at], sems.at[i, x]) for i, (a, b) in enumerate(((hid_ref, hid_hbm), (raw_ref, raw_hbm)))]

    lax.fori_loop(1, SIDE, plane, 0)
    assemble(dz_ref, INNER)
    for x in range(1, SIDE):
        for copy in copies(x):
            copy.wait()


def node_outer_kernel(place, sum_ref, hs_ref, gl_ref, nin_ref, nmid_ref, nb_ref, wmid_ref, eb_ref, g_in, sums_in,
                      rxl, rxh, ryl, ryh, rzl, rzh, hid_hbm, raw_hbm, dz_ref, grad_ref, xl, xh, yl, yh, zl, zh, acc, totals_ref, sums, hid_ref, raw_ref, sems, *weights):
    node_weights(nin_ref, nmid_ref, wmid_ref, eb_ref, weights)
    totals_ref[...] = g_in[...]
    sums[...] = sums_in[...]
    totals = [totals_ref.at[i] for i in range(4)]
    for box in OUTER:
        acc[at_box(box)] = sum_ref[at_box(box)]
    add_planes(acc, ((rxl, rxh), (ryl, ryh), (rzl, rzh)))
    for box in OUTER:
        degree = degree_of(tuple(a for a, _ in box), tuple(b - a for a, b in box))
        hidden, dz = node_chunk(get(acc, box), get(hs_ref, box), get(gl_ref, box), degree, nb_ref, weights, totals, sums)
        put(hid_ref, box, hidden)
        put(dz_ref, box, dz)
        put(raw_ref, box, dz)
    copies = [pltpu.make_async_copy(a.at[at_box(box)], b.at[at_box(box)], sems.at[i, j])
              for i, (a, b) in enumerate(((hid_ref, hid_hbm), (raw_ref, raw_hbm))) for j, box in enumerate(OUTER)]
    for copy in copies:
        copy.start()
    assemble(dz_ref, OUTER)
    emit_planes(dz_ref, ((xl, xh), (yl, yh), (zl, zh)))
    grad_ref[0:H, :] = quad(totals_ref[1])
    grad_ref[H:2 * H, :] = quad(totals_ref[0])
    grad_ref[2 * H:3 * H, :] = quad(totals_ref[2])
    grad_ref[3 * H:4 * H, :] = quad(totals_ref[3])
    for i in range(4):
        grad_ref[4 * H + i * 8:4 * H + i * 8 + 8, :] = sums[i]
    for copy in copies:
        copy.wait()


def merge_copies(inner_hbm, outer_hbm, dst, sems):
    parts = [(inner_hbm, INNER[0])] + [(outer_hbm, box) for box in OUTER]
    return [pltpu.make_async_copy(a.at[at_box(box)], dst.at[at_box(box)], sems.at[i]) for i, (a, box) in enumerate(parts)]


def new_feat_kernel(place, hid_inner, hid_outer, h_ref, lat_ref, nmid_ref, nb_ref, new_ref, acc, hid, sems, w1):
    copies = merge_copies(hid_inner, hid_outer, hid, sems)
    for copy in copies:
        copy.start()
    w1[...] = weight_split(nmid_ref[1])
    for copy in copies:
        copy.wait()

    def plane(x, carry):
        acc[x] = mm(split(hid[x].reshape(-1, H)), w1[...]).reshape(FULL[1:])
        return carry

    lax.fori_loop(0, SIDE, plane, 0)
    from_lattice(place, lat_ref, acc.reshape((ROWS, H)), h_ref, new_ref, nb_ref[2:3, :])


def feat_grad_kernel(place, dt_hbm, ds_hbm, raw_inner, raw_outer, g_ref, lat_ref, win_ref, nin_ref, feat_ref, acc, dt_ref, ds_ref, raw, sems, slab_sems, wtt, wst, wat):
    copies = merge_copies(raw_inner, raw_outer, raw, sems)
    for copy in copies:
        copy.start()

    def slabs(x):
        return [pltpu.make_async_copy(a.at[x], b.at[x], slab_sems.at[i, x]) for i, (a, b) in enumerate(((dt_hbm, dt_ref), (ds_hbm, ds_ref)))]

    for x in range(SIDE):
        for copy in slabs(x):
            copy.start()
    wtt[...] = weight_split(win_ref[0:H, :].T)
    wst[...] = weight_split(win_ref[H:, :].T)
    wat[...] = weight_split(nin_ref[0:H, :].T)
    for copy in copies:
        copy.wait()

    def plane(x, carry):
        for copy in slabs(x):
            copy.wait()
        dh = mm(split(dt_ref[x].reshape(-1, H)), wtt[...]) + mm(split(ds_ref[x].reshape(-1, H)), wst[...]) + mm(split(raw[x].reshape(-1, H)), wat[...])
        acc[x] = dh.reshape(FULL[1:])
        return carry

    lax.fori_loop(0, SIDE, plane, 0)
    from_lattice(place, lat_ref, acc.reshape((ROWS, H)), g_ref, feat_ref, None)


def back_weights(wmid_ref, nin_ref, w2, w2t, wct):
    w2[...] = weight_split(0.5 * wmid_ref[0])
    w2t[...] = weight_split(0.5 * wmid_ref[0].T)
    wct[...] = weight_split(0.5 * exact_dot(wmid_ref[1], nin_ref[H:, :]).T)


def backward_edge(u1, cot, w2, w2t, bias, g_2, total):
    t1, q1, s1 = half_silu(u1)
    s1s = split(s1)
    t2, q2, s2 = half_silu(mm(s1s, w2[...]) + bias)
    dz2 = cot * twice_slope(t2, q2, s2)
    total[...] += row_sum(dz2)
    dz2s = split(dz2)
    g_2[...] += mm_t(s1s, dz2s)
    return mm(dz2s, w2t[...]) * twice_slope(t1, q1, s1)


def back_inner_kernel(first, last, place, dz_ref, t_ref, s_ref, wmid_ref, nin_ref, eb_ref, dt_ref, ds_ref, g2_ref, total_ref, w2, w2t, wct, cot):
    back_weights(wmid_ref, nin_ref, w2, w2t, wct)
    bias = 0.5 * eb_ref[1:2, :]
    g2_ref[...] = jnp.zeros_like(g2_ref)
    total_ref[...] = jnp.zeros_like(total_ref)

    def clear(x, carry):
        ds_ref[x] = jnp.zeros(FULL[1:], F32)
        return carry

    lax.fori_loop(0, SIDE, clear, 0)

    def plane(x, carry):
        sput(dt_ref, (x, SLAB), jnp.zeros((49 * 8, H), F32))
        cot[0, pl.ds(1, 7), pl.ds(1, 7)] = mm(split(sget(dz_ref, (x, SLAB))), wct[...]).reshape(7, 7, ELEM_DEV, H)
        for receivers, senders, factor in slab_pairs(x):
            g = sget(cot, (0, receivers[1]))
            g = g if factor is None else g * factor
            dz1 = backward_edge(sget(t_ref, receivers) + sget(s_ref, senders), g, w2, w2t, bias, g2_ref, total_ref)
            sadd(dt_ref, receivers, dz1)
            sadd(ds_ref, senders, dz1)
        return carry

    lax.fori_loop(first, last, plane, 0)


def back_outer_kernel(place, dz_ref, t_ref, s_ref, hs_ref, wmid_ref, nin_ref, eb_ref, ngrad_ref, dt_a, ds_a, g2_a, total_a, dt_b, ds_b, g2_b, total_b,
                      rxl, rxh, ryl, ryh, rzl, rzh, grad_ref, dt_hbm, ds_hbm, acc, dt_ref, ds_ref, sems, w2, w2t, wct, g_2, g_t, g_s, sums):
    back_weights(wmid_ref, nin_ref, w2, w2t, wct)
    g_2[...] = g2_a[...] + g2_b[...]
    g_t[...] = jnp.zeros_like(g_t)
    g_s[...] = jnp.zeros_like(g_s)
    sums[0] = jnp.zeros((8, H), F32)
    sums[1] = total_a[...] + total_b[...]
    bias = 0.5 * eb_ref[1:2, :]
    for box in OUTER:
        acc[at_box(box)] = dz_ref[at_box(box)]
    add_planes(acc, ((rxl, rxh), (ryl, ryh), (rzl, rzh)))

    def senders_so_far(x, carry):
        ds_ref[x] = ds_a[x] + ds_b[x]
        return carry

    lax.fori_loop(0, SIDE, senders_so_far, 0)
    for source, first, last in ((dt_a, 1, HALF), (dt_b, HALF, SIDE)):
        dt_ref[first:last, 1:, 1:] = source[first:last, 1:, 1:]
    for box in OUTER:
        put(acc, box, mm(split(get(acc, box)), wct[...]))
        put(dt_ref, box, jnp.zeros((math.prod(shape_of(box)) // H, H), F32))
        for receivers, senders in pairs_of(box):
            dz1 = backward_edge(get(t_ref, receivers) + get(s_ref, senders), get(acc, receivers), w2, w2t, bias, g_2, sums.at[1])
            add(dt_ref, receivers, dz1)
            add(ds_ref, senders, dz1)

    def copies(x):
        return [pltpu.make_async_copy(a.at[x], b.at[x], sems.at[i, x]) for i, (a, b) in enumerate(((dt_ref, dt_hbm), (ds_ref, ds_hbm)))]

    for x in range(SIDE):
        for copy in copies(x):
            copy.start()

    def plane(x, carry):
        dt = dt_ref[x].reshape(-1, H)
        dts = split(dt)
        dss = split(ds_ref[x].reshape(-1, H))
        hs = split(hs_ref[x].reshape(-1, H))
        sums[0] += row_sum(dt)
        g_t[...] += mm_t(hs, dts)
        g_s[...] += mm_t(hs, dss)
        return carry

    lax.fori_loop(0, SIDE, plane, 0)
    grad_ref[0:4 * H, :] = ngrad_ref[0:4 * H, :]
    grad_ref[4 * H:5 * H, :] = quad(g_t[...])
    grad_ref[5 * H:6 * H, :] = quad(g_s[...])
    grad_ref[6 * H:7 * H, :] = quad(g_2[...])
    grad_ref[7 * H:, :] = jnp.zeros((PAYLOAD - 7 * H, H), F32)
    for i in range(4):
        grad_ref[7 * H + i:7 * H + i + 1, :] = jnp.sum(ngrad_ref[4 * H + i * 8:4 * H + i * 8 + 8, :], axis=0, keepdims=True)
    for i in range(2):
        grad_ref[7 * H + 4 + i:7 * H + 5 + i, :] = jnp.sum(sums[i], axis=0, keepdims=True)
    for x in range(SIDE):
        for copy in copies(x):
            copy.wait()


def finish_kernel(scale, total_ref, wmid_ref, nin_ref, eb_ref, ein_ref, emid_ref, ebias_ref, nino_ref, nmid_ref, nbias_ref):
    def rows(i):
        return total_ref[i * H:(i + 1) * H, :]

    m = rows(0)
    lower = nin_ref[H:, :]
    v = total_ref[7 * H + 3:7 * H + 4, :]
    ein_ref[0:H, :] = rows(4) * scale
    ein_ref[H:, :] = rows(5) * scale
    emid_ref[0] = rows(6) * scale
    emid_ref[1] = exact_dot(m, lower.T) * scale
    ebias_ref[0:2, :] = total_ref[7 * H + 4:7 * H + 6, :] * scale
    ebias_ref[2:3, :] = exact_dot(jnp.broadcast_to(v, (8, H)), lower.T)[0:1] * scale
    nino_ref[0:H, :] = rows(1) * scale
    outer = eb_ref[2:3, :].T * v
    nino_ref[H:, :] = (exact_dot(wmid_ref[1].T, m) + outer) * scale
    nmid_ref[0] = rows(2) * scale
    nmid_ref[1] = rows(3) * scale
    nbias_ref[...] = total_ref[7 * H:7 * H + 3, :] * scale


def fix_y_kernel(yl, yh, rzl, rzh, oyl, oyh):
    rz, out = (rzl, rzh), (oyl, oyh)
    oyl[...] = yl[...]
    oyh[...] = yh[...]
    line = pl.ds(0, 8, stride=SIDE)
    for p in range(8):
        b = bits(p)
        out[b[1]][slot_in_plane(1, p), line, :] += rz[b[2]][slot_in_plane(2, p), line, :]


def fix_x_kernel(xl, xh, rzl, rzh, ryl, ryh, oxl, oxh):
    rz, ry, out = (rzl, rzh), (ryl, ryh), (oxl, oxh)
    oxl[...] = xl[...]
    oxh[...] = xh[...]
    first = pl.ds(0, 8)
    for p in range(8):
        b = bits(p)
        mine = slot_in_plane(0, p)
        out[b[0]][mine, pl.ds(0, 8, stride=SIDE), :] += rz[b[2]][slot_in_plane(2, p), first, :]
        out[b[0]][mine, first, :] += ry[b[1]][slot_in_plane(1, p), first, :]


PLANE = jax.ShapeDtypeStruct((4, 64, H), F32)
VM = pl.BlockSpec(memory_space=pltpu.VMEM)
SM = pl.BlockSpec(memory_space=pltpu.SMEM)
HB = pl.BlockSpec(memory_space=pltpu.MemorySpace.HBM)


def in_hbm(*values):
    return [pltpu.with_memory_space_constraint(v, pltpu.MemorySpace.HBM) for v in values]


def shifted(block, distance):
    n = lax.axis_size("dom")
    depth = n // (DGX * DGY)
    limits, strides = (DGX, DGY, depth), (1, DGX, DGX * DGY)
    axis = strides.index(abs(distance))
    step = 1 if distance > 0 else -1
    route = []
    for i in range(n):
        to = i // strides[axis] % limits[axis] + step
        if 0 <= to < limits[axis]:
            route.append((i, i + distance))
    return lax.ppermute(block, "dom", route)


def sds(*shape, dtype=F32):
    return jax.ShapeDtypeStruct(shape, dtype)


HALF = 5
LATTICE = jax.ShapeDtypeStruct(FULL, F32)
LIMIT = 14
SMALL = pltpu.CompilerParams(vmem_limit_bytes=6 * 1024 * 1024)


def run(kernel, name, outs, scratch, args, micros, spec=VM, hbm_in=(), hbm_out=()):
    outs = [pltpu.MemorySpace.HBM(o.shape, o.dtype) if i in hbm_out else o for i, o in enumerate(outs)]
    call = pl.pallas_call(
        kernel, out_shape=outs, in_specs=[SM] + [HB if i in hbm_in else spec for i in range(1, len(args))], out_specs=[HB if i in hbm_out else VM for i in range(len(outs))], scratch_shapes=scratch,
        name=name,
        cost_estimate=pl.CostEstimate(flops=micros * 1000000000, bytes_accessed=8000000, transcendentals=0),
        compiler_params=pltpu.CompilerParams(vmem_limit_bytes=LIMIT * 1024 * 1024),
    )
    return list(call(*args))


def exchange(planes, beside_z, beside_y):
    xl, xh, yl, yh, zl, zh = planes
    with jax.named_scope("along_z"):
        rzh, rzl = shifted(zl, -DGX * DGY), shifted(zh, DGX * DGY)
    rzl, rzh = beside_z(rzl, rzh)
    yl, yh = pl.pallas_call(fix_y_kernel, out_shape=(PLANE, PLANE), in_specs=[VM] * 4, out_specs=(VM, VM), name="fix_y", compiler_params=SMALL)(yl, yh, rzl, rzh)
    with jax.named_scope("along_y"):
        ryh, ryl = shifted(yl, -DGX), shifted(yh, DGX)
    ryl, ryh = beside_y(ryl, ryh)
    xl, xh = pl.pallas_call(fix_x_kernel, out_shape=(PLANE, PLANE), in_specs=[VM] * 6, out_specs=(VM, VM), name="fix_x", compiler_params=SMALL)(xl, xh, rzl, rzh, ryl, ryh)
    with jax.named_scope("along_x"):
        rxh, rxl = shifted(xl, -1), shifted(xh, 1)
    return [rxl, rxh, ryl, ryh, rzl, rzh]


def total_over_devices(block, beside_first, beside_second):
    n = lax.axis_size("dom")
    parts = lax.all_to_all(block.reshape(n, -1, H), "dom", 0, 0, tiled=True)
    parts, first = lax.optimization_barrier((parts, beside_first()))
    mine = parts.sum(0)
    spread = jnp.broadcast_to(mine[None], (n,) + mine.shape)
    total = lax.all_to_all(spread, "dom", 0, 0, tiled=True)
    total, second = lax.optimization_barrier((total, beside_second()))
    return total.reshape(-1, H), first, second


def body(node_feat, out_grad, lattice_of, element_place, edge_in, edge_mid, edge_bias, node_in, node_mid, node_bias):
    n = lax.axis_size("dom")
    square, wide, acc = pltpu.VMEM((256, 256), BF16), pltpu.VMEM((256, 512), BF16), pltpu.VMEM(FULL, F32)
    total = pltpu.VMEM((256, 256), F32)

    outs = run(edge_outer_kernel, "edge_outer", [LATTICE] * 4 + [PLANE] * 6,
               [wide, square, pltpu.VMEM((ELEM_DEV, NODES_EL, H), F32), pltpu.VMEM((ELEM_DEV, NODES_EL), jnp.int32), pltpu.VMEM((256, H), F32),
                pltpu.VMEM((2, H, H), F32), pltpu.VMEM((3, H), F32), pltpu.SemaphoreType.DMA((4,)), pltpu.SemaphoreType.DMA((ELEM_DEV,))],
               (element_place, *in_hbm(node_feat, lattice_of, edge_in, edge_mid, edge_bias)), 8, HB)
    hs, tv, sv, outer_sum = outs[:4]
    node_args = (node_in, node_mid, node_bias, edge_mid, edge_bias)
    weights = [square] * 5 + [pltpu.VMEM((8, H), F32)]

    done = {}

    def beside_z(*got):
        inner_sum, gl = run(edge_inner_kernel, "edge_inner", [LATTICE] * 2, [square], (element_place, tv, sv, out_grad, lattice_of, edge_mid, edge_bias), 12)
        *got, done["sum"], done["gl"] = lax.optimization_barrier((*got, inner_sum, gl))
        return got

    def beside_y(*got):
        done["node"] = run(node_inner_kernel, "node_inner", [LATTICE] * 3 + [sds(4, 256, 256), sds(4, 8, H)], [acc, acc, pltpu.SemaphoreType.DMA((2, SIDE))] + weights,
                           (element_place, done["sum"], hs, done["gl"]) + node_args, 12, hbm_out=(0, 1))
        *got, done["node"][4] = lax.optimization_barrier((*got, done["node"][4]))
        return got

    received = exchange(outs[4:], beside_z, beside_y)
    gl = done["gl"]
    hid_inner, raw_inner, dz_inner, g4, g_sums = done["node"]
    outs = run(node_outer_kernel, "node_outer", [LATTICE] * 3 + [sds(4 * H + 32, H)] + [PLANE] * 6,
               [acc, pltpu.VMEM((4, 256, 256), F32), pltpu.VMEM((4, 8, H), F32), acc, acc, pltpu.SemaphoreType.DMA((2, 3))] + weights,
               (element_place, outer_sum, hs, gl) + node_args + (g4, g_sums, *received), 8, hbm_out=(0, 1))
    hid_outer, raw_outer, dz_outer, ngrad = outs[:4]
    hid_inner, raw_inner, hid_outer, raw_outer = in_hbm(hid_inner, raw_inner, hid_outer, raw_outer)

    def back_inner(first, last, dz):
        return run(functools.partial(back_inner_kernel, first, last), "back_inner", [LATTICE] * 2 + [sds(256, 256), sds(8, H)],
                   [square] * 3 + [pltpu.VMEM((1,) + FULL[1:], F32)], (element_place, dz, tv, sv, edge_mid, node_in, edge_bias), 10)

    done = {}

    def under_z(*got):
        done["a"] = back_inner(1, HALF, dz_inner)
        *got, done["a"][2] = lax.optimization_barrier((*got, done["a"][2]))
        return got

    def under_y(*got):
        done["b"] = back_inner(HALF, SIDE, dz_inner)
        *got, done["b"][2] = lax.optimization_barrier((*got, done["b"][2]))
        return got

    received = exchange(outs[4:], under_z, under_y)
    part_a, part_b = done["a"], done["b"]
    payload, dt, ds = run(back_outer_kernel, "back_outer", [sds(PAYLOAD, H), LATTICE, LATTICE],
                          [acc] * 3 + [pltpu.SemaphoreType.DMA((2, SIDE))] + [square] * 3 + [total] * 3 + [pltpu.VMEM((2, 8, H), F32)],
                          (element_place, dz_outer, tv, sv, hs, edge_mid, node_in, edge_bias, ngrad, *part_a, *part_b, *received), 10, hbm_out=(1, 2))
    dt, ds = in_hbm(dt, ds)

    def beside_first():
        return run(feat_grad_kernel, "feat_grad", [sds(ROWS, H)], [acc] * 4 + [pltpu.SemaphoreType.DMA((4,)), pltpu.SemaphoreType.DMA((2, SIDE))] + [square] * 3,
                   (element_place, dt, ds, raw_inner, raw_outer, out_grad, lattice_of, edge_in, node_in), 8, hbm_in=(1, 2, 3, 4))[0]

    def beside_second():
        return run(new_feat_kernel, "new_feat", [sds(ROWS, H)], [acc, acc, pltpu.SemaphoreType.DMA((4,)), square],
                   (element_place, hid_inner, hid_outer, node_feat, lattice_of, node_mid, node_bias), 8, hbm_in=(1, 2))[0]

    total, feat_grad, new_feat = total_over_devices(payload, beside_first, beside_second)
    scale = 1.0 / math.sqrt(n * ELEM_DEV * NODES_EL)
    weights = pl.pallas_call(
        functools.partial(finish_kernel, scale),
        out_shape=(sds(256, H), sds(2, H, H), sds(3, H), sds(256, H), sds(2, H, H), sds(3, H)),
        in_specs=[VM] * 4, out_specs=(VM,) * 6, name="finish", compiler_params=SMALL,
    )(total, edge_mid, node_in, edge_bias)
    return (new_feat, feat_grad) + tuple(weights)


def solution(mesh):
    in_specs = (P("dom", None),) * 4 + (P(),) * 6
    out_specs = (P("dom", None), P("dom", None)) + (P(),) * 6
    return jax.shard_map(body, mesh=mesh, in_specs=in_specs, out_specs=out_specs, check_vma=False)
```

```python
import functools
import math

import jax
import jax.numpy as jnp
from jax import lax
from jax.experimental import pallas as pl
from jax.experimental.pallas import tpu as pltpu
from jax.sharding import PartitionSpec as P

SIDE = 8
ELEM_DEV = 8
DGX = 4
DGY = 4
NODES_EL = 512
H = 128
ROWS = ELEM_DEV * NODES_EL
PAYLOAD = 1024
F32 = jnp.float32
BF16 = jnp.bfloat16


def split(x):
    high = x.astype(BF16)
    low = (x - high.astype(F32)).astype(BF16)
    return jnp.concatenate([high, low], axis=-1)


def weight_split(w):
    row = split(w)
    return jnp.concatenate([row, row], axis=0)


def dot(a, b):
    return jnp.dot(a, b, preferred_element_type=F32)


def fold(o):
    return o[:, :H] + o[:, H:]


def mm(xs, w):
    return fold(dot(xs, w))


def mm_t(xs, ys):
    return lax.dot_general(xs, ys, (((0,), (0,)), ((), ())), preferred_element_type=F32)


def quad(o):
    return o[:H, :H] + o[:H, H:] + o[H:, :H] + o[H:, H:]


def row_sum(x):
    return jnp.sum(x.reshape(-1, 8, H), axis=0)


def exact_dot(a, b):
    return jnp.dot(a, b, precision=lax.Precision.HIGHEST, preferred_element_type=F32)


def flip(e):
    return (e // 4) * 448 + (e // 2 % 2) * 56 + (e % 2) * 7


def to_lattice_onehot(lat_ref, slot, e):
    row = lat_ref[pl.ds(slot, 1), :] ^ flip(e)
    level = lax.broadcasted_iota(jnp.int32, (NODES_EL, NODES_EL), 0)
    return jnp.where(level == row, 1.0, 0.0).astype(BF16)


def from_lattice_onehot(turned, slot, e):
    lane = lax.broadcasted_iota(jnp.int32, (NODES_EL, ELEM_DEV), 1)
    column = jnp.sum(jnp.where(lane == slot, turned, 0.0), axis=1, keepdims=True).astype(jnp.int32) ^ flip(e)
    level = lax.broadcasted_iota(jnp.int32, (NODES_EL, NODES_EL), 1)
    return jnp.where(level == column, 1.0, 0.0).astype(BF16)


def slot_of(place, e):
    slot = jnp.int32(0)
    for i in range(1, ELEM_DEV):
        slot = jnp.where(place[0, i] == e, jnp.int32(i), slot)
    return slot


def slot_rows(slot):
    return pl.ds(pl.multiple_of(slot * NODES_EL, NODES_EL), NODES_EL)


def element_rows(e):
    return pl.ds(e, NODES_EL, stride=ELEM_DEV)


def to_lattice(place, lat_ref, src_ref, dst_ref):
    def one(e, carry):
        slot = slot_of(place, e)
        both = dot(to_lattice_onehot(lat_ref, slot, e), split(src_ref[slot_rows(slot), :]))
        dst_ref[element_rows(e), :] = fold(both)
        return carry

    lax.fori_loop(0, ELEM_DEV, one, 0)


def from_lattice(place, lat_ref, src_ref, add_ref, dst_ref, bias):
    turned = lat_ref[...].astype(F32).T

    def one(e, carry):
        slot = slot_of(place, e)
        back = from_lattice_onehot(turned, slot, e)
        rows = fold(dot(back, split(src_ref[element_rows(e), :])))
        rows = rows + add_ref[slot_rows(slot), :]
        dst_ref[slot_rows(slot), :] = rows if bias is None else rows + bias
        return carry

    lax.fori_loop(0, ELEM_DEV, one, 0)


FULL = (SIDE, SIDE, SIDE, ELEM_DEV, H)
OUTER = [((0, 1), (0, 8), (0, 8)), ((1, 8), (0, 1), (0, 8)), ((1, 8), (1, 8), (0, 1))]
INNER = [((1, 8), (1, 8), (1, 8))]


def at_box(box):
    return tuple(pl.ds(a, b - a) for a, b in box)


def get(ref, box):
    return ref[at_box(box)].reshape(-1, H)


def shape_of(box):
    return tuple(b - a for a, b in box) + (ELEM_DEV, H)


def put(ref, box, rows):
    ref[at_box(box)] = rows.reshape(shape_of(box))


def add(ref, box, rows):
    ref[at_box(box)] += rows.reshape(shape_of(box))


def pairs_of(box):
    out = []
    for axis in range(3):
        for step in (1, -1):
            a, b = box[axis]
            a, b = (a, min(b, SIDE - 1)) if step == 1 else (max(a, 1), b)
            if a < b:
                out.append((box[:axis] + ((a, b),) + box[axis + 1:], box[:axis] + ((a + step, b + step),) + box[axis + 1:]))
    return out


SLAB = ((1, 8), (1, 8))


def slab_pairs(x):
    out = [((x, SLAB), (x - 1, SLAB), None)]
    for axis in range(2):
        for step in (1, -1):
            a, b = (1, SIDE - 1) if step == 1 else (1, SIDE)
            receivers = SLAB[:axis] + ((a, b),) + SLAB[axis + 1:]
            senders = SLAB[:axis] + ((a + step, b + step),) + SLAB[axis + 1:]
            out.append(((x, receivers), (x, senders), None))
    upper = jnp.where(x < SIDE - 1, 1.0, 0.0)
    out.append(((x, SLAB), (jnp.minimum(x + 1, SIDE - 1), SLAB), upper))
    return out


def at_slab(where):
    x, box = where
    return (x,) + tuple(pl.ds(a, b - a) for a, b in box)


def sget(ref, where):
    return ref[at_slab(where)].reshape(-1, H)


def sshape(where):
    return tuple(b - a for a, b in where[1]) + (ELEM_DEV, H)


def sput(ref, where, rows):
    ref[at_slab(where)] = rows.reshape(sshape(where))


def sadd(ref, where, rows):
    ref[at_slab(where)] += rows.reshape(sshape(where))


def swap(v, axis):
    if axis == 0:
        return pltpu.roll(v, 4, 1)
    by = 2 if axis == 1 else 1
    e = lax.broadcasted_iota(jnp.int32, v.shape, 1)
    return jnp.where((e & by) == 0, pltpu.roll(v, ELEM_DEV - by, 1), pltpu.roll(v, by, 1))


def assemble(ref, boxes):
    for axis in (2, 1, 0):
        for box in boxes:
            if box[axis][1] == SIDE:
                face = box[:axis] + ((SIDE - 1, SIDE),) + box[axis + 1:]
                v = ref[at_box(face)].reshape(-1, ELEM_DEV, H)
                put(ref, face, v + swap(v, axis))


STRIDES = (1, DGX, DGX * DGY)
BIT = (4, 2, 1)


def above():
    index = lax.axis_index("dom")
    return [1 - index // stride % 2 for stride in STRIDES]


def sides(axis):
    up = above()[axis]
    return up, 1 - up


def outer_rows(axis, e):
    if axis == 0:
        return [(pl.ds(e, 64, stride=8), pl.ds(0, 64))]
    if axis == 2:
        return [(pl.ds(e, 64, stride=64), pl.ds(0, 64))]
    return [(pl.ds(x * 512 + e, 8, stride=8), pl.ds(x * 8, 8)) for x in range(SIDE)]


def others(axis):
    return [e for e in range(ELEM_DEV) if not e & BIT[axis]]


def emit_planes(ref, planes):
    flat = ref.reshape((ROWS, H))
    for axis in range(3):
        for side, plane in zip(sides(axis), planes[axis]):
            for j, e in enumerate(others(axis)):
                for rows, there in outer_rows(axis, e + side * BIT[axis]):
                    plane[j, there, :] = flat[rows, :]


def add_planes(ref, planes):
    flat = ref.reshape((ROWS, H))
    for axis in range(3):
        for side, plane in zip(sides(axis), planes[axis]):
            for j, e in enumerate(others(axis)):
                for rows, there in outer_rows(axis, e + side * BIT[axis]):
                    flat[rows, :] += plane[j, there, :]


def half_silu(u):
    t = jnp.tanh(u)
    q = 1.0 + t
    return t, q, u * q


def twice_slope(t, q, s):
    return q + s * (1.0 - t)


def forward_edge(u1, w2, bias):
    _, _, s1 = half_silu(u1)
    _, _, s2 = half_silu(mm(split(s1), w2[...]) + bias)
    return s2


def edge_outer_kernel(place, h_hbm, lat_hbm, win_hbm, wmid_hbm, eb_hbm, hs_ref, t_ref, s_ref, sum_ref, x1, x2, y1, y2, z1, z2,
                      wts, w2, h_ref, lat_ref, win_ref, wmid_ref, eb_ref, sems, h_sems):
    small = [pltpu.make_async_copy(a, b, sems.at[i]) for i, (a, b) in enumerate(
        ((lat_hbm, lat_ref), (win_hbm, win_ref), (wmid_hbm, wmid_ref), (eb_hbm, eb_ref)))]
    for copy in small:
        copy.start()

    def rows_of(e):
        return pltpu.make_async_copy(h_hbm.at[slot_rows(slot_of(place, e)), :], h_ref.at[e], h_sems.at[e])

    for e in range(ELEM_DEV):
        rows_of(e).start()
    for copy in small:
        copy.wait()
    wts[:, 0:256] = weight_split(0.5 * win_ref[0:H, :])
    wts[:, 256:512] = weight_split(0.5 * win_ref[H:, :])
    w2[...] = weight_split(0.5 * wmid_ref[0])
    flat = hs_ref.reshape((ROWS, H))

    def one(e, carry):
        rows_of(e).wait()
        both = dot(to_lattice_onehot(lat_ref, slot_of(place, e), e), split(h_ref[e]))
        flat[element_rows(e), :] = fold(both)
        return carry

    lax.fori_loop(0, ELEM_DEV, one, 0)
    half_bias = 0.5 * eb_ref[0:1, :]

    def plane(x, carry):
        both = dot(split(hs_ref[x].reshape(-1, H)), wts[...])
        t_ref[x] = (fold(both[:, 0:256]) + half_bias).reshape(FULL[1:])
        s_ref[x] = fold(both[:, 256:512]).reshape(FULL[1:])
        return carry

    lax.fori_loop(0, SIDE, plane, 0)
    bias = 0.5 * eb_ref[1:2, :]
    for box in OUTER:
        put(sum_ref, box, jnp.zeros((math.prod(shape_of(box)) // H, H), F32))
        for receivers, senders in pairs_of(box):
            add(sum_ref, receivers, forward_edge(get(t_ref, receivers) + get(s_ref, senders), w2, bias))
    assemble(sum_ref, OUTER)
    emit_planes(sum_ref, ((x1, x2), (y1, y2), (z1, z2)))


def edge_inner_kernel(place, t_ref, s_ref, g_ref, lat_ref, wmid_ref, eb_ref, sum_ref, gl_ref, w2):
    w2[...] = weight_split(0.5 * wmid_ref[0])
    bias = 0.5 * eb_ref[1:2, :]

    def plane(x, carry):
        sput(sum_ref, (x, SLAB), jnp.zeros((49 * 8, H), F32))
        for receivers, senders, factor in slab_pairs(x):
            s2 = forward_edge(sget(t_ref, receivers) + sget(s_ref, senders), w2, bias)
            sadd(sum_ref, receivers, s2 if factor is None else s2 * factor)
        return carry

    lax.fori_loop(1, SIDE, plane, 0)
    assemble(sum_ref, INNER)
    to_lattice(place, lat_ref, g_ref, gl_ref.reshape((ROWS, H)))


def degree_of(where, shape):
    full = shape + (ELEM_DEV, H)
    e = lax.broadcasted_iota(jnp.int32, (ELEM_DEV, H), 0)
    count, own = None, None
    index, depth = lax.axis_index("dom"), lax.axis_size("dom") // (DGX * DGY)
    grid = (index % DGX, index // DGX % DGY, index // (DGX * DGY))
    for axis, limit in ((0, DGX), (1, DGY), (2, depth)):
        side = (e >> (2 - axis)) & 1
        low = jnp.where(grid[axis] > 0, 2.0, 1.0)
        high = jnp.where(grid[axis] < limit - 1, 2.0, 1.0)
        outer = jnp.broadcast_to(jnp.where(side == 0, low, high), full)
        at = lax.broadcasted_iota(jnp.int32, full, axis) + where[axis]
        times = jnp.where(at == 0, outer, jnp.where(at == SIDE - 1, 2.0, 1.0))
        messages = jnp.where((at == 0) | (at == SIDE - 1), 1.0, 2.0)
        count = times if count is None else count * times
        own = messages if own is None else own + messages
    return (count * own).reshape(-1, H)


def node_weights(nin_ref, nmid_ref, wmid_ref, eb_ref, weights):
    wa, wc, w0, w0t, w1t, row = weights
    lower = nin_ref[H:, :]
    wa[...] = weight_split(0.5 * nin_ref[0:H, :])
    wc[...] = weight_split(0.5 * exact_dot(wmid_ref[1], lower))
    w0[...] = weight_split(0.5 * nmid_ref[0])
    w0t[...] = weight_split(0.5 * nmid_ref[0].T)
    w1t[...] = weight_split(0.5 * nmid_ref[1].T)
    row[...] = 0.5 * exact_dot(jnp.broadcast_to(eb_ref[2:3, :], (8, H)), lower)


def node_chunk(gathered, h, g, degree, nb_ref, weights, totals, sums):
    wa, wc, w0, w0t, w1t, row = weights
    g_a, g_m, g_0, g_1 = totals
    hs = split(h)
    gs = split(gathered)
    u = mm(hs, wa[...]) + mm(gs, wc[...]) + degree * row[0:1, :] + 0.5 * nb_ref[0:1, :]
    t, q, s = half_silu(u)
    slope = twice_slope(t, q, s)
    ss = split(s)
    t, q, s = half_silu(mm(ss, w0[...]) + 0.5 * nb_ref[1:2, :])
    slope1 = twice_slope(t, q, s)
    ss1 = split(s)
    hidden = s
    gl = split(g)
    sums[2] += row_sum(g)
    g_1[...] += mm_t(ss1, gl)
    dz1 = mm(gl, w1t[...]) * slope1
    sums[1] += row_sum(dz1)
    dz1s = split(dz1)
    g_0[...] += mm_t(ss, dz1s)
    dz = mm(dz1s, w0t[...]) * slope
    sums[0] += row_sum(dz)
    sums[3] += row_sum(dz * degree)
    dzs = split(dz)
    g_a[...] += mm_t(hs, dzs)
    g_m[...] += mm_t(gs, dzs)
    return hidden, dz


def node_inner_kernel(place, sum_ref, hs_ref, gl_ref, nin_ref, nmid_ref, nb_ref, wmid_ref, eb_ref, hid_hbm, raw_hbm, dz_ref, g_out, sums_out, hid_ref, raw_ref, sems, *weights):
    node_weights(nin_ref, nmid_ref, wmid_ref, eb_ref, weights)
    totals = [g_out.at[i] for i in range(4)]
    g_out[...] = jnp.zeros_like(g_out)
    sums_out[...] = jnp.zeros_like(sums_out)

    def plane(x, carry):
        where = (x, SLAB)
        degree = degree_of((x, 1, 1), (1, 7, 7))
        hidden, dz = node_chunk(sget(sum_ref, where), sget(hs_ref, where), sget(gl_ref, where), degree, nb_ref, weights, totals, sums_out)
        sput(hid_ref, where, hidden)
        sput(dz_ref, where, dz)
        sput(raw_ref, where, dz)
        for copy in copies(x):
            copy.start()
        return carry

    def copies(x):
        at = at_slab((x, SLAB))
        return [pltpu.make_async_copy(a.at[at], b.at[at], sems.at[i, x]) for i, (a, b) in enumerate(((hid_ref, hid_hbm), (raw_ref, raw_hbm)))]

    lax.fori_loop(1, SIDE, plane, 0)
    assemble(dz_ref, INNER)
    for x in range(1, SIDE):
        for copy in copies(x):
            copy.wait()


def node_outer_kernel(place, sum_ref, hs_ref, gl_ref, nin_ref, nmid_ref, nb_ref, wmid_ref, eb_ref, g_in, sums_in,
                      rx1, rx2, ry1, ry2, rz1, rz2, hid_hbm, raw_hbm, dz_ref, grad_ref, x1, x2, y1, y2, z1, z2, acc, totals_ref, sums, hid_ref, raw_ref, sems, *weights):
    node_weights(nin_ref, nmid_ref, wmid_ref, eb_ref, weights)
    totals_ref[...] = g_in[...]
    sums[...] = sums_in[...]
    totals = [totals_ref.at[i] for i in range(4)]
    for box in OUTER:
        acc[at_box(box)] = sum_ref[at_box(box)]
    add_planes(acc, ((rx1, rx2), (ry1, ry2), (rz1, rz2)))
    for box in OUTER:
        degree = degree_of(tuple(a for a, _ in box), tuple(b - a for a, b in box))
        hidden, dz = node_chunk(get(acc, box), get(hs_ref, box), get(gl_ref, box), degree, nb_ref, weights, totals, sums)
        put(hid_ref, box, hidden)
        put(dz_ref, box, dz)
        put(raw_ref, box, dz)
    copies = [pltpu.make_async_copy(a.at[at_box(box)], b.at[at_box(box)], sems.at[i, j])
              for i, (a, b) in enumerate(((hid_ref, hid_hbm), (raw_ref, raw_hbm))) for j, box in enumerate(OUTER)]
    for copy in copies:
        copy.start()
    assemble(dz_ref, OUTER)
    emit_planes(dz_ref, ((x1, x2), (y1, y2), (z1, z2)))
    grad_ref[0:H, :] = quad(totals_ref[1])
    grad_ref[H:2 * H, :] = quad(totals_ref[0])
    grad_ref[2 * H:3 * H, :] = quad(totals_ref[2])
    grad_ref[3 * H:4 * H, :] = quad(totals_ref[3])
    for i in range(4):
        grad_ref[4 * H + i * 8:4 * H + i * 8 + 8, :] = sums[i]
    for copy in copies:
        copy.wait()


def merge_copies(inner_hbm, outer_hbm, dst, sems):
    parts = [(inner_hbm, INNER[0])] + [(outer_hbm, box) for box in OUTER]
    return [pltpu.make_async_copy(a.at[at_box(box)], dst.at[at_box(box)], sems.at[i]) for i, (a, box) in enumerate(parts)]


def new_feat_kernel(place, hid_inner, hid_outer, h_ref, lat_ref, nmid_ref, nb_ref, new_ref, acc, hid, sems, w1):
    copies = merge_copies(hid_inner, hid_outer, hid, sems)
    for copy in copies:
        copy.start()
    w1[...] = weight_split(nmid_ref[1])
    for copy in copies:
        copy.wait()

    def plane(x, carry):
        acc[x] = mm(split(hid[x].reshape(-1, H)), w1[...]).reshape(FULL[1:])
        return carry

    lax.fori_loop(0, SIDE, plane, 0)
    from_lattice(place, lat_ref, acc.reshape((ROWS, H)), h_ref, new_ref, nb_ref[2:3, :])


def feat_grad_kernel(place, dt_hbm, ds_hbm, raw_inner, raw_outer, g_ref, lat_ref, win_ref, nin_ref, feat_ref, acc, dt_ref, ds_ref, raw, sems, slab_sems, wtt, wst, wat):
    copies = merge_copies(raw_inner, raw_outer, raw, sems)
    for copy in copies:
        copy.start()

    def slabs(x):
        return [pltpu.make_async_copy(a.at[x], b.at[x], slab_sems.at[i, x]) for i, (a, b) in enumerate(((dt_hbm, dt_ref), (ds_hbm, ds_ref)))]

    for x in range(SIDE):
        for copy in slabs(x):
            copy.start()
    wtt[...] = weight_split(win_ref[0:H, :].T)
    wst[...] = weight_split(win_ref[H:, :].T)
    wat[...] = weight_split(nin_ref[0:H, :].T)
    for copy in copies:
        copy.wait()

    def plane(x, carry):
        for copy in slabs(x):
            copy.wait()
        dh = mm(split(dt_ref[x].reshape(-1, H)), wtt[...]) + mm(split(ds_ref[x].reshape(-1, H)), wst[...]) + mm(split(raw[x].reshape(-1, H)), wat[...])
        acc[x] = dh.reshape(FULL[1:])
        return carry

    lax.fori_loop(0, SIDE, plane, 0)
    from_lattice(place, lat_ref, acc.reshape((ROWS, H)), g_ref, feat_ref, None)


def back_weights(wmid_ref, nin_ref, w2, w2t, wct):
    w2[...] = weight_split(0.5 * wmid_ref[0])
    w2t[...] = weight_split(0.5 * wmid_ref[0].T)
    wct[...] = weight_split(0.5 * exact_dot(wmid_ref[1], nin_ref[H:, :]).T)


def backward_edge(u1, cot, w2, w2t, bias, g_2, total):
    t1, q1, s1 = half_silu(u1)
    s1s = split(s1)
    t2, q2, s2 = half_silu(mm(s1s, w2[...]) + bias)
    dz2 = cot * twice_slope(t2, q2, s2)
    total[...] += row_sum(dz2)
    dz2s = split(dz2)
    g_2[...] += mm_t(s1s, dz2s)
    return mm(dz2s, w2t[...]) * twice_slope(t1, q1, s1)


def back_inner_kernel(first, last, place, dz_ref, t_ref, s_ref, wmid_ref, nin_ref, eb_ref, dt_ref, ds_ref, g2_ref, total_ref, w2, w2t, wct, cot):
    back_weights(wmid_ref, nin_ref, w2, w2t, wct)
    bias = 0.5 * eb_ref[1:2, :]
    g2_ref[...] = jnp.zeros_like(g2_ref)
    total_ref[...] = jnp.zeros_like(total_ref)

    def clear(x, carry):
        ds_ref[x] = jnp.zeros(FULL[1:], F32)
        return carry

    lax.fori_loop(0, SIDE, clear, 0)

    def plane(x, carry):
        sput(dt_ref, (x, SLAB), jnp.zeros((49 * 8, H), F32))
        cot[0, pl.ds(1, 7), pl.ds(1, 7)] = mm(split(sget(dz_ref, (x, SLAB))), wct[...]).reshape(7, 7, ELEM_DEV, H)
        for receivers, senders, factor in slab_pairs(x):
            g = sget(cot, (0, receivers[1]))
            g = g if factor is None else g * factor
            dz1 = backward_edge(sget(t_ref, receivers) + sget(s_ref, senders), g, w2, w2t, bias, g2_ref, total_ref)
            sadd(dt_ref, receivers, dz1)
            sadd(ds_ref, senders, dz1)
        return carry

    lax.fori_loop(first, last, plane, 0)


def back_outer_kernel(place, dz_ref, t_ref, s_ref, hs_ref, wmid_ref, nin_ref, eb_ref, ngrad_ref, dt_a, ds_a, g2_a, total_a, dt_b, ds_b, g2_b, total_b,
                      rx1, rx2, ry1, ry2, rz1, rz2, grad_ref, dt_hbm, ds_hbm, acc, dt_ref, ds_ref, sems, w2, w2t, wct, g_2, g_t, g_s, sums):
    back_weights(wmid_ref, nin_ref, w2, w2t, wct)
    g_2[...] = g2_a[...] + g2_b[...]
    g_t[...] = jnp.zeros_like(g_t)
    g_s[...] = jnp.zeros_like(g_s)
    sums[0] = jnp.zeros((8, H), F32)
    sums[1] = total_a[...] + total_b[...]
    bias = 0.5 * eb_ref[1:2, :]
    for box in OUTER:
        acc[at_box(box)] = dz_ref[at_box(box)]
    add_planes(acc, ((rx1, rx2), (ry1, ry2), (rz1, rz2)))

    def senders_so_far(x, carry):
        ds_ref[x] = ds_a[x] + ds_b[x]
        return carry

    lax.fori_loop(0, SIDE, senders_so_far, 0)
    for source, first, last in ((dt_a, 1, HALF), (dt_b, HALF, SIDE)):
        dt_ref[first:last, 1:, 1:] = source[first:last, 1:, 1:]
    for box in OUTER:
        put(acc, box, mm(split(get(acc, box)), wct[...]))
        put(dt_ref, box, jnp.zeros((math.prod(shape_of(box)) // H, H), F32))
        for receivers, senders in pairs_of(box):
            dz1 = backward_edge(get(t_ref, receivers) + get(s_ref, senders), get(acc, receivers), w2, w2t, bias, g_2, sums.at[1])
            add(dt_ref, receivers, dz1)
            add(ds_ref, senders, dz1)

    def copies(x):
        return [pltpu.make_async_copy(a.at[x], b.at[x], sems.at[i, x]) for i, (a, b) in enumerate(((dt_ref, dt_hbm), (ds_ref, ds_hbm)))]

    for x in range(SIDE):
        for copy in copies(x):
            copy.start()

    def plane(x, carry):
        dt = dt_ref[x].reshape(-1, H)
        dts = split(dt)
        dss = split(ds_ref[x].reshape(-1, H))
        hs = split(hs_ref[x].reshape(-1, H))
        sums[0] += row_sum(dt)
        g_t[...] += mm_t(hs, dts)
        g_s[...] += mm_t(hs, dss)
        return carry

    lax.fori_loop(0, SIDE, plane, 0)
    grad_ref[0:4 * H, :] = ngrad_ref[0:4 * H, :]
    grad_ref[4 * H:5 * H, :] = quad(g_t[...])
    grad_ref[5 * H:6 * H, :] = quad(g_s[...])
    grad_ref[6 * H:7 * H, :] = quad(g_2[...])
    grad_ref[7 * H:, :] = jnp.zeros((PAYLOAD - 7 * H, H), F32)
    for i in range(4):
        grad_ref[7 * H + i:7 * H + i + 1, :] = jnp.sum(ngrad_ref[4 * H + i * 8:4 * H + i * 8 + 8, :], axis=0, keepdims=True)
    for i in range(2):
        grad_ref[7 * H + 4 + i:7 * H + 5 + i, :] = jnp.sum(sums[i], axis=0, keepdims=True)
    for x in range(SIDE):
        for copy in copies(x):
            copy.wait()


def finish_kernel(scale, total_ref, wmid_ref, nin_ref, eb_ref, ein_ref, emid_ref, ebias_ref, nino_ref, nmid_ref, nbias_ref):
    def rows(i):
        return total_ref[i * H:(i + 1) * H, :]

    m = rows(0)
    lower = nin_ref[H:, :]
    v = total_ref[7 * H + 3:7 * H + 4, :]
    ein_ref[0:H, :] = rows(4) * scale
    ein_ref[H:, :] = rows(5) * scale
    emid_ref[0] = rows(6) * scale
    emid_ref[1] = exact_dot(m, lower.T) * scale
    ebias_ref[0:2, :] = total_ref[7 * H + 4:7 * H + 6, :] * scale
    ebias_ref[2:3, :] = exact_dot(jnp.broadcast_to(v, (8, H)), lower.T)[0:1] * scale
    nino_ref[0:H, :] = rows(1) * scale
    outer = eb_ref[2:3, :].T * v
    nino_ref[H:, :] = (exact_dot(wmid_ref[1].T, m) + outer) * scale
    nmid_ref[0] = rows(2) * scale
    nmid_ref[1] = rows(3) * scale
    nbias_ref[...] = total_ref[7 * H:7 * H + 3, :] * scale


def fix_y_kernel(y1, y2, rz1, rz2, o1, o2):
    o1[...] = y1[...]
    o2[...] = y2[...]
    line = pl.ds(0, 8, stride=SIDE)
    for py, out in zip(sides(1), (o1, o2)):
        for pz, rz in zip(sides(2), (rz1, rz2)):
            for px in range(2):
                out[px * 2 + pz, line, :] += rz[px * 2 + py, line, :]


def fix_x_kernel(x1, x2, rz1, rz2, ry1, ry2, o1, o2):
    o1[...] = x1[...]
    o2[...] = x2[...]
    first = pl.ds(0, 8)
    for px, out in zip(sides(0), (o1, o2)):
        for py, ry in zip(sides(1), (ry1, ry2)):
            for pz, rz in zip(sides(2), (rz1, rz2)):
                out[py * 2 + pz, pl.ds(0, 8, stride=SIDE), :] += rz[px * 2 + py, first, :]
                out[py * 2 + pz, first, :] += ry[px * 2 + pz, first, :]


PLANE = jax.ShapeDtypeStruct((4, 64, H), F32)
VM = pl.BlockSpec(memory_space=pltpu.VMEM)
SM = pl.BlockSpec(memory_space=pltpu.SMEM)
HB = pl.BlockSpec(memory_space=pltpu.MemorySpace.HBM)


def in_hbm(*values):
    return [pltpu.with_memory_space_constraint(v, pltpu.MemorySpace.HBM) for v in values]


def swapped(block, axis, second):
    n = lax.axis_size("dom")
    limit, stride = (DGX, DGY, n // (DGX * DGY))[axis], STRIDES[axis]
    route = []
    for i in range(n):
        at = i // stride % limit
        if at % 2 == second and at + 1 < limit:
            route += [(i, i + stride), (i + stride, i)]
    return lax.ppermute(block, "dom", route)


def sds(*shape, dtype=F32):
    return jax.ShapeDtypeStruct(shape, dtype)


HALF = 5
LATTICE = jax.ShapeDtypeStruct(FULL, F32)
LIMIT = 14
SMALL = pltpu.CompilerParams(vmem_limit_bytes=6 * 1024 * 1024)


def run(kernel, name, outs, scratch, args, micros, spec=VM, hbm_in=(), hbm_out=()):
    outs = [pltpu.MemorySpace.HBM(o.shape, o.dtype) if i in hbm_out else o for i, o in enumerate(outs)]
    call = pl.pallas_call(
        kernel, out_shape=outs, in_specs=[SM] + [HB if i in hbm_in else spec for i in range(1, len(args))], out_specs=[HB if i in hbm_out else VM for i in range(len(outs))], scratch_shapes=scratch,
        name=name,
        cost_estimate=pl.CostEstimate(flops=micros * 1000000000, bytes_accessed=8000000, transcendentals=0),
        compiler_params=pltpu.CompilerParams(vmem_limit_bytes=LIMIT * 1024 * 1024),
    )
    return list(call(*args))


def exchange(planes, beside_z, beside_y):
    x1, x2, y1, y2, z1, z2 = planes
    rz1, rz2 = swapped(z1, 2, 0), swapped(z2, 2, 1)
    rz1, rz2 = beside_z(rz1, rz2)
    y1, y2 = pl.pallas_call(fix_y_kernel, out_shape=(PLANE, PLANE), in_specs=[VM] * 4, out_specs=(VM, VM), name="fix_y", compiler_params=SMALL)(y1, y2, rz1, rz2)
    ry1, ry2 = swapped(y1, 1, 0), swapped(y2, 1, 1)
    ry1, ry2 = beside_y(ry1, ry2)
    x1, x2 = pl.pallas_call(fix_x_kernel, out_shape=(PLANE, PLANE), in_specs=[VM] * 6, out_specs=(VM, VM), name="fix_x", compiler_params=SMALL)(x1, x2, rz1, rz2, ry1, ry2)
    rx1, rx2 = swapped(x1, 0, 0), swapped(x2, 0, 1)
    return [rx1, rx2, ry1, ry2, rz1, rz2]


def total_over_devices(block, beside_first, beside_second):
    n = lax.axis_size("dom")
    parts = lax.all_to_all(block.reshape(n, -1, H), "dom", 0, 0, tiled=True)
    parts, first = lax.optimization_barrier((parts, beside_first()))
    mine = parts.sum(0)
    spread = jnp.broadcast_to(mine[None], (n,) + mine.shape)
    total = lax.all_to_all(spread, "dom", 0, 0, tiled=True)
    total, second = lax.optimization_barrier((total, beside_second()))
    return total.reshape(-1, H), first, second


def body(node_feat, out_grad, lattice_of, element_place, edge_in, edge_mid, edge_bias, node_in, node_mid, node_bias):
    n = lax.axis_size("dom")
    square, wide, acc = pltpu.VMEM((256, 256), BF16), pltpu.VMEM((256, 512), BF16), pltpu.VMEM(FULL, F32)
    total = pltpu.VMEM((256, 256), F32)

    outs = run(edge_outer_kernel, "edge_outer", [LATTICE] * 4 + [PLANE] * 6,
               [wide, square, pltpu.VMEM((ELEM_DEV, NODES_EL, H), F32), pltpu.VMEM((ELEM_DEV, NODES_EL), jnp.int32), pltpu.VMEM((256, H), F32),
                pltpu.VMEM((2, H, H), F32), pltpu.VMEM((3, H), F32), pltpu.SemaphoreType.DMA((4,)), pltpu.SemaphoreType.DMA((ELEM_DEV,))],
               (element_place, *in_hbm(node_feat, lattice_of, edge_in, edge_mid, edge_bias)), 8, HB)
    hs, tv, sv, outer_sum = outs[:4]
    node_args = (node_in, node_mid, node_bias, edge_mid, edge_bias)
    weights = [square] * 5 + [pltpu.VMEM((8, H), F32)]

    done = {}

    def beside_z(*got):
        inner_sum, gl = run(edge_inner_kernel, "edge_inner", [LATTICE] * 2, [square], (element_place, tv, sv, out_grad, lattice_of, edge_mid, edge_bias), 12)
        *got, done["sum"], done["gl"] = lax.optimization_barrier((*got, inner_sum, gl))
        return got

    def beside_y(*got):
        done["node"] = run(node_inner_kernel, "node_inner", [LATTICE] * 3 + [sds(4, 256, 256), sds(4, 8, H)], [acc, acc, pltpu.SemaphoreType.DMA((2, SIDE))] + weights,
                           (element_place, done["sum"], hs, done["gl"]) + node_args, 12, hbm_out=(0, 1))
        *got, done["node"][4] = lax.optimization_barrier((*got, done["node"][4]))
        return got

    received = exchange(outs[4:], beside_z, beside_y)
    gl = done["gl"]
    hid_inner, raw_inner, dz_inner, g4, g_sums = done["node"]
    outs = run(node_outer_kernel, "node_outer", [LATTICE] * 3 + [sds(4 * H + 32, H)] + [PLANE] * 6,
               [acc, pltpu.VMEM((4, 256, 256), F32), pltpu.VMEM((4, 8, H), F32), acc, acc, pltpu.SemaphoreType.DMA((2, 3))] + weights,
               (element_place, outer_sum, hs, gl) + node_args + (g4, g_sums, *received), 8, hbm_out=(0, 1))
    hid_outer, raw_outer, dz_outer, ngrad = outs[:4]
    hid_inner, raw_inner, hid_outer, raw_outer = in_hbm(hid_inner, raw_inner, hid_outer, raw_outer)

    def back_inner(first, last, dz):
        return run(functools.partial(back_inner_kernel, first, last), "back_inner", [LATTICE] * 2 + [sds(256, 256), sds(8, H)],
                   [square] * 3 + [pltpu.VMEM((1,) + FULL[1:], F32)], (element_place, dz, tv, sv, edge_mid, node_in, edge_bias), 10)

    done = {}

    def under_z(*got):
        done["a"] = back_inner(1, HALF, dz_inner)
        *got, done["a"][2] = lax.optimization_barrier((*got, done["a"][2]))
        return got

    def under_y(*got):
        done["b"] = back_inner(HALF, SIDE, dz_inner)
        *got, done["b"][2] = lax.optimization_barrier((*got, done["b"][2]))
        return got

    received = exchange(outs[4:], under_z, under_y)
    part_a, part_b = done["a"], done["b"]
    payload, dt, ds = run(back_outer_kernel, "back_outer", [sds(PAYLOAD, H), LATTICE, LATTICE],
                          [acc] * 3 + [pltpu.SemaphoreType.DMA((2, SIDE))] + [square] * 3 + [total] * 3 + [pltpu.VMEM((2, 8, H), F32)],
                          (element_place, dz_outer, tv, sv, hs, edge_mid, node_in, edge_bias, ngrad, *part_a, *part_b, *received), 10, hbm_out=(1, 2))
    dt, ds = in_hbm(dt, ds)

    def beside_first():
        return run(feat_grad_kernel, "feat_grad", [sds(ROWS, H)], [acc] * 4 + [pltpu.SemaphoreType.DMA((4,)), pltpu.SemaphoreType.DMA((2, SIDE))] + [square] * 3,
                   (element_place, dt, ds, raw_inner, raw_outer, out_grad, lattice_of, edge_in, node_in), 8, hbm_in=(1, 2, 3, 4))[0]

    def beside_second():
        return run(new_feat_kernel, "new_feat", [sds(ROWS, H)], [acc, acc, pltpu.SemaphoreType.DMA((4,)), square],
                   (element_place, hid_inner, hid_outer, node_feat, lattice_of, node_mid, node_bias), 8, hbm_in=(1, 2))[0]

    total, feat_grad, new_feat = total_over_devices(payload, beside_first, beside_second)
    scale = 1.0 / math.sqrt(n * ELEM_DEV * NODES_EL)
    weights = pl.pallas_call(
        functools.partial(finish_kernel, scale),
        out_shape=(sds(256, H), sds(2, H, H), sds(3, H), sds(256, H), sds(2, H, H), sds(3, H)),
        in_specs=[VM] * 4, out_specs=(VM,) * 6, name="finish", compiler_params=SMALL,
    )(total, edge_mid, node_in, edge_bias)
    return (new_feat, feat_grad) + tuple(weights)


def solution(mesh):
    in_specs = (P("dom", None),) * 4 + (P(),) * 6
    out_specs = (P("dom", None), P("dom", None)) + (P(),) * 6
    return jax.shard_map(body, mesh=mesh, in_specs=in_specs, out_specs=out_specs, check_vma=False)
```

```python
import functools
import math

import jax
import jax.numpy as jnp
from jax import lax
from jax.experimental import pallas as pl
from jax.experimental.pallas import tpu as pltpu
from jax.sharding import PartitionSpec as P

SIDE = 8
ELEM_DEV = 8
DGX = 4
DGY = 4
NODES_EL = 512
H = 128
ROWS = ELEM_DEV * NODES_EL
PAYLOAD = 1024
F32 = jnp.float32
BF16 = jnp.bfloat16


def split(x):
    high = x.astype(BF16)
    low = (x - high.astype(F32)).astype(BF16)
    return jnp.concatenate([high, low], axis=-1)


def weight_split(w):
    row = split(w)
    return jnp.concatenate([row, row], axis=0)


def dot(a, b):
    return jnp.dot(a, b, preferred_element_type=F32)


def fold(o):
    return o[:, :H] + o[:, H:]


def mm(xs, w):
    return fold(dot(xs, w))


def mm_t(xs, ys):
    return lax.dot_general(xs, ys, (((0,), (0,)), ((), ())), preferred_element_type=F32)


def quad(o):
    return o[:H, :H] + o[:H, H:] + o[H:, :H] + o[H:, H:]


def row_sum(x):
    return jnp.sum(x.reshape(-1, 8, H), axis=0)


def exact_dot(a, b):
    return jnp.dot(a, b, precision=lax.Precision.HIGHEST, preferred_element_type=F32)


def flip(e):
    return (e // 4) * 448 + (e // 2 % 2) * 56 + (e % 2) * 7


def to_lattice_onehot(lat_ref, slot, e):
    row = lat_ref[pl.ds(slot, 1), :] ^ flip(e)
    level = lax.broadcasted_iota(jnp.int32, (NODES_EL, NODES_EL), 0)
    return jnp.where(level == row, 1.0, 0.0).astype(BF16)


def from_lattice_onehot(turned, slot, e):
    lane = lax.broadcasted_iota(jnp.int32, (NODES_EL, ELEM_DEV), 1)
    column = jnp.sum(jnp.where(lane == slot, turned, 0.0), axis=1, keepdims=True).astype(jnp.int32) ^ flip(e)
    level = lax.broadcasted_iota(jnp.int32, (NODES_EL, NODES_EL), 1)
    return jnp.where(level == column, 1.0, 0.0).astype(BF16)


def slot_of(place, e):
    slot = jnp.int32(0)
    for i in range(1, ELEM_DEV):
        slot = jnp.where(place[0, i] == e, jnp.int32(i), slot)
    return slot


def slot_rows(slot):
    return pl.ds(pl.multiple_of(slot * NODES_EL, NODES_EL), NODES_EL)


def element_rows(e):
    return pl.ds(e, NODES_EL, stride=ELEM_DEV)


def to_lattice(place, lat_ref, src_ref, dst_ref):
    def one(i, carry):
        for e in (2 * i, 2 * i + 1):
            slot = slot_of(place, e)
            both = dot(to_lattice_onehot(lat_ref, slot, e), split(src_ref[slot_rows(slot), :]))
            dst_ref[element_rows(e), :] = fold(both)
        return carry

    lax.fori_loop(0, ELEM_DEV // 2, one, 0)


def from_lattice(place, lat_ref, src_ref, add_ref, dst_ref, bias):
    turned = lat_ref[...].astype(F32).T

    def one(i, carry):
        for e in (2 * i, 2 * i + 1):
            slot = slot_of(place, e)
            back = from_lattice_onehot(turned, slot, e)
            rows = fold(dot(back, split(src_ref[element_rows(e), :])))
            rows = rows + add_ref[slot_rows(slot), :]
            dst_ref[slot_rows(slot), :] = rows if bias is None else rows + bias
        return carry

    lax.fori_loop(0, ELEM_DEV // 2, one, 0)


FULL = (SIDE, SIDE, SIDE, ELEM_DEV, H)
def two(i):
    return pl.ds(2 * i, 2)


def rows_at(ref, at):
    return ref[at].reshape(-1, H)


OUTER = [((0, 1), (0, 8), (0, 8)), ((1, 8), (0, 1), (0, 8)), ((1, 8), (1, 8), (0, 1))]
INNER = [((1, 8), (1, 8), (1, 8))]


def at_box(box):
    return tuple(pl.ds(a, b - a) for a, b in box)


def get(ref, box):
    return ref[at_box(box)].reshape(-1, H)


def shape_of(box):
    return tuple(b - a for a, b in box) + (ELEM_DEV, H)


def put(ref, box, rows):
    ref[at_box(box)] = rows.reshape(shape_of(box))


def add(ref, box, rows):
    ref[at_box(box)] += rows.reshape(shape_of(box))


def pairs_of(box):
    out = []
    for axis in range(3):
        for step in (1, -1):
            a, b = box[axis]
            a, b = (a, min(b, SIDE - 1)) if step == 1 else (max(a, 1), b)
            if a < b:
                out.append((box[:axis] + ((a, b),) + box[axis + 1:], box[:axis] + ((a + step, b + step),) + box[axis + 1:]))
    return out


SLAB = ((1, 8), (1, 8))


def slab_pairs(x):
    out = [((x, SLAB), (x - 1, SLAB), None)]
    for axis in range(2):
        for step in (1, -1):
            a, b = (1, SIDE - 1) if step == 1 else (1, SIDE)
            receivers = SLAB[:axis] + ((a, b),) + SLAB[axis + 1:]
            senders = SLAB[:axis] + ((a + step, b + step),) + SLAB[axis + 1:]
            out.append(((x, receivers), (x, senders), None))
    upper = jnp.where(x < SIDE - 1, 1.0, 0.0)
    out.append(((x, SLAB), (jnp.minimum(x + 1, SIDE - 1), SLAB), upper))
    return out


def at_slab(where):
    x, box = where
    return (x,) + tuple(pl.ds(a, b - a) for a, b in box)


def sget(ref, where):
    return ref[at_slab(where)].reshape(-1, H)


def sshape(where):
    return tuple(b - a for a, b in where[1]) + (ELEM_DEV, H)


def sput(ref, where, rows):
    ref[at_slab(where)] = rows.reshape(sshape(where))


def sadd(ref, where, rows):
    ref[at_slab(where)] += rows.reshape(sshape(where))


def swap(v, axis):
    if axis == 0:
        return pltpu.roll(v, 4, 1)
    by = 2 if axis == 1 else 1
    e = lax.broadcasted_iota(jnp.int32, v.shape, 1)
    return jnp.where((e & by) == 0, pltpu.roll(v, ELEM_DEV - by, 1), pltpu.roll(v, by, 1))


def assemble(ref, boxes):
    for axis in (2, 1, 0):
        for box in boxes:
            if box[axis][1] == SIDE:
                face = box[:axis] + ((SIDE - 1, SIDE),) + box[axis + 1:]
                v = ref[at_box(face)].reshape(-1, ELEM_DEV, H)
                put(ref, face, v + swap(v, axis))


STRIDES = (1, DGX, DGX * DGY)
BIT = (4, 2, 1)


def above():
    index = lax.axis_index("dom")
    return [1 - index // stride % 2 for stride in STRIDES]


def sides(axis):
    up = above()[axis]
    return up, 1 - up


def outer_rows(axis, e):
    if axis == 0:
        return [(pl.ds(e, 64, stride=8), pl.ds(0, 64))]
    if axis == 2:
        return [(pl.ds(e, 64, stride=64), pl.ds(0, 64))]
    return [(pl.ds(x * 512 + e, 8, stride=8), pl.ds(x * 8, 8)) for x in range(SIDE)]


def others(axis):
    return [e for e in range(ELEM_DEV) if not e & BIT[axis]]


def emit_planes(ref, planes):
    flat = ref.reshape((ROWS, H))
    for axis in range(3):
        for side, plane in zip(sides(axis), planes[axis]):
            for j, e in enumerate(others(axis)):
                for rows, there in outer_rows(axis, e + side * BIT[axis]):
                    plane[j, there, :] = flat[rows, :]


def add_planes(ref, planes):
    flat = ref.reshape((ROWS, H))
    for axis in range(3):
        for side, plane in zip(sides(axis), planes[axis]):
            for j, e in enumerate(others(axis)):
                for rows, there in outer_rows(axis, e + side * BIT[axis]):
                    flat[rows, :] += plane[j, there, :]


def half_silu(u):
    t = jnp.tanh(u)
    q = 1.0 + t
    return t, q, u * q


def twice_slope(t, q, s):
    return q + s * (1.0 - t)


def forward_edge(u1, w2, bias):
    _, _, s1 = half_silu(u1)
    _, _, s2 = half_silu(mm(split(s1), w2[...]) + bias)
    return s2


def edge_outer_kernel(place, h_hbm, lat_hbm, win_hbm, wmid_hbm, eb_hbm, hs_ref, t_ref, s_ref, sum_ref, x1, x2, y1, y2, z1, z2, w2,
                      wts, h_ref, lat_ref, win_ref, wmid_ref, eb_ref, sems, h_sems):
    small = [pltpu.make_async_copy(a, b, sems.at[i]) for i, (a, b) in enumerate(
        ((lat_hbm, lat_ref), (win_hbm, win_ref), (wmid_hbm, wmid_ref), (eb_hbm, eb_ref)))]
    for copy in small:
        copy.start()

    def rows_of(e):
        return pltpu.make_async_copy(h_hbm.at[slot_rows(slot_of(place, e)), :], h_ref.at[e], h_sems.at[e])

    for e in range(ELEM_DEV):
        rows_of(e).start()
    for copy in small:
        copy.wait()
    wts[:, 0:256] = weight_split(0.5 * win_ref[0:H, :])
    wts[:, 256:512] = weight_split(0.5 * win_ref[H:, :])
    w2[...] = weight_split(0.5 * wmid_ref[0])
    flat = hs_ref.reshape((ROWS, H))

    def one(i, carry):
        for e in (2 * i, 2 * i + 1):
            rows_of(e).wait()
        for e in (2 * i, 2 * i + 1):
            both = dot(to_lattice_onehot(lat_ref, slot_of(place, e), e), split(h_ref[e]))
            flat[element_rows(e), :] = fold(both)
        return carry

    lax.fori_loop(0, ELEM_DEV // 2, one, 0)
    half_bias = 0.5 * eb_ref[0:1, :]

    def plane(i, carry):
        both = dot(split(rows_at(hs_ref, two(i))), wts[...])
        t_ref[two(i)] = (fold(both[:, 0:256]) + half_bias).reshape((2,) + FULL[1:])
        s_ref[two(i)] = fold(both[:, 256:512]).reshape((2,) + FULL[1:])
        return carry

    lax.fori_loop(0, SIDE // 2, plane, 0)
    bias = 0.5 * eb_ref[1:2, :]
    for box in OUTER:
        put(sum_ref, box, jnp.zeros((math.prod(shape_of(box)) // H, H), F32))
        for receivers, senders in pairs_of(box):
            add(sum_ref, receivers, forward_edge(get(t_ref, receivers) + get(s_ref, senders), w2, bias))
    assemble(sum_ref, OUTER)
    emit_planes(sum_ref, ((x1, x2), (y1, y2), (z1, z2)))


def edge_inner_kernel(place, t_ref, s_ref, g_ref, lat_ref, eb_ref, w2, sum_ref, gl_ref):
    bias = 0.5 * eb_ref[1:2, :]

    def plane(x, carry):
        sput(sum_ref, (x, SLAB), jnp.zeros((49 * 8, H), F32))
        for receivers, senders, factor in slab_pairs(x):
            s2 = forward_edge(sget(t_ref, receivers) + sget(s_ref, senders), w2, bias)
            sadd(sum_ref, receivers, s2 if factor is None else s2 * factor)
        return carry

    lax.fori_loop(1, SIDE, plane, 0)
    assemble(sum_ref, INNER)
    to_lattice(place, lat_ref, g_ref, gl_ref.reshape((ROWS, H)))


def degree_of(where, shape):
    full = shape + (ELEM_DEV, H)
    e = lax.broadcasted_iota(jnp.int32, (ELEM_DEV, H), 0)
    count, own = None, None
    index, depth = lax.axis_index("dom"), lax.axis_size("dom") // (DGX * DGY)
    grid = (index % DGX, index // DGX % DGY, index // (DGX * DGY))
    for axis, limit in ((0, DGX), (1, DGY), (2, depth)):
        side = (e >> (2 - axis)) & 1
        low = jnp.where(grid[axis] > 0, 2.0, 1.0)
        high = jnp.where(grid[axis] < limit - 1, 2.0, 1.0)
        outer = jnp.broadcast_to(jnp.where(side == 0, low, high), full)
        at = lax.broadcasted_iota(jnp.int32, full, axis) + where[axis]
        times = jnp.where(at == 0, outer, jnp.where(at == SIDE - 1, 2.0, 1.0))
        messages = jnp.where((at == 0) | (at == SIDE - 1), 1.0, 2.0)
        count = times if count is None else count * times
        own = messages if own is None else own + messages
    return (count * own).reshape(-1, H)


def node_weights(nin_ref, nmid_ref, wmid_ref, eb_ref, weights):
    wa, wc, w0, w0t, w1t, row, merged_ref = weights
    lower = nin_ref[H:, :]
    wa[...] = weight_split(0.5 * nin_ref[0:H, :])
    merged = exact_dot(wmid_ref[1], lower)
    merged_ref[...] = merged
    wc[...] = weight_split(0.5 * merged)
    w0[...] = weight_split(0.5 * nmid_ref[0])
    w0t[...] = weight_split(0.5 * nmid_ref[0].T)
    w1t[...] = weight_split(0.5 * nmid_ref[1].T)
    row[...] = 0.5 * exact_dot(jnp.broadcast_to(eb_ref[2:3, :], (8, H)), lower)


def node_chunk(gathered, h, g, degree, nb_ref, weights, totals, sums):
    wa, wc, w0, w0t, w1t, row = weights[:6]
    g_a, g_m, g_0, g_1 = totals
    hs = split(h)
    gs = split(gathered)
    u = mm(hs, wa[...]) + mm(gs, wc[...]) + degree * row[0:1, :] + 0.5 * nb_ref[0:1, :]
    t, q, s = half_silu(u)
    slope = twice_slope(t, q, s)
    ss = split(s)
    t, q, s = half_silu(mm(ss, w0[...]) + 0.5 * nb_ref[1:2, :])
    slope1 = twice_slope(t, q, s)
    ss1 = split(s)
    hidden = s
    gl = split(g)
    sums[2] += row_sum(g)
    g_1[...] += mm_t(ss1, gl)
    dz1 = mm(gl, w1t[...]) * slope1
    sums[1] += row_sum(dz1)
    dz1s = split(dz1)
    g_0[...] += mm_t(ss, dz1s)
    dz = mm(dz1s, w0t[...]) * slope
    sums[0] += row_sum(dz)
    sums[3] += row_sum(dz * degree)
    dzs = split(dz)
    g_a[...] += mm_t(hs, dzs)
    g_m[...] += mm_t(gs, dzs)
    return hidden, dz


def node_inner_kernel(place, sum_ref, hs_ref, gl_ref, nin_ref, nmid_ref, nb_ref, wmid_ref, eb_ref, hid_hbm, raw_hbm, dz_ref, g_out, sums_out, *rest):
    weights, (hid_ref, raw_ref, sems) = rest[:7], rest[7:]
    node_weights(nin_ref, nmid_ref, wmid_ref, eb_ref, weights)
    totals = [g_out.at[i] for i in range(4)]
    g_out[...] = jnp.zeros_like(g_out)
    sums_out[...] = jnp.zeros_like(sums_out)

    def box_at(x, n):
        return (pl.ds(x, n), pl.ds(1, 7), pl.ds(1, 7))

    def planes(x, n):
        at, shape = box_at(x, n), (n, 7, 7, ELEM_DEV, H)
        hidden, dz = node_chunk(rows_at(sum_ref, at), rows_at(hs_ref, at), rows_at(gl_ref, at), degree_of((x, 1, 1), (n, 7, 7)), nb_ref, weights, totals, sums_out)
        hid_ref[at] = hidden.reshape(shape)
        dz_ref[at] = dz.reshape(shape)
        raw_ref[at] = dz.reshape(shape)
        for copy in copies(x, n):
            copy.start()

    def copies(x, n):
        at = box_at(x, n)
        return [pltpu.make_async_copy(a.at[at], b.at[at], sems.at[i, x]) for i, (a, b) in enumerate(((hid_ref, hid_hbm), (raw_ref, raw_hbm)))]

    def pair(i, carry):
        planes(2 * i + 1, 2)
        return carry

    lax.fori_loop(0, 3, pair, 0)
    planes(7, 1)
    assemble(dz_ref, INNER)
    for x, n in ((1, 2), (3, 2), (5, 2), (7, 1)):
        for copy in copies(x, n):
            copy.wait()


def node_outer_kernel(place, sum_ref, hs_ref, gl_ref, nb_ref, wa, wc, w0, w0t, w1t, row, g_in, sums_in,
                      rx1, rx2, ry1, ry2, rz1, rz2, hid_hbm, raw_hbm, dz_ref, grad_ref, x1, x2, y1, y2, z1, z2, acc, totals_ref, sums, hid_ref, raw_ref, sems):
    weights = (wa, wc, w0, w0t, w1t, row)
    totals_ref[...] = g_in[...]
    sums[...] = sums_in[...]
    totals = [totals_ref.at[i] for i in range(4)]
    for box in OUTER:
        acc[at_box(box)] = sum_ref[at_box(box)]
    add_planes(acc, ((rx1, rx2), (ry1, ry2), (rz1, rz2)))
    for box in OUTER:
        degree = degree_of(tuple(a for a, _ in box), tuple(b - a for a, b in box))
        hidden, dz = node_chunk(get(acc, box), get(hs_ref, box), get(gl_ref, box), degree, nb_ref, weights, totals, sums)
        put(hid_ref, box, hidden)
        put(dz_ref, box, dz)
        put(raw_ref, box, dz)
    copies = [pltpu.make_async_copy(a.at[at_box(box)], b.at[at_box(box)], sems.at[i, j])
              for i, (a, b) in enumerate(((hid_ref, hid_hbm), (raw_ref, raw_hbm))) for j, box in enumerate(OUTER)]
    for copy in copies:
        copy.start()
    assemble(dz_ref, OUTER)
    emit_planes(dz_ref, ((x1, x2), (y1, y2), (z1, z2)))
    grad_ref[0:H, :] = quad(totals_ref[1])
    grad_ref[H:2 * H, :] = quad(totals_ref[0])
    grad_ref[2 * H:3 * H, :] = quad(totals_ref[2])
    grad_ref[3 * H:4 * H, :] = quad(totals_ref[3])
    for i in range(4):
        grad_ref[4 * H + i * 8:4 * H + i * 8 + 8, :] = sums[i]
    for copy in copies:
        copy.wait()


def merge_copies(inner_hbm, outer_hbm, dst, sems):
    parts = [(inner_hbm, INNER[0])] + [(outer_hbm, box) for box in OUTER]
    return [pltpu.make_async_copy(a.at[at_box(box)], dst.at[at_box(box)], sems.at[i]) for i, (a, box) in enumerate(parts)]


def new_feat_kernel(place, hid_inner, hid_outer, h_ref, lat_ref, nmid_ref, nb_ref, new_ref, acc, hid, sems, w1):
    copies = merge_copies(hid_inner, hid_outer, hid, sems)
    for copy in copies:
        copy.start()
    w1[...] = weight_split(nmid_ref[1])
    for copy in copies:
        copy.wait()

    def plane(i, carry):
        acc[two(i)] = mm(split(rows_at(hid, two(i))), w1[...]).reshape((2,) + FULL[1:])
        return carry

    lax.fori_loop(0, SIDE // 2, plane, 0)
    from_lattice(place, lat_ref, acc.reshape((ROWS, H)), h_ref, new_ref, nb_ref[2:3, :])


def feat_grad_kernel(place, dt_hbm, ds_hbm, raw_inner, raw_outer, g_ref, lat_ref, win_ref, nin_ref, feat_ref, acc, dt_ref, ds_ref, raw, sems, slab_sems, wtt, wst, wat):
    copies = merge_copies(raw_inner, raw_outer, raw, sems)
    for copy in copies:
        copy.start()

    def slabs(x):
        return [pltpu.make_async_copy(a.at[x], b.at[x], slab_sems.at[i, x]) for i, (a, b) in enumerate(((dt_hbm, dt_ref), (ds_hbm, ds_ref)))]

    for x in range(SIDE):
        for copy in slabs(x):
            copy.start()
    wtt[...] = weight_split(win_ref[0:H, :].T)
    wst[...] = weight_split(win_ref[H:, :].T)
    wat[...] = weight_split(nin_ref[0:H, :].T)
    for copy in copies:
        copy.wait()

    def plane(i, carry):
        for copy in slabs(2 * i) + slabs(2 * i + 1):
            copy.wait()
        dh = mm(split(rows_at(dt_ref, two(i))), wtt[...]) + mm(split(rows_at(ds_ref, two(i))), wst[...]) + mm(split(rows_at(raw, two(i))), wat[...])
        acc[two(i)] = dh.reshape((2,) + FULL[1:])
        return carry

    lax.fori_loop(0, SIDE // 2, plane, 0)
    from_lattice(place, lat_ref, acc.reshape((ROWS, H)), g_ref, feat_ref, None)


def back_first_kernel(first, last, place, dz_ref, t_ref, s_ref, wmid_ref, merged_ref, eb_ref, w2, dt_ref, ds_ref, g2_ref, total_ref, w2t, wct, cot):
    w2t[...] = weight_split(0.5 * wmid_ref[0].T)
    wct[...] = weight_split(0.5 * merged_ref[...].T)
    back_inner_kernel(first, last, place, dz_ref, t_ref, s_ref, eb_ref, w2, w2t, wct, dt_ref, ds_ref, g2_ref, total_ref, cot)


def backward_edge(u1, cot, w2, w2t, bias, g_2, total):
    t1, q1, s1 = half_silu(u1)
    s1s = split(s1)
    t2, q2, s2 = half_silu(mm(s1s, w2[...]) + bias)
    dz2 = cot * twice_slope(t2, q2, s2)
    total[...] += row_sum(dz2)
    dz2s = split(dz2)
    g_2[...] += mm_t(s1s, dz2s)
    return mm(dz2s, w2t[...]) * twice_slope(t1, q1, s1)


def back_inner_kernel(first, last, place, dz_ref, t_ref, s_ref, eb_ref, w2, w2t, wct, dt_ref, ds_ref, g2_ref, total_ref, cot):
    bias = 0.5 * eb_ref[1:2, :]
    g2_ref[...] = jnp.zeros_like(g2_ref)
    total_ref[...] = jnp.zeros_like(total_ref)

    def clear(x, carry):
        ds_ref[x] = jnp.zeros(FULL[1:], F32)
        return carry

    lax.fori_loop(0, SIDE, clear, 0)

    def plane(x, carry):
        sput(dt_ref, (x, SLAB), jnp.zeros((49 * 8, H), F32))
        cot[0, pl.ds(1, 7), pl.ds(1, 7)] = mm(split(sget(dz_ref, (x, SLAB))), wct[...]).reshape(7, 7, ELEM_DEV, H)
        for receivers, senders, factor in slab_pairs(x):
            g = sget(cot, (0, receivers[1]))
            g = g if factor is None else g * factor
            dz1 = backward_edge(sget(t_ref, receivers) + sget(s_ref, senders), g, w2, w2t, bias, g2_ref, total_ref)
            sadd(dt_ref, receivers, dz1)
            sadd(ds_ref, senders, dz1)
        return carry

    lax.fori_loop(first, last, plane, 0)


def back_outer_kernel(place, dz_ref, t_ref, s_ref, hs_ref, eb_ref, w2, w2t, wct, ngrad_ref, dt_a, ds_a, g2_a, total_a, dt_b, ds_b, g2_b, total_b,
                      rx1, rx2, ry1, ry2, rz1, rz2, grad_ref, dt_hbm, ds_hbm, acc, dt_ref, ds_ref, sems, g_2, g_t, g_s, sums):
    g_2[...] = g2_a[...] + g2_b[...]
    g_t[...] = jnp.zeros_like(g_t)
    g_s[...] = jnp.zeros_like(g_s)
    sums[0] = jnp.zeros((8, H), F32)
    sums[1] = total_a[...] + total_b[...]
    bias = 0.5 * eb_ref[1:2, :]
    for box in OUTER:
        acc[at_box(box)] = dz_ref[at_box(box)]
    add_planes(acc, ((rx1, rx2), (ry1, ry2), (rz1, rz2)))

    def senders_so_far(x, carry):
        ds_ref[x] = ds_a[x] + ds_b[x]
        return carry

    lax.fori_loop(0, SIDE, senders_so_far, 0)
    for source, first, last in ((dt_a, 1, HALF), (dt_b, HALF, SIDE)):
        dt_ref[first:last, 1:, 1:] = source[first:last, 1:, 1:]
    for box in OUTER:
        put(acc, box, mm(split(get(acc, box)), wct[...]))
        put(dt_ref, box, jnp.zeros((math.prod(shape_of(box)) // H, H), F32))
        for receivers, senders in pairs_of(box):
            dz1 = backward_edge(get(t_ref, receivers) + get(s_ref, senders), get(acc, receivers), w2, w2t, bias, g_2, sums.at[1])
            add(dt_ref, receivers, dz1)
            add(ds_ref, senders, dz1)

    def copies(x):
        return [pltpu.make_async_copy(a.at[x], b.at[x], sems.at[i, x]) for i, (a, b) in enumerate(((dt_ref, dt_hbm), (ds_ref, ds_hbm)))]

    for x in range(SIDE):
        for copy in copies(x):
            copy.start()

    def plane(i, carry):
        dt = rows_at(dt_ref, two(i))
        dts = split(dt)
        dss = split(rows_at(ds_ref, two(i)))
        hs = split(rows_at(hs_ref, two(i)))
        sums[0] += row_sum(dt)
        g_t[...] += mm_t(hs, dts)
        g_s[...] += mm_t(hs, dss)
        return carry

    lax.fori_loop(0, SIDE // 2, plane, 0)
    grad_ref[0:4 * H, :] = ngrad_ref[0:4 * H, :]
    grad_ref[4 * H:5 * H, :] = quad(g_t[...])
    grad_ref[5 * H:6 * H, :] = quad(g_s[...])
    grad_ref[6 * H:7 * H, :] = quad(g_2[...])
    grad_ref[7 * H:, :] = jnp.zeros((PAYLOAD - 7 * H, H), F32)
    for i in range(4):
        grad_ref[7 * H + i:7 * H + i + 1, :] = jnp.sum(ngrad_ref[4 * H + i * 8:4 * H + i * 8 + 8, :], axis=0, keepdims=True)
    for i in range(2):
        grad_ref[7 * H + 4 + i:7 * H + 5 + i, :] = jnp.sum(sums[i], axis=0, keepdims=True)
    for x in range(SIDE):
        for copy in copies(x):
            copy.wait()


def finish_kernel(scale, total_ref, wmid_ref, nin_ref, eb_ref, ein_ref, emid_ref, ebias_ref, nino_ref, nmid_ref, nbias_ref):
    def rows(i):
        return total_ref[i * H:(i + 1) * H, :]

    m = rows(0)
    lower = nin_ref[H:, :]
    v = total_ref[7 * H + 3:7 * H + 4, :]
    ein_ref[0:H, :] = rows(4) * scale
    ein_ref[H:, :] = rows(5) * scale
    emid_ref[0] = rows(6) * scale
    emid_ref[1] = exact_dot(m, lower.T) * scale
    ebias_ref[0:2, :] = total_ref[7 * H + 4:7 * H + 6, :] * scale
    ebias_ref[2:3, :] = exact_dot(jnp.broadcast_to(v, (8, H)), lower.T)[0:1] * scale
    nino_ref[0:H, :] = rows(1) * scale
    outer = eb_ref[2:3, :].T * v
    nino_ref[H:, :] = (exact_dot(wmid_ref[1].T, m) + outer) * scale
    nmid_ref[0] = rows(2) * scale
    nmid_ref[1] = rows(3) * scale
    nbias_ref[...] = total_ref[7 * H:7 * H + 3, :] * scale


def fix_y_kernel(y1, y2, rz1, rz2, o1, o2):
    o1[...] = y1[...]
    o2[...] = y2[...]
    line = pl.ds(0, 8, stride=SIDE)
    for py, out in zip(sides(1), (o1, o2)):
        for pz, rz in zip(sides(2), (rz1, rz2)):
            for px in range(2):
                out[px * 2 + pz, line, :] += rz[px * 2 + py, line, :]


def fix_x_kernel(x1, x2, rz1, rz2, ry1, ry2, o1, o2):
    o1[...] = x1[...]
    o2[...] = x2[...]
    first = pl.ds(0, 8)
    for px, out in zip(sides(0), (o1, o2)):
        for py, ry in zip(sides(1), (ry1, ry2)):
            for pz, rz in zip(sides(2), (rz1, rz2)):
                out[py * 2 + pz, pl.ds(0, 8, stride=SIDE), :] += rz[px * 2 + py, first, :]
                out[py * 2 + pz, first, :] += ry[px * 2 + pz, first, :]


PLANE = jax.ShapeDtypeStruct((4, 64, H), F32)
VM = pl.BlockSpec(memory_space=pltpu.VMEM)
SM = pl.BlockSpec(memory_space=pltpu.SMEM)
HB = pl.BlockSpec(memory_space=pltpu.MemorySpace.HBM)


def in_hbm(*values):
    return [pltpu.with_memory_space_constraint(v, pltpu.MemorySpace.HBM) for v in values]


def swapped(block, axis, second):
    n = lax.axis_size("dom")
    limit, stride = (DGX, DGY, n // (DGX * DGY))[axis], STRIDES[axis]
    route = []
    for i in range(n):
        at = i // stride % limit
        if at % 2 == second and at + 1 < limit:
            route += [(i, i + stride), (i + stride, i)]
    return lax.ppermute(block, "dom", route)


def sds(*shape, dtype=F32):
    return jax.ShapeDtypeStruct(shape, dtype)


HALF = 5
LATTICE = jax.ShapeDtypeStruct(FULL, F32)
LIMIT = 14
SMALL = pltpu.CompilerParams(vmem_limit_bytes=6 * 1024 * 1024)


def run(kernel, name, outs, scratch, args, micros, spec=VM, hbm_in=(), hbm_out=()):
    outs = [pltpu.MemorySpace.HBM(o.shape, o.dtype) if i in hbm_out else o for i, o in enumerate(outs)]
    call = pl.pallas_call(
        kernel, out_shape=outs, in_specs=[SM] + [HB if i in hbm_in else spec for i in range(1, len(args))], out_specs=[HB if i in hbm_out else VM for i in range(len(outs))], scratch_shapes=scratch,
        name=name,
        cost_estimate=pl.CostEstimate(flops=micros * 1000000000, bytes_accessed=8000000, transcendentals=0),
        compiler_params=pltpu.CompilerParams(vmem_limit_bytes=LIMIT * 1024 * 1024),
    )
    return list(call(*args))


def exchange(planes, beside_z, beside_y):
    x1, x2, y1, y2, z1, z2 = planes
    rz1, rz2 = swapped(z1, 2, 0), swapped(z2, 2, 1)
    rz1, rz2 = beside_z(rz1, rz2)
    y1, y2 = pl.pallas_call(fix_y_kernel, out_shape=(PLANE, PLANE), in_specs=[VM] * 4, out_specs=(VM, VM), name="fix_y", compiler_params=SMALL)(y1, y2, rz1, rz2)
    ry1, ry2 = swapped(y1, 1, 0), swapped(y2, 1, 1)
    ry1, ry2 = beside_y(ry1, ry2)
    x1, x2 = pl.pallas_call(fix_x_kernel, out_shape=(PLANE, PLANE), in_specs=[VM] * 6, out_specs=(VM, VM), name="fix_x", compiler_params=SMALL)(x1, x2, rz1, rz2, ry1, ry2)
    rx1, rx2 = swapped(x1, 0, 0), swapped(x2, 0, 1)
    return [rx1, rx2, ry1, ry2, rz1, rz2]


def spread_kernel(parts_hbm, out_ref, parts, sem):
    copy = pltpu.make_async_copy(parts_hbm, parts, sem)
    copy.start()
    copy.wait()
    out_ref[...] = jnp.broadcast_to(jnp.sum(parts[...], axis=0, keepdims=True), out_ref.shape)


def total_over_devices(block, beside_first, beside_second):
    n = lax.axis_size("dom")
    parts = lax.all_to_all(block.reshape(n, -1, H), "dom", 0, 0, tiled=True)
    parts, first = lax.optimization_barrier((parts, beside_first()))
    spread = pl.pallas_call(
        spread_kernel, out_shape=sds(*parts.shape), in_specs=[HB], out_specs=VM, name="spread",
        scratch_shapes=[pltpu.VMEM(parts.shape, F32), pltpu.SemaphoreType.DMA], compiler_params=SMALL,
    )(*in_hbm(parts))
    total = lax.all_to_all(spread, "dom", 0, 0, tiled=True)
    total, second = lax.optimization_barrier((total, beside_second()))
    return total.reshape(-1, H), first, second


def body(node_feat, out_grad, lattice_of, element_place, edge_in, edge_mid, edge_bias, node_in, node_mid, node_bias):
    n = lax.axis_size("dom")
    square, wide, acc = pltpu.VMEM((256, 256), BF16), pltpu.VMEM((256, 512), BF16), pltpu.VMEM(FULL, F32)
    total = pltpu.VMEM((256, 256), F32)

    split_weight = sds(256, 256, dtype=BF16)
    outs = run(edge_outer_kernel, "edge_outer", [LATTICE] * 4 + [PLANE] * 6 + [split_weight],
               [wide, pltpu.VMEM((ELEM_DEV, NODES_EL, H), F32), pltpu.VMEM((ELEM_DEV, NODES_EL), jnp.int32), pltpu.VMEM((256, H), F32),
                pltpu.VMEM((2, H, H), F32), pltpu.VMEM((3, H), F32), pltpu.SemaphoreType.DMA((4,)), pltpu.SemaphoreType.DMA((ELEM_DEV,))],
               (element_place, *in_hbm(node_feat, lattice_of, edge_in, edge_mid, edge_bias)), 8, HB)
    hs, tv, sv, outer_sum = outs[:4]
    w2 = outs[10]
    node_args = (node_in, node_mid, node_bias, edge_mid, edge_bias)
    weights = [split_weight] * 5 + [sds(8, H), sds(H, H)]

    done = {}

    def beside_z(*got):
        inner_sum, gl = run(edge_inner_kernel, "edge_inner", [LATTICE] * 2, [], (element_place, tv, sv, out_grad, lattice_of, edge_bias, w2), 12)
        *got, done["sum"], done["gl"] = lax.optimization_barrier((*got, inner_sum, gl))
        return got

    def beside_y(*got):
        done["node"] = run(node_inner_kernel, "node_inner", [LATTICE] * 3 + [sds(4, 256, 256), sds(4, 8, H)] + weights, [acc, acc, pltpu.SemaphoreType.DMA((2, SIDE))],
                           (element_place, done["sum"], hs, done["gl"]) + node_args, 12, hbm_out=(0, 1))
        *got, done["node"][4] = lax.optimization_barrier((*got, done["node"][4]))
        return got

    received = exchange(outs[4:10], beside_z, beside_y)
    gl = done["gl"]
    hid_inner, raw_inner, dz_inner, g4, g_sums, *weights, merged = done["node"]
    outs = run(node_outer_kernel, "node_outer", [LATTICE] * 3 + [sds(4 * H + 32, H)] + [PLANE] * 6,
               [acc, pltpu.VMEM((4, 256, 256), F32), pltpu.VMEM((4, 8, H), F32), acc, acc, pltpu.SemaphoreType.DMA((2, 3))],
               (element_place, outer_sum, hs, gl, node_bias, *weights, g4, g_sums, *received), 8, hbm_out=(0, 1))
    hid_outer, raw_outer, dz_outer, ngrad = outs[:4]
    hid_inner, raw_inner, hid_outer, raw_outer = in_hbm(hid_inner, raw_inner, hid_outer, raw_outer)

    cot = [pltpu.VMEM((1,) + FULL[1:], F32)]
    parts = [LATTICE] * 2 + [sds(256, 256), sds(8, H)]

    done = {}

    def under_z(*got):
        *done["a"], w2t, wct = run(functools.partial(back_first_kernel, 1, HALF), "back_inner", parts + [split_weight] * 2, cot,
                                   (element_place, dz_inner, tv, sv, edge_mid, merged, edge_bias, w2), 10)
        done["w"] = (w2, w2t, wct)
        *got, done["a"][2] = lax.optimization_barrier((*got, done["a"][2]))
        return got

    def under_y(*got):
        done["b"] = run(functools.partial(back_inner_kernel, HALF, SIDE), "back_inner", parts, cot, (element_place, dz_inner, tv, sv, edge_bias, *done["w"]), 10)
        *got, done["b"][2] = lax.optimization_barrier((*got, done["b"][2]))
        return got

    received = exchange(outs[4:], under_z, under_y)
    part_a, part_b = done["a"], done["b"]
    payload, dt, ds = run(back_outer_kernel, "back_outer", [sds(PAYLOAD, H), LATTICE, LATTICE],
                          [acc] * 3 + [pltpu.SemaphoreType.DMA((2, SIDE))] + [total] * 3 + [pltpu.VMEM((2, 8, H), F32)],
                          (element_place, dz_outer, tv, sv, hs, edge_bias, *done["w"], ngrad, *part_a, *part_b, *received), 10, hbm_out=(1, 2))
    dt, ds = in_hbm(dt, ds)

    def beside_first():
        return run(feat_grad_kernel, "feat_grad", [sds(ROWS, H)], [acc] * 4 + [pltpu.SemaphoreType.DMA((4,)), pltpu.SemaphoreType.DMA((2, SIDE))] + [square] * 3,
                   (element_place, dt, ds, raw_inner, raw_outer, out_grad, lattice_of, edge_in, node_in), 8, hbm_in=(1, 2, 3, 4))[0]

    def beside_second():
        return run(new_feat_kernel, "new_feat", [sds(ROWS, H)], [acc, acc, pltpu.SemaphoreType.DMA((4,)), square],
                   (element_place, hid_inner, hid_outer, node_feat, lattice_of, node_mid, node_bias), 8, hbm_in=(1, 2))[0]

    total, feat_grad, new_feat = total_over_devices(payload, beside_first, beside_second)
    scale = 1.0 / math.sqrt(n * ELEM_DEV * NODES_EL)
    weights = pl.pallas_call(
        functools.partial(finish_kernel, scale),
        out_shape=(sds(256, H), sds(2, H, H), sds(3, H), sds(256, H), sds(2, H, H), sds(3, H)),
        in_specs=[VM] * 4, out_specs=(VM,) * 6, name="finish", compiler_params=SMALL,
    )(total, edge_mid, node_in, edge_bias)
    return (new_feat, feat_grad) + tuple(weights)


def solution(mesh):
    in_specs = (P("dom", None),) * 4 + (P(),) * 6
    out_specs = (P("dom", None), P("dom", None)) + (P(),) * 6
    return jax.shard_map(body, mesh=mesh, in_specs=in_specs, out_specs=out_specs, check_vma=False)
```

```python
import functools
import math

import jax
import jax.numpy as jnp
from jax import lax
from jax.experimental import pallas as pl
from jax.experimental.pallas import tpu as pltpu
from jax.sharding import PartitionSpec as P

SIDE = 8
ELEM_DEV = 8
DGX = 4
DGY = 4
NODES_EL = 512
H = 128
ROWS = ELEM_DEV * NODES_EL
PAYLOAD = 1024
HALF_LOAD = PAYLOAD // 2
F32 = jnp.float32
BF16 = jnp.bfloat16


def split(x):
    high = x.astype(BF16)
    low = (x - high.astype(F32)).astype(BF16)
    return jnp.concatenate([high, low], axis=-1)


def weight_split(w):
    row = split(w)
    return jnp.concatenate([row, row], axis=0)


def dot(a, b):
    return jnp.dot(a, b, preferred_element_type=F32)


def fold(o):
    return o[:, :H] + o[:, H:]


def mm(xs, w):
    return fold(dot(xs, w))


def mm_t(xs, ys):
    return lax.dot_general(xs, ys, (((0,), (0,)), ((), ())), preferred_element_type=F32)


def quad(o):
    return o[:H, :H] + o[:H, H:] + o[H:, :H] + o[H:, H:]


def row_sum(x):
    return jnp.sum(x.reshape(-1, 8, H), axis=0)


def exact_dot(a, b):
    return jnp.dot(a, b, precision=lax.Precision.HIGHEST, preferred_element_type=F32)


def flip(e):
    return (e // 4) * 448 + (e // 2 % 2) * 56 + (e % 2) * 7


def to_lattice_onehot(lat_ref, slot, e):
    row = lat_ref[pl.ds(slot, 1), :] ^ flip(e)
    level = lax.broadcasted_iota(jnp.int32, (NODES_EL, NODES_EL), 0)
    return jnp.where(level == row, 1.0, 0.0).astype(BF16)


def from_lattice_onehot(turned, slot, e):
    lane = lax.broadcasted_iota(jnp.int32, (NODES_EL, ELEM_DEV), 1)
    column = jnp.sum(jnp.where(lane == slot, turned, 0.0), axis=1, keepdims=True).astype(jnp.int32) ^ flip(e)
    level = lax.broadcasted_iota(jnp.int32, (NODES_EL, NODES_EL), 1)
    return jnp.where(level == column, 1.0, 0.0).astype(BF16)


def slot_of(place, e):
    slot = jnp.int32(0)
    for i in range(1, ELEM_DEV):
        slot = jnp.where(place[0, i] == e, jnp.int32(i), slot)
    return slot


def slot_rows(slot):
    return pl.ds(pl.multiple_of(slot * NODES_EL, NODES_EL), NODES_EL)


def element_rows(e):
    return pl.ds(e, NODES_EL, stride=ELEM_DEV)


def to_lattice(place, lat_ref, src_ref, dst_ref):
    def one(i, carry):
        for e in (2 * i, 2 * i + 1):
            slot = slot_of(place, e)
            both = dot(to_lattice_onehot(lat_ref, slot, e), split(src_ref[slot_rows(slot), :]))
            dst_ref[element_rows(e), :] = fold(both)
        return carry

    lax.fori_loop(0, ELEM_DEV // 2, one, 0)


def from_lattice(place, lat_ref, src_ref, add_ref, dst_ref, bias):
    turned = lat_ref[...].astype(F32).T

    def one(i, carry):
        for e in (2 * i, 2 * i + 1):
            slot = slot_of(place, e)
            back = from_lattice_onehot(turned, slot, e)
            rows = fold(dot(back, split(src_ref[element_rows(e), :])))
            rows = rows + add_ref[slot_rows(slot), :]
            dst_ref[slot_rows(slot), :] = rows if bias is None else rows + bias
        return carry

    lax.fori_loop(0, ELEM_DEV // 2, one, 0)


FULL = (SIDE, SIDE, SIDE, ELEM_DEV, H)
def two(i):
    return pl.ds(2 * i, 2)


def rows_at(ref, at):
    return ref[at].reshape(-1, H)


OUTER = [((0, 1), (0, 8), (0, 8)), ((1, 8), (0, 1), (0, 8)), ((1, 8), (1, 8), (0, 1))]
INNER = [((1, 8), (1, 8), (1, 8))]


def at_box(box):
    return tuple(pl.ds(a, b - a) for a, b in box)


def get(ref, box):
    return ref[at_box(box)].reshape(-1, H)


def shape_of(box):
    return tuple(b - a for a, b in box) + (ELEM_DEV, H)


def put(ref, box, rows):
    ref[at_box(box)] = rows.reshape(shape_of(box))


def add(ref, box, rows):
    ref[at_box(box)] += rows.reshape(shape_of(box))


def pairs_of(box):
    out = []
    for axis in range(3):
        for step in (1, -1):
            a, b = box[axis]
            a, b = (a, min(b, SIDE - 1)) if step == 1 else (max(a, 1), b)
            if a < b:
                out.append((box[:axis] + ((a, b),) + box[axis + 1:], box[:axis] + ((a + step, b + step),) + box[axis + 1:]))
    return out


SLAB = ((1, 8), (1, 8))


def slab_pairs(x):
    out = [((x, SLAB), (x - 1, SLAB), None)]
    for axis in range(2):
        for step in (1, -1):
            a, b = (1, SIDE - 1) if step == 1 else (1, SIDE)
            receivers = SLAB[:axis] + ((a, b),) + SLAB[axis + 1:]
            senders = SLAB[:axis] + ((a + step, b + step),) + SLAB[axis + 1:]
            out.append(((x, receivers), (x, senders), None))
    upper = jnp.where(x < SIDE - 1, 1.0, 0.0)
    out.append(((x, SLAB), (jnp.minimum(x + 1, SIDE - 1), SLAB), upper))
    return out


def at_slab(where):
    x, box = where
    return (x,) + tuple(pl.ds(a, b - a) for a, b in box)


def sget(ref, where):
    return ref[at_slab(where)].reshape(-1, H)


def sshape(where):
    return tuple(b - a for a, b in where[1]) + (ELEM_DEV, H)


def sput(ref, where, rows):
    ref[at_slab(where)] = rows.reshape(sshape(where))


def sadd(ref, where, rows):
    ref[at_slab(where)] += rows.reshape(sshape(where))


def swap(v, axis):
    if axis == 0:
        return pltpu.roll(v, 4, 1)
    by = 2 if axis == 1 else 1
    e = lax.broadcasted_iota(jnp.int32, v.shape, 1)
    return jnp.where((e & by) == 0, pltpu.roll(v, ELEM_DEV - by, 1), pltpu.roll(v, by, 1))


def assemble(ref, boxes):
    for axis in (2, 1, 0):
        for box in boxes:
            if box[axis][1] == SIDE:
                face = box[:axis] + ((SIDE - 1, SIDE),) + box[axis + 1:]
                v = ref[at_box(face)].reshape(-1, ELEM_DEV, H)
                put(ref, face, v + swap(v, axis))


STRIDES = (1, DGX, DGX * DGY)
BIT = (4, 2, 1)


def above():
    index = lax.axis_index("dom")
    return [1 - index // stride % 2 for stride in STRIDES]


def sides(axis):
    up = above()[axis]
    return up, 1 - up


def outer_rows(axis, e):
    if axis == 0:
        return [(pl.ds(e, 64, stride=8), pl.ds(0, 64))]
    if axis == 2:
        return [(pl.ds(e, 64, stride=64), pl.ds(0, 64))]
    return [(pl.ds(x * 512 + e, 8, stride=8), pl.ds(x * 8, 8)) for x in range(SIDE)]


def others(axis):
    return [e for e in range(ELEM_DEV) if not e & BIT[axis]]


def emit_planes(ref, planes):
    flat = ref.reshape((ROWS, H))
    for axis in range(3):
        for side, plane in zip(sides(axis), planes[axis]):
            for j, e in enumerate(others(axis)):
                for rows, there in outer_rows(axis, e + side * BIT[axis]):
                    plane[j, there, :] = flat[rows, :]


def add_planes(ref, planes):
    flat = ref.reshape((ROWS, H))
    for axis in range(3):
        for side, plane in zip(sides(axis), planes[axis]):
            for j, e in enumerate(others(axis)):
                for rows, there in outer_rows(axis, e + side * BIT[axis]):
                    flat[rows, :] += plane[j, there, :]


def half_silu(u):
    t = jnp.tanh(u)
    q = 1.0 + t
    return t, q, u * q


def twice_slope(t, q, s):
    return q + s * (1.0 - t)


def forward_edge(u1, w2, bias):
    _, _, s1 = half_silu(u1)
    _, _, s2 = half_silu(mm(split(s1), w2[...]) + bias)
    return s2


def edge_outer_kernel(place, h_hbm, lat_hbm, win_hbm, wmid_hbm, eb_hbm, hs_ref, t_ref, s_ref, sum_ref, x1, x2, y1, y2, z1, z2, w2,
                      wts, h_ref, lat_ref, win_ref, wmid_ref, eb_ref, sems, h_sems):
    small = [pltpu.make_async_copy(a, b, sems.at[i]) for i, (a, b) in enumerate(
        ((lat_hbm, lat_ref), (win_hbm, win_ref), (wmid_hbm, wmid_ref), (eb_hbm, eb_ref)))]
    for copy in small:
        copy.start()

    def rows_of(e):
        return pltpu.make_async_copy(h_hbm.at[slot_rows(slot_of(place, e)), :], h_ref.at[e], h_sems.at[e])

    for e in range(ELEM_DEV):
        rows_of(e).start()
    for copy in small:
        copy.wait()
    wts[:, 0:256] = weight_split(0.5 * win_ref[0:H, :])
    wts[:, 256:512] = weight_split(0.5 * win_ref[H:, :])
    w2[...] = weight_split(0.5 * wmid_ref[0])
    flat = hs_ref.reshape((ROWS, H))

    def one(i, carry):
        for e in (2 * i, 2 * i + 1):
            rows_of(e).wait()
        for e in (2 * i, 2 * i + 1):
            both = dot(to_lattice_onehot(lat_ref, slot_of(place, e), e), split(h_ref[e]))
            flat[element_rows(e), :] = fold(both)
        return carry

    lax.fori_loop(0, ELEM_DEV // 2, one, 0)
    half_bias = 0.5 * eb_ref[0:1, :]

    def plane(i, carry):
        both = dot(split(rows_at(hs_ref, two(i))), wts[...])
        t_ref[two(i)] = (fold(both[:, 0:256]) + half_bias).reshape((2,) + FULL[1:])
        s_ref[two(i)] = fold(both[:, 256:512]).reshape((2,) + FULL[1:])
        return carry

    lax.fori_loop(0, SIDE // 2, plane, 0)
    bias = 0.5 * eb_ref[1:2, :]
    for box in OUTER:
        put(sum_ref, box, jnp.zeros((math.prod(shape_of(box)) // H, H), F32))
        for receivers, senders in pairs_of(box):
            add(sum_ref, receivers, forward_edge(get(t_ref, receivers) + get(s_ref, senders), w2, bias))
    assemble(sum_ref, OUTER)
    emit_planes(sum_ref, ((x1, x2), (y1, y2), (z1, z2)))


def edge_inner_kernel(place, t_ref, s_ref, g_ref, lat_ref, eb_ref, w2, sum_ref, gl_ref):
    bias = 0.5 * eb_ref[1:2, :]

    def plane(x, carry):
        sput(sum_ref, (x, SLAB), jnp.zeros((49 * 8, H), F32))
        for receivers, senders, factor in slab_pairs(x):
            s2 = forward_edge(sget(t_ref, receivers) + sget(s_ref, senders), w2, bias)
            sadd(sum_ref, receivers, s2 if factor is None else s2 * factor)
        return carry

    lax.fori_loop(1, SIDE, plane, 0)
    assemble(sum_ref, INNER)
    to_lattice(place, lat_ref, g_ref, gl_ref.reshape((ROWS, H)))


def degree_of(where, shape):
    full = shape + (ELEM_DEV, H)
    e = lax.broadcasted_iota(jnp.int32, (ELEM_DEV, H), 0)
    count, own = None, None
    index, depth = lax.axis_index("dom"), lax.axis_size("dom") // (DGX * DGY)
    grid = (index % DGX, index // DGX % DGY, index // (DGX * DGY))
    for axis, limit in ((0, DGX), (1, DGY), (2, depth)):
        side = (e >> (2 - axis)) & 1
        low = jnp.where(grid[axis] > 0, 2.0, 1.0)
        high = jnp.where(grid[axis] < limit - 1, 2.0, 1.0)
        outer = jnp.broadcast_to(jnp.where(side == 0, low, high), full)
        at = lax.broadcasted_iota(jnp.int32, full, axis) + where[axis]
        times = jnp.where(at == 0, outer, jnp.where(at == SIDE - 1, 2.0, 1.0))
        messages = jnp.where((at == 0) | (at == SIDE - 1), 1.0, 2.0)
        count = times if count is None else count * times
        own = messages if own is None else own + messages
    return (count * own).reshape(-1, H)


def node_weights(nin_ref, nmid_ref, wmid_ref, eb_ref, weights):
    wa, wc, w0, w0t, w1t, row, merged_ref = weights
    lower = nin_ref[H:, :]
    wa[...] = weight_split(0.5 * nin_ref[0:H, :])
    merged = exact_dot(wmid_ref[1], lower)
    merged_ref[...] = merged
    wc[...] = weight_split(0.5 * merged)
    w0[...] = weight_split(0.5 * nmid_ref[0])
    w0t[...] = weight_split(0.5 * nmid_ref[0].T)
    w1t[...] = weight_split(0.5 * nmid_ref[1].T)
    row[...] = 0.5 * exact_dot(jnp.broadcast_to(eb_ref[2:3, :], (8, H)), lower)


def node_chunk(gathered, h, g, degree, nb_ref, weights, totals, sums):
    wa, wc, w0, w0t, w1t, row = weights[:6]
    g_a, g_m, g_0, g_1 = totals
    hs = split(h)
    gs = split(gathered)
    u = mm(hs, wa[...]) + mm(gs, wc[...]) + degree * row[0:1, :] + 0.5 * nb_ref[0:1, :]
    t, q, s = half_silu(u)
    slope = twice_slope(t, q, s)
    ss = split(s)
    t, q, s = half_silu(mm(ss, w0[...]) + 0.5 * nb_ref[1:2, :])
    slope1 = twice_slope(t, q, s)
    ss1 = split(s)
    hidden = s
    gl = split(g)
    sums[2] += row_sum(g)
    g_1[...] += mm_t(ss1, gl)
    dz1 = mm(gl, w1t[...]) * slope1
    sums[1] += row_sum(dz1)
    dz1s = split(dz1)
    g_0[...] += mm_t(ss, dz1s)
    dz = mm(dz1s, w0t[...]) * slope
    sums[0] += row_sum(dz)
    sums[3] += row_sum(dz * degree)
    dzs = split(dz)
    g_a[...] += mm_t(hs, dzs)
    g_m[...] += mm_t(gs, dzs)
    return hidden, dz


def node_inner_kernel(place, sum_ref, hs_ref, gl_ref, nin_ref, nmid_ref, nb_ref, wmid_ref, eb_ref, hid_hbm, raw_hbm, dz_ref, g_out, sums_out, *rest):
    weights, (hid_ref, raw_ref, sems) = rest[:7], rest[7:]
    node_weights(nin_ref, nmid_ref, wmid_ref, eb_ref, weights)
    totals = [g_out.at[i] for i in range(4)]
    g_out[...] = jnp.zeros_like(g_out)
    sums_out[...] = jnp.zeros_like(sums_out)

    def box_at(x, n):
        return (pl.ds(x, n), pl.ds(1, 7), pl.ds(1, 7))

    def planes(x, n):
        at, shape = box_at(x, n), (n, 7, 7, ELEM_DEV, H)
        hidden, dz = node_chunk(rows_at(sum_ref, at), rows_at(hs_ref, at), rows_at(gl_ref, at), degree_of((x, 1, 1), (n, 7, 7)), nb_ref, weights, totals, sums_out)
        hid_ref[at] = hidden.reshape(shape)
        dz_ref[at] = dz.reshape(shape)
        raw_ref[at] = dz.reshape(shape)
        for copy in copies(x, n):
            copy.start()

    def copies(x, n):
        at = box_at(x, n)
        return [pltpu.make_async_copy(a.at[at], b.at[at], sems.at[i, x]) for i, (a, b) in enumerate(((hid_ref, hid_hbm), (raw_ref, raw_hbm)))]

    def pair(i, carry):
        planes(2 * i + 1, 2)
        return carry

    lax.fori_loop(0, 3, pair, 0)
    planes(7, 1)
    assemble(dz_ref, INNER)
    for x, n in ((1, 2), (3, 2), (5, 2), (7, 1)):
        for copy in copies(x, n):
            copy.wait()


def node_outer_kernel(place, sum_ref, hs_ref, gl_ref, nb_ref, wa, wc, w0, w0t, w1t, row, g_in, sums_in,
                      rx1, rx2, ry1, ry2, rz1, rz2, hid_hbm, raw_hbm, dz_ref, grad_ref, x1, x2, y1, y2, z1, z2, acc, totals_ref, sums, hid_ref, raw_ref, sems):
    weights = (wa, wc, w0, w0t, w1t, row)
    totals_ref[...] = g_in[...]
    sums[...] = sums_in[...]
    totals = [totals_ref.at[i] for i in range(4)]
    for box in OUTER:
        acc[at_box(box)] = sum_ref[at_box(box)]
    add_planes(acc, ((rx1, rx2), (ry1, ry2), (rz1, rz2)))
    for box in OUTER:
        degree = degree_of(tuple(a for a, _ in box), tuple(b - a for a, b in box))
        hidden, dz = node_chunk(get(acc, box), get(hs_ref, box), get(gl_ref, box), degree, nb_ref, weights, totals, sums)
        put(hid_ref, box, hidden)
        put(dz_ref, box, dz)
        put(raw_ref, box, dz)
    copies = [pltpu.make_async_copy(a.at[at_box(box)], b.at[at_box(box)], sems.at[i, j])
              for i, (a, b) in enumerate(((hid_ref, hid_hbm), (raw_ref, raw_hbm))) for j, box in enumerate(OUTER)]
    for copy in copies:
        copy.start()
    assemble(dz_ref, OUTER)
    emit_planes(dz_ref, ((x1, x2), (y1, y2), (z1, z2)))
    grad_ref[0:H, :] = quad(totals_ref[1])
    grad_ref[H:2 * H, :] = quad(totals_ref[0])
    grad_ref[2 * H:3 * H, :] = quad(totals_ref[2])
    grad_ref[3 * H:4 * H, :] = quad(totals_ref[3])
    for i in range(4):
        grad_ref[4 * H + i * 8:4 * H + i * 8 + 8, :] = sums[i]
    for copy in copies:
        copy.wait()


def merge_copies(inner_hbm, outer_hbm, dst, sems):
    parts = [(inner_hbm, INNER[0])] + [(outer_hbm, box) for box in OUTER]
    return [pltpu.make_async_copy(a.at[at_box(box)], dst.at[at_box(box)], sems.at[i]) for i, (a, box) in enumerate(parts)]


def new_feat_kernel(place, hid_inner, hid_outer, h_ref, lat_ref, nmid_ref, nb_ref, new_ref, acc, hid, sems, w1):
    copies = merge_copies(hid_inner, hid_outer, hid, sems)
    for copy in copies:
        copy.start()
    w1[...] = weight_split(nmid_ref[1])
    for copy in copies:
        copy.wait()

    def plane(i, carry):
        acc[two(i)] = mm(split(rows_at(hid, two(i))), w1[...]).reshape((2,) + FULL[1:])
        return carry

    lax.fori_loop(0, SIDE // 2, plane, 0)
    from_lattice(place, lat_ref, acc.reshape((ROWS, H)), h_ref, new_ref, nb_ref[2:3, :])


def feat_grad_kernel(place, dt_hbm, ds_hbm, raw_inner, raw_outer, g_ref, lat_ref, win_ref, nin_ref, feat_ref, acc, dt_ref, ds_ref, raw, sems, slab_sems, wtt, wst, wat):
    copies = merge_copies(raw_inner, raw_outer, raw, sems)
    for copy in copies:
        copy.start()

    def slabs(x):
        return [pltpu.make_async_copy(a.at[x], b.at[x], slab_sems.at[i, x]) for i, (a, b) in enumerate(((dt_hbm, dt_ref), (ds_hbm, ds_ref)))]

    for x in range(SIDE):
        for copy in slabs(x):
            copy.start()
    wtt[...] = weight_split(win_ref[0:H, :].T)
    wst[...] = weight_split(win_ref[H:, :].T)
    wat[...] = weight_split(nin_ref[0:H, :].T)
    for copy in copies:
        copy.wait()

    def plane(i, carry):
        for copy in slabs(2 * i) + slabs(2 * i + 1):
            copy.wait()
        dh = mm(split(rows_at(dt_ref, two(i))), wtt[...]) + mm(split(rows_at(ds_ref, two(i))), wst[...]) + mm(split(rows_at(raw, two(i))), wat[...])
        acc[two(i)] = dh.reshape((2,) + FULL[1:])
        return carry

    lax.fori_loop(0, SIDE // 2, plane, 0)
    from_lattice(place, lat_ref, acc.reshape((ROWS, H)), g_ref, feat_ref, None)


def back_first_kernel(first, last, place, dz_ref, t_ref, s_ref, wmid_ref, merged_ref, eb_ref, w2, dt_ref, ds_ref, g2_ref, total_ref, w2t, wct, cot):
    w2t[...] = weight_split(0.5 * wmid_ref[0].T)
    wct[...] = weight_split(0.5 * merged_ref[...].T)
    back_inner_kernel(first, last, place, dz_ref, t_ref, s_ref, eb_ref, w2, w2t, wct, dt_ref, ds_ref, g2_ref, total_ref, cot)


def backward_edge(u1, cot, w2, w2t, bias, g_2, total):
    t1, q1, s1 = half_silu(u1)
    s1s = split(s1)
    t2, q2, s2 = half_silu(mm(s1s, w2[...]) + bias)
    dz2 = cot * twice_slope(t2, q2, s2)
    total[...] += row_sum(dz2)
    dz2s = split(dz2)
    g_2[...] += mm_t(s1s, dz2s)
    return mm(dz2s, w2t[...]) * twice_slope(t1, q1, s1)


def back_inner_kernel(first, last, place, dz_ref, t_ref, s_ref, eb_ref, w2, w2t, wct, dt_ref, ds_ref, g2_ref, total_ref, cot):
    bias = 0.5 * eb_ref[1:2, :]
    g2_ref[...] = jnp.zeros_like(g2_ref)
    total_ref[...] = jnp.zeros_like(total_ref)

    def clear(x, carry):
        ds_ref[x] = jnp.zeros(FULL[1:], F32)
        return carry

    lax.fori_loop(0, SIDE, clear, 0)

    def plane(x, carry):
        sput(dt_ref, (x, SLAB), jnp.zeros((49 * 8, H), F32))
        cot[0, pl.ds(1, 7), pl.ds(1, 7)] = mm(split(sget(dz_ref, (x, SLAB))), wct[...]).reshape(7, 7, ELEM_DEV, H)
        for receivers, senders, factor in slab_pairs(x):
            g = sget(cot, (0, receivers[1]))
            g = g if factor is None else g * factor
            dz1 = backward_edge(sget(t_ref, receivers) + sget(s_ref, senders), g, w2, w2t, bias, g2_ref, total_ref)
            sadd(dt_ref, receivers, dz1)
            sadd(ds_ref, senders, dz1)
        return carry

    lax.fori_loop(first, last, plane, 0)


def back_outer_kernel(place, dz_ref, t_ref, s_ref, hs_ref, eb_ref, w2, w2t, wct, ngrad_ref, dt_a, ds_a, g2_a, total_a, dt_b, ds_b, g2_b, total_b,
                      rx1, rx2, ry1, ry2, rz1, rz2, keep_ref, give_ref, dt_hbm, ds_hbm, acc, dt_ref, ds_ref, sems, g_2, g_t, g_s, sums, grad_ref):
    g_2[...] = g2_a[...] + g2_b[...]
    g_t[...] = jnp.zeros_like(g_t)
    g_s[...] = jnp.zeros_like(g_s)
    sums[0] = jnp.zeros((8, H), F32)
    sums[1] = total_a[...] + total_b[...]
    bias = 0.5 * eb_ref[1:2, :]
    for box in OUTER:
        acc[at_box(box)] = dz_ref[at_box(box)]
    add_planes(acc, ((rx1, rx2), (ry1, ry2), (rz1, rz2)))

    def senders_so_far(x, carry):
        ds_ref[x] = ds_a[x] + ds_b[x]
        return carry

    lax.fori_loop(0, SIDE, senders_so_far, 0)
    for source, first, last in ((dt_a, 1, HALF), (dt_b, HALF, SIDE)):
        dt_ref[first:last, 1:, 1:] = source[first:last, 1:, 1:]
    for box in OUTER:
        put(acc, box, mm(split(get(acc, box)), wct[...]))
        put(dt_ref, box, jnp.zeros((math.prod(shape_of(box)) // H, H), F32))
        for receivers, senders in pairs_of(box):
            dz1 = backward_edge(get(t_ref, receivers) + get(s_ref, senders), get(acc, receivers), w2, w2t, bias, g_2, sums.at[1])
            add(dt_ref, receivers, dz1)
            add(ds_ref, senders, dz1)

    def copies(x):
        return [pltpu.make_async_copy(a.at[x], b.at[x], sems.at[i, x]) for i, (a, b) in enumerate(((dt_ref, dt_hbm), (ds_ref, ds_hbm)))]

    for x in range(SIDE):
        for copy in copies(x):
            copy.start()

    def plane(i, carry):
        dt = rows_at(dt_ref, two(i))
        dts = split(dt)
        dss = split(rows_at(ds_ref, two(i)))
        hs = split(rows_at(hs_ref, two(i)))
        sums[0] += row_sum(dt)
        g_t[...] += mm_t(hs, dts)
        g_s[...] += mm_t(hs, dss)
        return carry

    lax.fori_loop(0, SIDE // 2, plane, 0)
    grad_ref[0:4 * H, :] = ngrad_ref[0:4 * H, :]
    grad_ref[4 * H:5 * H, :] = quad(g_t[...])
    grad_ref[5 * H:6 * H, :] = quad(g_s[...])
    grad_ref[6 * H:7 * H, :] = quad(g_2[...])
    grad_ref[7 * H:, :] = jnp.zeros((PAYLOAD - 7 * H, H), F32)
    for i in range(4):
        grad_ref[7 * H + i:7 * H + i + 1, :] = jnp.sum(ngrad_ref[4 * H + i * 8:4 * H + i * 8 + 8, :], axis=0, keepdims=True)
    for i in range(2):
        grad_ref[7 * H + 4 + i:7 * H + 5 + i, :] = jnp.sum(sums[i], axis=0, keepdims=True)
    core = lax.axis_index("dom") % 2
    keep_ref[...] = grad_ref[pl.ds(pl.multiple_of(core * HALF_LOAD, HALF_LOAD), HALF_LOAD), :]
    give_ref[...] = grad_ref[pl.ds(pl.multiple_of((1 - core) * HALF_LOAD, HALF_LOAD), HALF_LOAD), :]
    for x in range(SIDE):
        for copy in copies(x):
            copy.wait()


def finish_kernel(scale, mine_ref, other_ref, wmid_ref, nin_ref, eb_ref, ein_ref, emid_ref, ebias_ref, nino_ref, nmid_ref, nbias_ref):
    core = lax.axis_index("dom") % 2

    def span(a, b):
        half = a // HALF_LOAD
        at = slice(a - half * HALF_LOAD, b - half * HALF_LOAD)
        return jnp.where(core == half, mine_ref[at, :], other_ref[at, :])

    def rows(i):
        return span(i * H, (i + 1) * H)

    m = rows(0)
    lower = nin_ref[H:, :]
    biases = span(7 * H, 7 * H + 8)
    v = biases[3:4]
    ein_ref[0:H, :] = rows(4) * scale
    ein_ref[H:, :] = rows(5) * scale
    emid_ref[0] = rows(6) * scale
    emid_ref[1] = exact_dot(m, lower.T) * scale
    ebias_ref[0:2, :] = biases[4:6] * scale
    ebias_ref[2:3, :] = exact_dot(jnp.broadcast_to(v, (8, H)), lower.T)[0:1] * scale
    nino_ref[0:H, :] = rows(1) * scale
    outer = eb_ref[2:3, :].T * v
    nino_ref[H:, :] = (exact_dot(wmid_ref[1].T, m) + outer) * scale
    nmid_ref[0] = rows(2) * scale
    nmid_ref[1] = rows(3) * scale
    nbias_ref[...] = biases[0:3] * scale


def fix_y_kernel(y1, y2, rz1, rz2, o1, o2):
    o1[...] = y1[...]
    o2[...] = y2[...]
    line = pl.ds(0, 8, stride=SIDE)
    for py, out in zip(sides(1), (o1, o2)):
        for pz, rz in zip(sides(2), (rz1, rz2)):
            for px in range(2):
                out[px * 2 + pz, line, :] += rz[px * 2 + py, line, :]


def fix_x_kernel(x1, x2, rz1, rz2, ry1, ry2, o1, o2):
    o1[...] = x1[...]
    o2[...] = x2[...]
    first = pl.ds(0, 8)
    for px, out in zip(sides(0), (o1, o2)):
        for py, ry in zip(sides(1), (ry1, ry2)):
            for pz, rz in zip(sides(2), (rz1, rz2)):
                out[py * 2 + pz, pl.ds(0, 8, stride=SIDE), :] += rz[px * 2 + py, first, :]
                out[py * 2 + pz, first, :] += ry[px * 2 + pz, first, :]


PLANE = jax.ShapeDtypeStruct((4, 64, H), F32)
VM = pl.BlockSpec(memory_space=pltpu.VMEM)
SM = pl.BlockSpec(memory_space=pltpu.SMEM)
HB = pl.BlockSpec(memory_space=pltpu.MemorySpace.HBM)


def in_hbm(*values):
    return [pltpu.with_memory_space_constraint(v, pltpu.MemorySpace.HBM) for v in values]


def swapped(block, axis, second):
    n = lax.axis_size("dom")
    limit, stride = (DGX, DGY, n // (DGX * DGY))[axis], STRIDES[axis]
    route = []
    for i in range(n):
        at = i // stride % limit
        if at % 2 == second and at + 1 < limit:
            route += [(i, i + stride), (i + stride, i)]
    return lax.ppermute(block, "dom", route)


def sds(*shape, dtype=F32):
    return jax.ShapeDtypeStruct(shape, dtype)


HALF = 5
LATTICE = jax.ShapeDtypeStruct(FULL, F32)
LIMIT = 14
SMALL = pltpu.CompilerParams(vmem_limit_bytes=6 * 1024 * 1024)


def run(kernel, name, outs, scratch, args, micros, spec=VM, hbm_in=(), hbm_out=()):
    outs = [pltpu.MemorySpace.HBM(o.shape, o.dtype) if i in hbm_out else o for i, o in enumerate(outs)]
    call = pl.pallas_call(
        kernel, out_shape=outs, in_specs=[SM] + [HB if i in hbm_in else spec for i in range(1, len(args))], out_specs=[HB if i in hbm_out else VM for i in range(len(outs))], scratch_shapes=scratch,
        name=name,
        cost_estimate=pl.CostEstimate(flops=micros * 1000000000, bytes_accessed=8000000, transcendentals=0),
        compiler_params=pltpu.CompilerParams(vmem_limit_bytes=LIMIT * 1024 * 1024),
    )
    return list(call(*args))


def exchange(planes, beside_z, beside_y):
    x1, x2, y1, y2, z1, z2 = planes
    rz1, rz2 = swapped(z1, 2, 0), swapped(z2, 2, 1)
    rz1, rz2 = beside_z(rz1, rz2)
    y1, y2 = pl.pallas_call(fix_y_kernel, out_shape=(PLANE, PLANE), in_specs=[VM] * 4, out_specs=(VM, VM), name="fix_y", compiler_params=SMALL)(y1, y2, rz1, rz2)
    ry1, ry2 = swapped(y1, 1, 0), swapped(y2, 1, 1)
    ry1, ry2 = beside_y(ry1, ry2)
    x1, x2 = pl.pallas_call(fix_x_kernel, out_shape=(PLANE, PLANE), in_specs=[VM] * 6, out_specs=(VM, VM), name="fix_x", compiler_params=SMALL)(x1, x2, rz1, rz2, ry1, ry2)
    rx1, rx2 = swapped(x1, 0, 0), swapped(x2, 0, 1)
    return [rx1, rx2, ry1, ry2, rz1, rz2]


def spread_kernel(parts, out_ref):
    out_ref[...] = jnp.broadcast_to(jnp.sum(parts[...], axis=0, keepdims=True), out_ref.shape)


def total_over_devices(keep, give, beside_first, beside_second):
    n = lax.axis_size("dom")
    pairs = [(i, i ^ 1) for i in range(n)]
    cores = [list(range(core, n, 2)) for core in range(2)]
    block = keep + lax.ppermute(give, "dom", pairs)
    parts = lax.all_to_all(block.reshape(n // 2, -1, H), "dom", 0, 0, axis_index_groups=cores, tiled=True)
    parts, first = lax.optimization_barrier((parts, beside_first()))
    spread = pl.pallas_call(
        spread_kernel, out_shape=sds(*parts.shape), in_specs=[VM], out_specs=VM, name="spread", compiler_params=SMALL,
    )(parts)
    total = lax.all_to_all(spread, "dom", 0, 0, axis_index_groups=cores, tiled=True)
    total, second = lax.optimization_barrier((total, beside_second()))
    total = total.reshape(-1, H)
    return total, lax.ppermute(total, "dom", pairs), first, second


def body(node_feat, out_grad, lattice_of, element_place, edge_in, edge_mid, edge_bias, node_in, node_mid, node_bias):
    n = lax.axis_size("dom")
    square, wide, acc = pltpu.VMEM((256, 256), BF16), pltpu.VMEM((256, 512), BF16), pltpu.VMEM(FULL, F32)
    total = pltpu.VMEM((256, 256), F32)

    split_weight = sds(256, 256, dtype=BF16)
    outs = run(edge_outer_kernel, "edge_outer", [LATTICE] * 4 + [PLANE] * 6 + [split_weight],
               [wide, pltpu.VMEM((ELEM_DEV, NODES_EL, H), F32), pltpu.VMEM((ELEM_DEV, NODES_EL), jnp.int32), pltpu.VMEM((256, H), F32),
                pltpu.VMEM((2, H, H), F32), pltpu.VMEM((3, H), F32), pltpu.SemaphoreType.DMA((4,)), pltpu.SemaphoreType.DMA((ELEM_DEV,))],
               (element_place, *in_hbm(node_feat, lattice_of, edge_in, edge_mid, edge_bias)), 8, HB)
    hs, tv, sv, outer_sum = outs[:4]
    w2 = outs[10]
    node_args = (node_in, node_mid, node_bias, edge_mid, edge_bias)
    weights = [split_weight] * 5 + [sds(8, H), sds(H, H)]

    done = {}

    def beside_z(*got):
        inner_sum, gl = run(edge_inner_kernel, "edge_inner", [LATTICE] * 2, [], (element_place, tv, sv, out_grad, lattice_of, edge_bias, w2), 12)
        *got, done["sum"], done["gl"] = lax.optimization_barrier((*got, inner_sum, gl))
        return got

    def beside_y(*got):
        done["node"] = run(node_inner_kernel, "node_inner", [LATTICE] * 3 + [sds(4, 256, 256), sds(4, 8, H)] + weights, [acc, acc, pltpu.SemaphoreType.DMA((2, SIDE))],
                           (element_place, done["sum"], hs, done["gl"]) + node_args, 12, hbm_out=(0, 1))
        *got, done["node"][4] = lax.optimization_barrier((*got, done["node"][4]))
        return got

    received = exchange(outs[4:10], beside_z, beside_y)
    gl = done["gl"]
    hid_inner, raw_inner, dz_inner, g4, g_sums, *weights, merged = done["node"]
    outs = run(node_outer_kernel, "node_outer", [LATTICE] * 3 + [sds(4 * H + 32, H)] + [PLANE] * 6,
               [acc, pltpu.VMEM((4, 256, 256), F32), pltpu.VMEM((4, 8, H), F32), acc, acc, pltpu.SemaphoreType.DMA((2, 3))],
               (element_place, outer_sum, hs, gl, node_bias, *weights, g4, g_sums, *received), 8, hbm_out=(0, 1))
    hid_outer, raw_outer, dz_outer, ngrad = outs[:4]
    hid_inner, raw_inner, hid_outer, raw_outer = in_hbm(hid_inner, raw_inner, hid_outer, raw_outer)

    cot = [pltpu.VMEM((1,) + FULL[1:], F32)]
    parts = [LATTICE] * 2 + [sds(256, 256), sds(8, H)]

    done = {}

    def under_z(*got):
        *done["a"], w2t, wct = run(functools.partial(back_first_kernel, 1, HALF), "back_inner", parts + [split_weight] * 2, cot,
                                   (element_place, dz_inner, tv, sv, edge_mid, merged, edge_bias, w2), 10)
        done["w"] = (w2, w2t, wct)
        *got, done["a"][2] = lax.optimization_barrier((*got, done["a"][2]))
        return got

    def under_y(*got):
        done["b"] = run(functools.partial(back_inner_kernel, HALF, SIDE), "back_inner", parts, cot, (element_place, dz_inner, tv, sv, edge_bias, *done["w"]), 10)
        *got, done["b"][2] = lax.optimization_barrier((*got, done["b"][2]))
        return got

    received = exchange(outs[4:], under_z, under_y)
    part_a, part_b = done["a"], done["b"]
    keep, give, dt, ds = run(back_outer_kernel, "back_outer", [sds(HALF_LOAD, H), sds(HALF_LOAD, H), LATTICE, LATTICE],
                          [acc] * 3 + [pltpu.SemaphoreType.DMA((2, SIDE))] + [total] * 3 + [pltpu.VMEM((2, 8, H), F32), pltpu.VMEM((PAYLOAD, H), F32)],
                          (element_place, dz_outer, tv, sv, hs, edge_bias, *done["w"], ngrad, *part_a, *part_b, *received), 10, hbm_out=(2, 3))
    dt, ds = in_hbm(dt, ds)

    def beside_first():
        return run(feat_grad_kernel, "feat_grad", [sds(ROWS, H)], [acc] * 4 + [pltpu.SemaphoreType.DMA((4,)), pltpu.SemaphoreType.DMA((2, SIDE))] + [square] * 3,
                   (element_place, dt, ds, raw_inner, raw_outer, out_grad, lattice_of, edge_in, node_in), 8, hbm_in=(1, 2, 3, 4))[0]

    def beside_second():
        return run(new_feat_kernel, "new_feat", [sds(ROWS, H)], [acc, acc, pltpu.SemaphoreType.DMA((4,)), square],
                   (element_place, hid_inner, hid_outer, node_feat, lattice_of, node_mid, node_bias), 8, hbm_in=(1, 2))[0]

    mine, other, feat_grad, new_feat = total_over_devices(keep, give, beside_first, beside_second)
    scale = 1.0 / math.sqrt(n * ELEM_DEV * NODES_EL)
    weights = pl.pallas_call(
        functools.partial(finish_kernel, scale),
        out_shape=(sds(256, H), sds(2, H, H), sds(3, H), sds(256, H), sds(2, H, H), sds(3, H)),
        in_specs=[VM] * 5, out_specs=(VM,) * 6, name="finish", compiler_params=SMALL,
    )(mine, other, edge_mid, node_in, edge_bias)
    return (new_feat, feat_grad) + tuple(weights)


def solution(mesh):
    in_specs = (P("dom", None),) * 4 + (P(),) * 6
    out_specs = (P("dom", None), P("dom", None)) + (P(),) * 6
    return jax.shard_map(body, mesh=mesh, in_specs=in_specs, out_specs=out_specs, check_vma=False)
```

```python
import functools
import math

import jax
import jax.numpy as jnp
from jax import lax
from jax.experimental import pallas as pl
from jax.experimental.pallas import tpu as pltpu
from jax.sharding import PartitionSpec as P

SIDE = 8
ELEM_DEV = 8
DGX = 4
DGY = 4
NODES_EL = 512
H = 128
ROWS = ELEM_DEV * NODES_EL
PAYLOAD = 1024
HALF_LOAD = PAYLOAD // 2
F32 = jnp.float32
BF16 = jnp.bfloat16


def split(x):
    high = x.astype(BF16)
    low = (x - high.astype(F32)).astype(BF16)
    return jnp.concatenate([high, low], axis=-1)


def weight_split(w):
    row = split(w)
    return jnp.concatenate([row, row], axis=0)


def dot(a, b):
    return jnp.dot(a, b, preferred_element_type=F32)


def fold(o):
    return o[:, :H] + o[:, H:]


def mm(xs, w):
    return fold(dot(xs, w))


def mm_t(xs, ys):
    return lax.dot_general(xs, ys, (((0,), (0,)), ((), ())), preferred_element_type=F32)


def quad(o):
    return o[:H, :H] + o[:H, H:] + o[H:, :H] + o[H:, H:]


def row_sum(x):
    return jnp.sum(x.reshape(-1, 8, H), axis=0)


def exact_dot(a, b):
    return jnp.dot(a, b, precision=lax.Precision.HIGHEST, preferred_element_type=F32)


def flip(e):
    return (e // 4) * 448 + (e // 2 % 2) * 56 + (e % 2) * 7


def to_lattice_onehot(lat_ref, slot, e):
    row = lat_ref[pl.ds(slot, 1), :] ^ flip(e)
    level = lax.broadcasted_iota(jnp.int32, (NODES_EL, NODES_EL), 0)
    return jnp.where(level == row, 1.0, 0.0).astype(BF16)


def from_lattice_onehot(turned, slot, e):
    lane = lax.broadcasted_iota(jnp.int32, (NODES_EL, ELEM_DEV), 1)
    column = jnp.sum(jnp.where(lane == slot, turned, 0.0), axis=1, keepdims=True).astype(jnp.int32) ^ flip(e)
    level = lax.broadcasted_iota(jnp.int32, (NODES_EL, NODES_EL), 1)
    return jnp.where(level == column, 1.0, 0.0).astype(BF16)


def slot_of(place, e):
    slot = jnp.int32(0)
    for i in range(1, ELEM_DEV):
        slot = jnp.where(place[0, i] == e, jnp.int32(i), slot)
    return slot


def slot_rows(slot):
    return pl.ds(pl.multiple_of(slot * NODES_EL, NODES_EL), NODES_EL)


def element_rows(e):
    return pl.ds(e, NODES_EL, stride=ELEM_DEV)


def to_lattice(place, lat_ref, src_ref, dst_ref):
    def one(i, carry):
        for e in (2 * i, 2 * i + 1):
            slot = slot_of(place, e)
            both = dot(to_lattice_onehot(lat_ref, slot, e), split(src_ref[slot_rows(slot), :]))
            dst_ref[element_rows(e), :] = fold(both)
        return carry

    lax.fori_loop(0, ELEM_DEV // 2, one, 0)


def from_lattice(place, lat_ref, src_ref, add_ref, dst_ref, bias):
    turned = lat_ref[...].astype(F32).T

    def one(i, carry):
        for e in (2 * i, 2 * i + 1):
            slot = slot_of(place, e)
            back = from_lattice_onehot(turned, slot, e)
            rows = fold(dot(back, split(src_ref[element_rows(e), :])))
            rows = rows + add_ref[slot_rows(slot), :]
            dst_ref[slot_rows(slot), :] = rows if bias is None else rows + bias
        return carry

    lax.fori_loop(0, ELEM_DEV // 2, one, 0)


FULL = (SIDE, SIDE, SIDE, ELEM_DEV, H)
def two(i):
    return pl.ds(2 * i, 2)


def rows_at(ref, at):
    return ref[at].reshape(-1, H)


OUTER = [((0, 1), (0, 8), (0, 8)), ((1, 8), (0, 1), (0, 8)), ((1, 8), (1, 8), (0, 1))]
INNER = [((1, 8), (1, 8), (1, 8))]


def at_box(box):
    return tuple(pl.ds(a, b - a) for a, b in box)


def get(ref, box):
    return ref[at_box(box)].reshape(-1, H)


def shape_of(box):
    return tuple(b - a for a, b in box) + (ELEM_DEV, H)


def put(ref, box, rows):
    ref[at_box(box)] = rows.reshape(shape_of(box))


def add(ref, box, rows):
    ref[at_box(box)] += rows.reshape(shape_of(box))


def pairs_of(box):
    out = []
    for axis in range(3):
        for step in (1, -1):
            a, b = box[axis]
            a, b = (a, min(b, SIDE - 1)) if step == 1 else (max(a, 1), b)
            if a < b:
                out.append((box[:axis] + ((a, b),) + box[axis + 1:], box[:axis] + ((a + step, b + step),) + box[axis + 1:]))
    return out


SLAB = ((1, 8), (1, 8))


def slab_pairs(x):
    out = [((x, SLAB), (x - 1, SLAB), None)]
    for axis in range(2):
        for step in (1, -1):
            a, b = (1, SIDE - 1) if step == 1 else (1, SIDE)
            receivers = SLAB[:axis] + ((a, b),) + SLAB[axis + 1:]
            senders = SLAB[:axis] + ((a + step, b + step),) + SLAB[axis + 1:]
            out.append(((x, receivers), (x, senders), None))
    upper = jnp.where(x < SIDE - 1, 1.0, 0.0)
    out.append(((x, SLAB), (jnp.minimum(x + 1, SIDE - 1), SLAB), upper))
    return out


def at_slab(where):
    x, box = where
    return (x,) + tuple(pl.ds(a, b - a) for a, b in box)


def sget(ref, where):
    return ref[at_slab(where)].reshape(-1, H)


def sshape(where):
    return tuple(b - a for a, b in where[1]) + (ELEM_DEV, H)


def sput(ref, where, rows):
    ref[at_slab(where)] = rows.reshape(sshape(where))


def sadd(ref, where, rows):
    ref[at_slab(where)] += rows.reshape(sshape(where))


def swap(v, axis):
    if axis == 0:
        return pltpu.roll(v, 4, 1)
    by = 2 if axis == 1 else 1
    e = lax.broadcasted_iota(jnp.int32, v.shape, 1)
    return jnp.where((e & by) == 0, pltpu.roll(v, ELEM_DEV - by, 1), pltpu.roll(v, by, 1))


def assemble(ref, boxes):
    for axis in (2, 1, 0):
        for box in boxes:
            if box[axis][1] == SIDE:
                face = box[:axis] + ((SIDE - 1, SIDE),) + box[axis + 1:]
                v = ref[at_box(face)].reshape(-1, ELEM_DEV, H)
                put(ref, face, v + swap(v, axis))


STRIDES = (1, DGX, DGX * DGY)
BIT = (4, 2, 1)


def above():
    index = lax.axis_index("dom")
    return [1 - index // stride % 2 for stride in STRIDES]


def sides(axis):
    up = above()[axis]
    return up, 1 - up


def outer_rows(axis, e):
    if axis == 0:
        return [(pl.ds(e, 64, stride=8), pl.ds(0, 64))]
    if axis == 2:
        return [(pl.ds(e, 64, stride=64), pl.ds(0, 64))]
    return [(pl.ds(x * 512 + e, 8, stride=8), pl.ds(x * 8, 8)) for x in range(SIDE)]


def others(axis):
    return [e for e in range(ELEM_DEV) if not e & BIT[axis]]


def emit_planes(ref, planes):
    flat = ref.reshape((ROWS, H))
    for axis in range(3):
        for side, plane in zip(sides(axis), planes[axis]):
            for j, e in enumerate(others(axis)):
                for rows, there in outer_rows(axis, e + side * BIT[axis]):
                    plane[j, there, :] = flat[rows, :]


def add_planes(ref, planes):
    flat = ref.reshape((ROWS, H))
    for axis in range(3):
        for side, plane in zip(sides(axis), planes[axis]):
            for j, e in enumerate(others(axis)):
                for rows, there in outer_rows(axis, e + side * BIT[axis]):
                    flat[rows, :] += plane[j, there, :]


def half_silu(u):
    t = jnp.tanh(u)
    q = 1.0 + t
    return t, q, u * q


def twice_slope(t, q, s):
    return q + s * (1.0 - t)


def forward_edge(u1, w2, bias):
    _, _, s1 = half_silu(u1)
    _, _, s2 = half_silu(mm(split(s1), w2[...]) + bias)
    return s2


def edge_outer_kernel(place, h_hbm, lat_hbm, win_hbm, wmid_hbm, eb_hbm, hs_ref, t_ref, s_ref, sum_ref, x1, x2, y1, y2, z1, z2, w2,
                      wts, h_ref, lat_ref, win_ref, wmid_ref, eb_ref, sems, h_sems):
    small = [pltpu.make_async_copy(a, b, sems.at[i]) for i, (a, b) in enumerate(
        ((lat_hbm, lat_ref), (win_hbm, win_ref), (wmid_hbm, wmid_ref), (eb_hbm, eb_ref)))]
    for copy in small:
        copy.start()

    def rows_of(e):
        return pltpu.make_async_copy(h_hbm.at[slot_rows(slot_of(place, e)), :], h_ref.at[e], h_sems.at[e])

    for e in range(ELEM_DEV):
        rows_of(e).start()
    for copy in small:
        copy.wait()
    wts[:, 0:256] = weight_split(0.5 * win_ref[0:H, :])
    wts[:, 256:512] = weight_split(0.5 * win_ref[H:, :])
    w2[...] = weight_split(0.5 * wmid_ref[0])
    flat = hs_ref.reshape((ROWS, H))

    def one(i, carry):
        for e in (2 * i, 2 * i + 1):
            rows_of(e).wait()
        for e in (2 * i, 2 * i + 1):
            both = dot(to_lattice_onehot(lat_ref, slot_of(place, e), e), split(h_ref[e]))
            flat[element_rows(e), :] = fold(both)
        return carry

    lax.fori_loop(0, ELEM_DEV // 2, one, 0)
    half_bias = 0.5 * eb_ref[0:1, :]

    def plane(i, carry):
        both = dot(split(rows_at(hs_ref, two(i))), wts[...])
        t_ref[two(i)] = (fold(both[:, 0:256]) + half_bias).reshape((2,) + FULL[1:])
        s_ref[two(i)] = fold(both[:, 256:512]).reshape((2,) + FULL[1:])
        return carry

    lax.fori_loop(0, SIDE // 2, plane, 0)
    bias = 0.5 * eb_ref[1:2, :]
    for box in OUTER:
        put(sum_ref, box, jnp.zeros((math.prod(shape_of(box)) // H, H), F32))
        for receivers, senders in pairs_of(box):
            add(sum_ref, receivers, forward_edge(get(t_ref, receivers) + get(s_ref, senders), w2, bias))
    assemble(sum_ref, OUTER)
    emit_planes(sum_ref, ((x1, x2), (y1, y2), (z1, z2)))


def edge_inner_kernel(place, t_ref, s_ref, g_ref, lat_ref, eb_ref, w2, sum_ref, gl_ref):
    bias = 0.5 * eb_ref[1:2, :]

    def plane(x, carry):
        sput(sum_ref, (x, SLAB), jnp.zeros((49 * 8, H), F32))
        for receivers, senders, factor in slab_pairs(x):
            s2 = forward_edge(sget(t_ref, receivers) + sget(s_ref, senders), w2, bias)
            sadd(sum_ref, receivers, s2 if factor is None else s2 * factor)
        return carry

    lax.fori_loop(1, SIDE, plane, 0)
    assemble(sum_ref, INNER)
    to_lattice(place, lat_ref, g_ref, gl_ref.reshape((ROWS, H)))


def degree_of(where, shape):
    full = shape + (ELEM_DEV, H)
    e = lax.broadcasted_iota(jnp.int32, (ELEM_DEV, H), 0)
    count, own = None, None
    index, depth = lax.axis_index("dom"), lax.axis_size("dom") // (DGX * DGY)
    grid = (index % DGX, index // DGX % DGY, index // (DGX * DGY))
    for axis, limit in ((0, DGX), (1, DGY), (2, depth)):
        side = (e >> (2 - axis)) & 1
        low = jnp.where(grid[axis] > 0, 2.0, 1.0)
        high = jnp.where(grid[axis] < limit - 1, 2.0, 1.0)
        outer = jnp.broadcast_to(jnp.where(side == 0, low, high), full)
        at = lax.broadcasted_iota(jnp.int32, full, axis) + where[axis]
        times = jnp.where(at == 0, outer, jnp.where(at == SIDE - 1, 2.0, 1.0))
        messages = jnp.where((at == 0) | (at == SIDE - 1), 1.0, 2.0)
        count = times if count is None else count * times
        own = messages if own is None else own + messages
    return (count * own).reshape(-1, H)


def node_weights(nin_ref, nmid_ref, wmid_ref, eb_ref, weights):
    wa, wc, w0, w0t, w1t, row, merged_ref = weights
    lower = nin_ref[H:, :]
    wa[...] = weight_split(0.5 * nin_ref[0:H, :])
    merged = exact_dot(wmid_ref[1], lower)
    merged_ref[...] = merged
    wc[...] = weight_split(0.5 * merged)
    w0[...] = weight_split(0.5 * nmid_ref[0])
    w0t[...] = weight_split(0.5 * nmid_ref[0].T)
    w1t[...] = weight_split(0.5 * nmid_ref[1].T)
    row[...] = 0.5 * exact_dot(jnp.broadcast_to(eb_ref[2:3, :], (8, H)), lower)


def node_chunk(gathered, h, g, degree, nb_ref, weights, totals, sums):
    wa, wc, w0, w0t, w1t, row = weights[:6]
    g_a, g_m, g_0, g_1 = totals
    hs = split(h)
    gs = split(gathered)
    u = mm(hs, wa[...]) + mm(gs, wc[...]) + degree * row[0:1, :] + 0.5 * nb_ref[0:1, :]
    t, q, s = half_silu(u)
    slope = twice_slope(t, q, s)
    ss = split(s)
    t, q, s = half_silu(mm(ss, w0[...]) + 0.5 * nb_ref[1:2, :])
    slope1 = twice_slope(t, q, s)
    ss1 = split(s)
    hidden = s
    gl = split(g)
    sums[2] += row_sum(g)
    g_1[...] += mm_t(ss1, gl)
    dz1 = mm(gl, w1t[...]) * slope1
    sums[1] += row_sum(dz1)
    dz1s = split(dz1)
    g_0[...] += mm_t(ss, dz1s)
    dz = mm(dz1s, w0t[...]) * slope
    sums[0] += row_sum(dz)
    sums[3] += row_sum(dz * degree)
    dzs = split(dz)
    g_a[...] += mm_t(hs, dzs)
    g_m[...] += mm_t(gs, dzs)
    return hidden, dz


def node_inner_kernel(place, sum_ref, hs_ref, gl_ref, nin_ref, nmid_ref, nb_ref, wmid_ref, eb_ref, hid_hbm, raw_hbm, dz_ref, g_out, sums_out, *rest):
    weights, (hid_ref, raw_ref, sems) = rest[:7], rest[7:]
    node_weights(nin_ref, nmid_ref, wmid_ref, eb_ref, weights)
    totals = [g_out.at[i] for i in range(4)]
    g_out[...] = jnp.zeros_like(g_out)
    sums_out[...] = jnp.zeros_like(sums_out)

    def box_at(x, n):
        return (pl.ds(x, n), pl.ds(1, 7), pl.ds(1, 7))

    def planes(x, n):
        at, shape = box_at(x, n), (n, 7, 7, ELEM_DEV, H)
        hidden, dz = node_chunk(rows_at(sum_ref, at), rows_at(hs_ref, at), rows_at(gl_ref, at), degree_of((x, 1, 1), (n, 7, 7)), nb_ref, weights, totals, sums_out)
        hid_ref[at] = hidden.reshape(shape)
        dz_ref[at] = dz.reshape(shape)
        raw_ref[at] = dz.reshape(shape)
        for copy in copies(x, n):
            copy.start()

    def copies(x, n):
        at = box_at(x, n)
        return [pltpu.make_async_copy(a.at[at], b.at[at], sems.at[i, x]) for i, (a, b) in enumerate(((hid_ref, hid_hbm), (raw_ref, raw_hbm)))]

    def pair(i, carry):
        planes(2 * i + 1, 2)
        return carry

    lax.fori_loop(0, 3, pair, 0)
    planes(7, 1)
    assemble(dz_ref, INNER)
    for x, n in ((1, 2), (3, 2), (5, 2), (7, 1)):
        for copy in copies(x, n):
            copy.wait()


def node_outer_kernel(place, sum_ref, hs_ref, gl_ref, nb_ref, wa, wc, w0, w0t, w1t, row, g_in, sums_in,
                      rx1, rx2, ry1, ry2, rz1, rz2, hid_hbm, raw_hbm, dz_ref, grad_ref, x1, x2, y1, y2, z1, z2, acc, totals_ref, sums, hid_ref, raw_ref, sems):
    weights = (wa, wc, w0, w0t, w1t, row)
    totals_ref[...] = g_in[...]
    sums[...] = sums_in[...]
    totals = [totals_ref.at[i] for i in range(4)]
    for box in OUTER:
        acc[at_box(box)] = sum_ref[at_box(box)]
    add_planes(acc, ((rx1, rx2), (ry1, ry2), (rz1, rz2)))
    for box in OUTER:
        degree = degree_of(tuple(a for a, _ in box), tuple(b - a for a, b in box))
        hidden, dz = node_chunk(get(acc, box), get(hs_ref, box), get(gl_ref, box), degree, nb_ref, weights, totals, sums)
        put(hid_ref, box, hidden)
        put(dz_ref, box, dz)
        put(raw_ref, box, dz)
    copies = [pltpu.make_async_copy(a.at[at_box(box)], b.at[at_box(box)], sems.at[i, j])
              for i, (a, b) in enumerate(((hid_ref, hid_hbm), (raw_ref, raw_hbm))) for j, box in enumerate(OUTER)]
    for copy in copies:
        copy.start()
    assemble(dz_ref, OUTER)
    emit_planes(dz_ref, ((x1, x2), (y1, y2), (z1, z2)))
    grad_ref[0:H, :] = quad(totals_ref[1])
    grad_ref[H:2 * H, :] = quad(totals_ref[0])
    grad_ref[2 * H:3 * H, :] = quad(totals_ref[2])
    grad_ref[3 * H:4 * H, :] = quad(totals_ref[3])
    for i in range(4):
        grad_ref[4 * H + i * 8:4 * H + i * 8 + 8, :] = sums[i]
    for copy in copies:
        copy.wait()


def merge_copies(inner_hbm, outer_hbm, dst, sems):
    parts = [(inner_hbm, INNER[0])] + [(outer_hbm, box) for box in OUTER]
    return [pltpu.make_async_copy(a.at[at_box(box)], dst.at[at_box(box)], sems.at[i]) for i, (a, box) in enumerate(parts)]


def new_feat_kernel(place, hid_inner, hid_outer, h_hbm, lat_ref, nmid_ref, nb_ref, new_ref, acc, hid, sems, w1, h_ref, h_sem):
    copies = merge_copies(hid_inner, hid_outer, hid, sems)
    features = pltpu.make_async_copy(h_hbm, h_ref, h_sem)
    for copy in copies:
        copy.start()
    features.start()
    w1[...] = weight_split(nmid_ref[1])
    for copy in copies:
        copy.wait()

    def plane(i, carry):
        acc[two(i)] = mm(split(rows_at(hid, two(i))), w1[...]).reshape((2,) + FULL[1:])
        return carry

    lax.fori_loop(0, SIDE // 2, plane, 0)
    features.wait()
    from_lattice(place, lat_ref, acc.reshape((ROWS, H)), h_ref, new_ref, nb_ref[2:3, :])


def feat_grad_kernel(place, dt_hbm, ds_hbm, raw_inner, raw_outer, g_ref, lat_ref, win_ref, nin_ref, feat_ref, acc, dt_ref, ds_ref, raw, sems, slab_sems, wtt, wst, wat):
    copies = merge_copies(raw_inner, raw_outer, raw, sems)
    for copy in copies:
        copy.start()

    def slabs(x):
        return [pltpu.make_async_copy(a.at[x], b.at[x], slab_sems.at[i, x]) for i, (a, b) in enumerate(((dt_hbm, dt_ref), (ds_hbm, ds_ref)))]

    for x in range(SIDE):
        for copy in slabs(x):
            copy.start()
    wtt[...] = weight_split(win_ref[0:H, :].T)
    wst[...] = weight_split(win_ref[H:, :].T)
    wat[...] = weight_split(nin_ref[0:H, :].T)
    for copy in copies:
        copy.wait()

    def plane(i, carry):
        for copy in slabs(2 * i) + slabs(2 * i + 1):
            copy.wait()
        dh = mm(split(rows_at(dt_ref, two(i))), wtt[...]) + mm(split(rows_at(ds_ref, two(i))), wst[...]) + mm(split(rows_at(raw, two(i))), wat[...])
        acc[two(i)] = dh.reshape((2,) + FULL[1:])
        return carry

    lax.fori_loop(0, SIDE // 2, plane, 0)
    from_lattice(place, lat_ref, acc.reshape((ROWS, H)), g_ref, feat_ref, None)


def back_first_kernel(first, last, place, dz_ref, t_ref, s_ref, wmid_ref, merged_ref, eb_ref, w2, dt_ref, ds_ref, g2_ref, total_ref, w2t, wct, cot):
    w2t[...] = weight_split(0.5 * wmid_ref[0].T)
    wct[...] = weight_split(0.5 * merged_ref[...].T)
    back_inner_kernel(first, last, place, dz_ref, t_ref, s_ref, eb_ref, w2, w2t, wct, dt_ref, ds_ref, g2_ref, total_ref, cot)


def backward_edge(u1, cot, w2, w2t, bias, g_2, total):
    t1, q1, s1 = half_silu(u1)
    s1s = split(s1)
    t2, q2, s2 = half_silu(mm(s1s, w2[...]) + bias)
    dz2 = cot * twice_slope(t2, q2, s2)
    total[...] += row_sum(dz2)
    dz2s = split(dz2)
    g_2[...] += mm_t(s1s, dz2s)
    return mm(dz2s, w2t[...]) * twice_slope(t1, q1, s1)


def back_inner_kernel(first, last, place, dz_ref, t_ref, s_ref, eb_ref, w2, w2t, wct, dt_ref, ds_ref, g2_ref, total_ref, cot):
    bias = 0.5 * eb_ref[1:2, :]
    g2_ref[...] = jnp.zeros_like(g2_ref)
    total_ref[...] = jnp.zeros_like(total_ref)

    def clear(x, carry):
        ds_ref[x] = jnp.zeros(FULL[1:], F32)
        return carry

    lax.fori_loop(0, SIDE, clear, 0)

    def plane(x, carry):
        sput(dt_ref, (x, SLAB), jnp.zeros((49 * 8, H), F32))
        cot[0, pl.ds(1, 7), pl.ds(1, 7)] = mm(split(sget(dz_ref, (x, SLAB))), wct[...]).reshape(7, 7, ELEM_DEV, H)
        for receivers, senders, factor in slab_pairs(x):
            g = sget(cot, (0, receivers[1]))
            g = g if factor is None else g * factor
            dz1 = backward_edge(sget(t_ref, receivers) + sget(s_ref, senders), g, w2, w2t, bias, g2_ref, total_ref)
            sadd(dt_ref, receivers, dz1)
            sadd(ds_ref, senders, dz1)
        return carry

    lax.fori_loop(first, last, plane, 0)


def back_outer_kernel(place, dz_ref, t_ref, s_ref, hs_ref, eb_ref, w2, w2t, wct, ngrad_ref, dt_a, ds_a, g2_a, total_a, dt_b, ds_b, g2_b, total_b,
                      rx1, rx2, ry1, ry2, rz1, rz2, keep_ref, give_ref, dt_hbm, ds_hbm, acc, dt_ref, ds_ref, sems, g_2, g_t, g_s, sums, grad_ref):
    g_2[...] = g2_a[...] + g2_b[...]
    g_t[...] = jnp.zeros_like(g_t)
    g_s[...] = jnp.zeros_like(g_s)
    sums[0] = jnp.zeros((8, H), F32)
    sums[1] = total_a[...] + total_b[...]
    bias = 0.5 * eb_ref[1:2, :]
    for box in OUTER:
        acc[at_box(box)] = dz_ref[at_box(box)]
    add_planes(acc, ((rx1, rx2), (ry1, ry2), (rz1, rz2)))

    def senders_so_far(x, carry):
        ds_ref[x] = ds_a[x] + ds_b[x]
        return carry

    lax.fori_loop(0, SIDE, senders_so_far, 0)
    for source, first, last in ((dt_a, 1, HALF), (dt_b, HALF, SIDE)):
        dt_ref[first:last, 1:, 1:] = source[first:last, 1:, 1:]
    for box in OUTER:
        put(acc, box, mm(split(get(acc, box)), wct[...]))
        put(dt_ref, box, jnp.zeros((math.prod(shape_of(box)) // H, H), F32))
        for receivers, senders in pairs_of(box):
            dz1 = backward_edge(get(t_ref, receivers) + get(s_ref, senders), get(acc, receivers), w2, w2t, bias, g_2, sums.at[1])
            add(dt_ref, receivers, dz1)
            add(ds_ref, senders, dz1)

    def copies(x):
        return [pltpu.make_async_copy(a.at[x], b.at[x], sems.at[i, x]) for i, (a, b) in enumerate(((dt_ref, dt_hbm), (ds_ref, ds_hbm)))]

    for x in range(SIDE):
        for copy in copies(x):
            copy.start()

    def plane(i, carry):
        dt = rows_at(dt_ref, two(i))
        dts = split(dt)
        dss = split(rows_at(ds_ref, two(i)))
        hs = split(rows_at(hs_ref, two(i)))
        sums[0] += row_sum(dt)
        g_t[...] += mm_t(hs, dts)
        g_s[...] += mm_t(hs, dss)
        return carry

    lax.fori_loop(0, SIDE // 2, plane, 0)
    grad_ref[0:4 * H, :] = ngrad_ref[0:4 * H, :]
    grad_ref[4 * H:5 * H, :] = quad(g_t[...])
    grad_ref[5 * H:6 * H, :] = quad(g_s[...])
    grad_ref[6 * H:7 * H, :] = quad(g_2[...])
    grad_ref[7 * H:, :] = jnp.zeros((PAYLOAD - 7 * H, H), F32)
    for i in range(4):
        grad_ref[7 * H + i:7 * H + i + 1, :] = jnp.sum(ngrad_ref[4 * H + i * 8:4 * H + i * 8 + 8, :], axis=0, keepdims=True)
    for i in range(2):
        grad_ref[7 * H + 4 + i:7 * H + 5 + i, :] = jnp.sum(sums[i], axis=0, keepdims=True)
    core = lax.axis_index("dom") % 2
    keep_ref[...] = grad_ref[pl.ds(pl.multiple_of(core * HALF_LOAD, HALF_LOAD), HALF_LOAD), :]
    give_ref[...] = grad_ref[pl.ds(pl.multiple_of((1 - core) * HALF_LOAD, HALF_LOAD), HALF_LOAD), :]
    for x in range(SIDE):
        for copy in copies(x):
            copy.wait()


def finish_kernel(scale, mine_ref, other_ref, wmid_ref, nin_ref, eb_ref, ein_ref, emid_ref, ebias_ref, nino_ref, nmid_ref, nbias_ref):
    core = lax.axis_index("dom") % 2

    def span(a, b):
        half = a // HALF_LOAD
        at = slice(a - half * HALF_LOAD, b - half * HALF_LOAD)
        return jnp.where(core == half, mine_ref[at, :], other_ref[at, :])

    def rows(i):
        return span(i * H, (i + 1) * H)

    m = rows(0)
    lower = nin_ref[H:, :]
    biases = span(7 * H, 7 * H + 8)
    v = biases[3:4]
    ein_ref[0:H, :] = rows(4) * scale
    ein_ref[H:, :] = rows(5) * scale
    emid_ref[0] = rows(6) * scale
    emid_ref[1] = exact_dot(m, lower.T) * scale
    ebias_ref[0:2, :] = biases[4:6] * scale
    ebias_ref[2:3, :] = exact_dot(jnp.broadcast_to(v, (8, H)), lower.T)[0:1] * scale
    nino_ref[0:H, :] = rows(1) * scale
    outer = eb_ref[2:3, :].T * v
    nino_ref[H:, :] = (exact_dot(wmid_ref[1].T, m) + outer) * scale
    nmid_ref[0] = rows(2) * scale
    nmid_ref[1] = rows(3) * scale
    nbias_ref[...] = biases[0:3] * scale


def fix_y_kernel(y1, y2, rz1, rz2, o1, o2):
    o1[...] = y1[...]
    o2[...] = y2[...]
    line = pl.ds(0, 8, stride=SIDE)
    for py, out in zip(sides(1), (o1, o2)):
        for pz, rz in zip(sides(2), (rz1, rz2)):
            for px in range(2):
                out[px * 2 + pz, line, :] += rz[px * 2 + py, line, :]


def fix_x_kernel(x1, x2, rz1, rz2, ry1, ry2, o1, o2):
    o1[...] = x1[...]
    o2[...] = x2[...]
    first = pl.ds(0, 8)
    for px, out in zip(sides(0), (o1, o2)):
        for py, ry in zip(sides(1), (ry1, ry2)):
            for pz, rz in zip(sides(2), (rz1, rz2)):
                out[py * 2 + pz, pl.ds(0, 8, stride=SIDE), :] += rz[px * 2 + py, first, :]
                out[py * 2 + pz, first, :] += ry[px * 2 + pz, first, :]


PLANE = jax.ShapeDtypeStruct((4, 64, H), F32)
VM = pl.BlockSpec(memory_space=pltpu.VMEM)
SM = pl.BlockSpec(memory_space=pltpu.SMEM)
HB = pl.BlockSpec(memory_space=pltpu.MemorySpace.HBM)


def in_hbm(*values):
    return [pltpu.with_memory_space_constraint(v, pltpu.MemorySpace.HBM) for v in values]


def swapped(block, axis, second):
    n = lax.axis_size("dom")
    limit, stride = (DGX, DGY, n // (DGX * DGY))[axis], STRIDES[axis]
    route = []
    for i in range(n):
        at = i // stride % limit
        if at % 2 == second and at + 1 < limit:
            route += [(i, i + stride), (i + stride, i)]
    return lax.ppermute(block, "dom", route)


def sds(*shape, dtype=F32):
    return jax.ShapeDtypeStruct(shape, dtype)


HALF = 5
LATTICE = jax.ShapeDtypeStruct(FULL, F32)
LIMIT = 14
SMALL = pltpu.CompilerParams(vmem_limit_bytes=6 * 1024 * 1024)


def run(kernel, name, outs, scratch, args, micros, spec=VM, hbm_in=(), hbm_out=()):
    outs = [pltpu.MemorySpace.HBM(o.shape, o.dtype) if i in hbm_out else o for i, o in enumerate(outs)]
    call = pl.pallas_call(
        kernel, out_shape=outs, in_specs=[SM] + [HB if i in hbm_in else spec for i in range(1, len(args))], out_specs=[HB if i in hbm_out else VM for i in range(len(outs))], scratch_shapes=scratch,
        name=name,
        cost_estimate=pl.CostEstimate(flops=micros * 1000000000, bytes_accessed=8000000, transcendentals=0),
        compiler_params=pltpu.CompilerParams(vmem_limit_bytes=LIMIT * 1024 * 1024),
    )
    return list(call(*args))


def exchange(planes, beside_z, beside_y):
    x1, x2, y1, y2, z1, z2 = planes
    rz1, rz2 = swapped(z1, 2, 0), swapped(z2, 2, 1)
    rz1, rz2 = beside_z(rz1, rz2)
    y1, y2 = pl.pallas_call(fix_y_kernel, out_shape=(PLANE, PLANE), in_specs=[VM] * 4, out_specs=(VM, VM), name="fix_y", compiler_params=SMALL)(y1, y2, rz1, rz2)
    ry1, ry2 = swapped(y1, 1, 0), swapped(y2, 1, 1)
    ry1, ry2 = beside_y(ry1, ry2)
    x1, x2 = pl.pallas_call(fix_x_kernel, out_shape=(PLANE, PLANE), in_specs=[VM] * 6, out_specs=(VM, VM), name="fix_x", compiler_params=SMALL)(x1, x2, rz1, rz2, ry1, ry2)
    rx1, rx2 = swapped(x1, 0, 0), swapped(x2, 0, 1)
    return [rx1, rx2, ry1, ry2, rz1, rz2]


def spread_kernel(parts, out_ref):
    out_ref[...] = jnp.broadcast_to(jnp.sum(parts[...], axis=0, keepdims=True), out_ref.shape)


def total_over_devices(keep, give, beside_first, beside_second):
    n = lax.axis_size("dom")
    pairs = [(i, i ^ 1) for i in range(n)]
    cores = [list(range(core, n, 2)) for core in range(2)]
    block = keep + lax.ppermute(give, "dom", pairs)
    parts = lax.all_to_all(block.reshape(n // 2, -1, H), "dom", 0, 0, axis_index_groups=cores, tiled=True)
    parts, first = lax.optimization_barrier((parts, beside_first()))
    spread = pl.pallas_call(
        spread_kernel, out_shape=sds(*parts.shape), in_specs=[VM], out_specs=VM, name="spread", compiler_params=SMALL,
    )(parts)
    total = lax.all_to_all(spread, "dom", 0, 0, axis_index_groups=cores, tiled=True)
    total, second = lax.optimization_barrier((total, beside_second()))
    total = total.reshape(-1, H)
    return total, lax.ppermute(total, "dom", pairs), first, second


def body(node_feat, out_grad, lattice_of, element_place, edge_in, edge_mid, edge_bias, node_in, node_mid, node_bias):
    n = lax.axis_size("dom")
    square, wide, acc = pltpu.VMEM((256, 256), BF16), pltpu.VMEM((256, 512), BF16), pltpu.VMEM(FULL, F32)
    total = pltpu.VMEM((256, 256), F32)

    split_weight = sds(256, 256, dtype=BF16)
    outs = run(edge_outer_kernel, "edge_outer", [LATTICE] * 4 + [PLANE] * 6 + [split_weight],
               [wide, pltpu.VMEM((ELEM_DEV, NODES_EL, H), F32), pltpu.VMEM((ELEM_DEV, NODES_EL), jnp.int32), pltpu.VMEM((256, H), F32),
                pltpu.VMEM((2, H, H), F32), pltpu.VMEM((3, H), F32), pltpu.SemaphoreType.DMA((4,)), pltpu.SemaphoreType.DMA((ELEM_DEV,))],
               (element_place, *in_hbm(node_feat, lattice_of, edge_in, edge_mid, edge_bias)), 8, HB)
    hs, tv, sv, outer_sum = outs[:4]
    w2 = outs[10]
    node_args = (node_in, node_mid, node_bias, edge_mid, edge_bias)
    weights = [split_weight] * 5 + [sds(8, H), sds(H, H)]

    done = {}

    def beside_z(*got):
        inner_sum, gl = run(edge_inner_kernel, "edge_inner", [LATTICE] * 2, [], (element_place, tv, sv, out_grad, lattice_of, edge_bias, w2), 12)
        *got, done["sum"], done["gl"] = lax.optimization_barrier((*got, inner_sum, gl))
        return got

    def beside_y(*got):
        done["node"] = run(node_inner_kernel, "node_inner", [LATTICE] * 3 + [sds(4, 256, 256), sds(4, 8, H)] + weights, [acc, acc, pltpu.SemaphoreType.DMA((2, SIDE))],
                           (element_place, done["sum"], hs, done["gl"]) + node_args, 12, hbm_out=(0, 1))
        *got, done["node"][4] = lax.optimization_barrier((*got, done["node"][4]))
        return got

    received = exchange(outs[4:10], beside_z, beside_y)
    gl = done["gl"]
    hid_inner, raw_inner, dz_inner, g4, g_sums, *weights, merged = done["node"]
    outs = run(node_outer_kernel, "node_outer", [LATTICE] * 3 + [sds(4 * H + 32, H)] + [PLANE] * 6,
               [acc, pltpu.VMEM((4, 256, 256), F32), pltpu.VMEM((4, 8, H), F32), acc, acc, pltpu.SemaphoreType.DMA((2, 3))],
               (element_place, outer_sum, hs, gl, node_bias, *weights, g4, g_sums, *received), 8, hbm_out=(0, 1))
    hid_outer, raw_outer, dz_outer, ngrad = outs[:4]
    hid_inner, raw_inner, hid_outer, raw_outer = in_hbm(hid_inner, raw_inner, hid_outer, raw_outer)

    cot = [pltpu.VMEM((1,) + FULL[1:], F32)]
    parts = [LATTICE] * 2 + [sds(256, 256), sds(8, H)]

    done = {}

    def under_z(*got):
        *done["a"], w2t, wct = run(functools.partial(back_first_kernel, 1, HALF), "back_inner", parts + [split_weight] * 2, cot,
                                   (element_place, dz_inner, tv, sv, edge_mid, merged, edge_bias, w2), 10)
        done["w"] = (w2, w2t, wct)
        *got, done["a"][2] = lax.optimization_barrier((*got, done["a"][2]))
        return got

    def under_y(*got):
        done["b"] = run(functools.partial(back_inner_kernel, HALF, SIDE), "back_inner", parts, cot, (element_place, dz_inner, tv, sv, edge_bias, *done["w"]), 10)
        *got, done["b"][2] = lax.optimization_barrier((*got, done["b"][2]))
        return got

    received = exchange(outs[4:], under_z, under_y)
    part_a, part_b = done["a"], done["b"]
    keep, give, dt, ds = run(back_outer_kernel, "back_outer", [sds(HALF_LOAD, H), sds(HALF_LOAD, H), LATTICE, LATTICE],
                          [acc] * 3 + [pltpu.SemaphoreType.DMA((2, SIDE))] + [total] * 3 + [pltpu.VMEM((2, 8, H), F32), pltpu.VMEM((PAYLOAD, H), F32)],
                          (element_place, dz_outer, tv, sv, hs, edge_bias, *done["w"], ngrad, *part_a, *part_b, *received), 10, hbm_out=(2, 3))
    dt, ds = in_hbm(dt, ds)

    def beside_first():
        return run(feat_grad_kernel, "feat_grad", [sds(ROWS, H)], [acc] * 4 + [pltpu.SemaphoreType.DMA((4,)), pltpu.SemaphoreType.DMA((2, SIDE))] + [square] * 3,
                   (element_place, dt, ds, raw_inner, raw_outer, out_grad, lattice_of, edge_in, node_in), 8, hbm_in=(1, 2, 3, 4))[0]

    def beside_second():
        return run(new_feat_kernel, "new_feat", [sds(ROWS, H)], [acc, acc, pltpu.SemaphoreType.DMA((4,)), square, pltpu.VMEM((ROWS, H), F32), pltpu.SemaphoreType.DMA],
                   (element_place, hid_inner, hid_outer, *in_hbm(node_feat), lattice_of, node_mid, node_bias), 8, hbm_in=(1, 2, 3))[0]

    mine, other, feat_grad, new_feat = total_over_devices(keep, give, beside_first, beside_second)
    scale = 1.0 / math.sqrt(n * ELEM_DEV * NODES_EL)
    weights = pl.pallas_call(
        functools.partial(finish_kernel, scale),
        out_shape=(sds(256, H), sds(2, H, H), sds(3, H), sds(256, H), sds(2, H, H), sds(3, H)),
        in_specs=[VM] * 5, out_specs=(VM,) * 6, name="finish", compiler_params=SMALL,
    )(mine, other, edge_mid, node_in, edge_bias)
    return (new_feat, feat_grad) + tuple(weights)


def solution(mesh):
    in_specs = (P("dom", None),) * 4 + (P(),) * 6
    out_specs = (P("dom", None), P("dom", None)) + (P(),) * 6
    return jax.shard_map(body, mesh=mesh, in_specs=in_specs, out_specs=out_specs, check_vma=False)
```
